768 devices in a mesh: curve: 384 (over z, y, x), sub: 2 (over core).
Axes of the slice: x: 4, y: 8, z: 12, core: 2. Of those that a mesh axis runs over, the one named last changes fastest.
Arguments:
- pressure: float32 [3072, 4096], P(('curve', 'sub')), may hold values from -6 to 6
- source_term: float32 [3072, 4096], P(('curve', 'sub')), may hold values from -7 to 7
- coefficient: float32 [3072, 4096], P(('curve', 'sub')), may hold values from 0.05 to 2
- new_slot: int32 [3072], P(('curve', 'sub')), may hold values from 0 to 7, as said below
- face_links: int32 [3072, 6], P(('curve', 'sub')), may hold values from -1 to 3071, as said below
Outputs:
- corrected: float32 [3072, 4096], P(('curve', 'sub'))
The draws below stay inside these ranges and needn't reach their ends.
Inputs may be any that keep to these rules, and one draw needn't show every extreme that they name: `new_slot`: every block stays within its Z-order range of 8 blocks; within a range the slots form a permutation, each device receives exactly 4 blocks, and one device hands at most 2 blocks to one device, a bound reached by every device. `face_links`: A neighbour of block b lies in range b // 8 - 1, b // 8 or b // 8 + 1.
All inputs are finite; a program needn't handle non-finite values.
Results may differ from the reference program's by a relative error of at most 0.0001.
Values sent between devices are 32-bit elements; how exact they have to be, the bound alone decides.
No kernel may reach another device: no remote copies, remote signals or barrier semaphores. Data moves between devices by JAX's collectives and lax.ppermute only.
A program may use at most 32 MiB of HBM per device.

```python
import math
import jax
import jax.numpy as jnp

B_DEV = 4
PRE_SWEEPS = 2
COARSE_SWEEPS = 4
MOST = 2
GROUP = 8
BLOCKS = 3072


def draw_new_slot(key, part):
    ngroups = BLOCKS // GROUP
    nsub = GROUP // B_DEV
    kinds = B_DEV // MOST
    first_key, second_key = jax.random.split(jax.random.fold_in(key, 11))
    offsets = jax.vmap(lambda k: jax.random.permutation(k, nsub))(jax.random.split(first_key, ngroups))[:, :kinds]
    orders = jax.vmap(lambda k: jax.random.permutation(k, B_DEV))(jax.random.split(second_key, ngroups * nsub))
    orders = orders.reshape(ngroups, nsub, B_DEV)
    kind_of = orders // MOST
    within = orders % MOST
    spread = jnp.broadcast_to(offsets[:, None, :], (ngroups, nsub, kinds))
    chosen = jnp.take_along_axis(spread, kind_of, axis=2)
    sub_index = jnp.arange(nsub, dtype=jnp.int32)[None, :, None]
    target_dev = (sub_index + chosen) % nsub
    position = kind_of * MOST + within
    return (target_dev * B_DEV + position).reshape(-1).astype(jnp.int32)


def draw_face_links(key, part):
    ngroups = BLOCKS // GROUP
    first_key, second_key, third_key = jax.random.split(jax.random.fold_in(key, 23), 3)
    ranges = (jnp.arange(BLOCKS, dtype=jnp.int32) // GROUP)[:, None]
    moves = jax.random.randint(first_key, (BLOCKS, 6), -1, 2)
    inner = jax.random.randint(second_key, (BLOCKS, 6), 0, GROUP)
    walls = jax.random.randint(third_key, (BLOCKS, 6), 0, 8) == 0
    other = ranges + moves
    usable = (other >= 0) & (other < ngroups) & jnp.logical_not(walls)
    links = jnp.where(usable, other * GROUP + inner, -1)
    links = links.at[0, 0].set(-1).at[BLOCKS - 2, 1].set(BLOCKS - 1)
    return links.astype(jnp.int32)


def draw_source_term(key, part):
    noise_key, level_key, sign_key = jax.random.split(jax.random.fold_in(key, 37), 3)
    noise = jnp.clip(jax.random.normal(noise_key, (BLOCKS, 4096), jnp.float32), -4.0, 4.0)
    magnitude = jax.random.uniform(level_key, (BLOCKS, 1), jnp.float32, 0.5, 3.0)
    signs = jnp.where(jax.random.uniform(sign_key, (BLOCKS, 1), jnp.float32) < 0.5, -1.0, 1.0)
    level = magnitude * signs
    return (noise + level).astype(jnp.float32)


def shard_levels(own_key, dims, shards, low, largest):
    def one(dim, parts):
        heights = jax.random.uniform(jax.random.fold_in(jax.random.fold_in(own_key, 6), dim), (parts,), jnp.float32, low / len(shards), largest / len(shards))
        return jnp.repeat(jnp.exp(heights), dims[dim] // parts).reshape((-1,) + (1,) * (len(dims) - dim - 1))

    gain = one(*shards[0])
    for cut in shards[1:]:
        gain = gain * one(*cut)
    return gain


def scatter_about(stream_key, dims, deviation, limit, cuts=(), kind=jnp.bfloat16):
    gain = shard_levels(stream_key, dims, cuts, -0.22, 0.18) if cuts else 1.0
    entries = jax.random.normal(stream_key, dims, jnp.float32) * deviation * gain
    return jnp.minimum(jnp.maximum(entries, -limit), limit).astype(kind)


def setup_inputs(seed: int = 0) -> dict:
    key_of = jax.random.split(jax.random.key(seed), 6)
    pressure = scatter_about(key_of[0], (BLOCKS, 4096), 1.0, 6.0, ((0, 768),), jnp.float32)
    source_term = draw_source_term(jax.random.fold_in(key_of[5], 71), 0)
    coefficient = jnp.clip(jnp.exp(math.log(2.0) - 3.6888794 * jax.random.uniform(key_of[2], (BLOCKS, 4096), jnp.float32) ** shard_levels(key_of[2], (BLOCKS, 4096), ((0, 768),), -0.2, 0.2)), 0.05, 2.0)
    new_slot = draw_new_slot(jax.random.fold_in(key_of[5], 71), 0)
    face_links = draw_face_links(jax.random.fold_in(key_of[5], 71), 0)
    return dict(pressure=pressure, source_term=source_term, coefficient=coefficient, new_slot=new_slot, face_links=face_links)


relaxation = 0.8


def face_stack(field):
    cubes = field.reshape(-1, 16, 16, 16)
    layers = [cubes[:, 0], cubes[:, -1], cubes[:, :, 0], cubes[:, :, -1], cubes[:, :, :, 0], cubes[:, :, :, -1]]
    return jnp.stack(layers, axis=1).reshape(-1, 6, 256)


def apply_operator(field, ghosts, coefficient):
    cubes = field.reshape(-1, 16, 16, 16)
    sides = ghosts.reshape(-1, 6, 16, 16)
    padded = jnp.pad(cubes, ((0, 0), (1, 1), (1, 1), (1, 1)))
    padded = padded.at[:, 0, 1:-1, 1:-1].set(sides[:, 0]).at[:, -1, 1:-1, 1:-1].set(sides[:, 1])
    padded = padded.at[:, 1:-1, 0, 1:-1].set(sides[:, 2]).at[:, 1:-1, -1, 1:-1].set(sides[:, 3])
    padded = padded.at[:, 1:-1, 1:-1, 0].set(sides[:, 4]).at[:, 1:-1, 1:-1, -1].set(sides[:, 5])
    beside = padded[:, 2:, 1:-1, 1:-1] + padded[:, :-2, 1:-1, 1:-1]
    beside = beside + padded[:, 1:-1, 2:, 1:-1] + padded[:, 1:-1, :-2, 1:-1]
    beside = beside + padded[:, 1:-1, 1:-1, 2:] + padded[:, 1:-1, 1:-1, :-2]
    return (6.0 + coefficient) * field - beside.reshape(-1, 4096)


def ghost_layers(field, face_links):
    faces = face_stack(field)
    opposite = faces[:, jnp.array([1, 0, 3, 2, 5, 4], dtype=jnp.int32)]
    clipped = jnp.clip(face_links, 0, faces.shape[0] - 1)
    picked = opposite[clipped, jnp.arange(6, dtype=jnp.int32)[None, :]]
    return picked * (face_links >= 0).astype(jnp.float32)[:, :, None]


def sweep(field, source, coefficient, face_links):
    image = apply_operator(field, ghost_layers(field, face_links), coefficient)
    return field + relaxation * (source - image) / (6.0 + coefficient)


def reference(pressure, source_term, coefficient, new_slot, face_links):
    ranges = jnp.arange(BLOCKS, dtype=jnp.int32) // GROUP
    target = (ranges * GROUP + new_slot).astype(jnp.int32)
    empty = jnp.zeros((BLOCKS, 4096), jnp.float32)
    moved_p = empty.at[target].set(pressure)
    moved_f = empty.at[target].set(source_term)
    moved_c = empty.at[target].set(coefficient)
    smoothed = moved_p
    for step in range(PRE_SWEEPS):
        smoothed = sweep(smoothed, moved_f, moved_c, face_links)
    residual = moved_f - apply_operator(smoothed, ghost_layers(smoothed, face_links), moved_c)
    block_residual = jnp.mean(residual, axis=1)
    block_diag = 6.0 + jnp.mean(moved_c, axis=1)
    block_error = jnp.zeros((BLOCKS,), jnp.float32)
    valid = face_links >= 0
    clipped = jnp.clip(face_links, 0, BLOCKS - 1)
    for step in range(COARSE_SWEEPS):
        beside = jnp.sum(jnp.where(valid, block_error[clipped], 0.0), axis=1)
        block_error = block_error + relaxation * (block_residual - block_diag * block_error + beside) / block_diag
    lifted = smoothed + block_error[:, None]
    return sweep(lifted, moved_f, moved_c, face_links)
```

```python
import functools

import jax
import jax.numpy as jnp
from jax import lax
from jax.experimental import pallas as pl
from jax.experimental.pallas import tpu as pltpu
from jax.sharding import Mesh, PartitionSpec as P

PRE_SWEEPS = 2
COARSE_SWEEPS = 4
RELAXATION = 0.8

SIDE = 16
RANGE = 8
LANES = 128
CELLS = 4096
FACES = 6
FLIPPED = (1, 0, 3, 2, 5, 4)
ROW = 4
SLOTS = LANES // RANGE

VMEM = pl.BlockSpec(memory_space=pltpu.VMEM)
SMEM = pl.BlockSpec(memory_space=pltpu.SMEM)


def f32(*shape):
    return jax.ShapeDtypeStruct(shape, jnp.float32)


def lanes():
    return lax.broadcasted_iota(jnp.int32, (RANGE, LANES), 1)


def sublanes():
    return lax.broadcasted_iota(jnp.int32, (RANGE, LANES), 0)


def roll(tile, amount):
    amount = amount % LANES
    return tile if amount == 0 else pltpu.roll(tile, amount, 1)


def load(ref):
    return [[ref[2 * x + h] for h in range(2)] for x in range(SIDE)]


def store(ref, tiles):
    for x in range(SIDE):
        for h in range(2):
            ref[2 * x + h] = tiles[x][h]


def pack_faces(tiles):
    lane = lanes()
    zero = jnp.zeros((RANGE, LANES), jnp.float32)
    y_low, y_high, z_low, z_high = [[zero, zero] for _ in range(4)]
    for x in range(SIDE):
        part, place = x // 8, x % 8
        here = lane // SIDE == place
        y_low[part] = jnp.where(here, roll(tiles[x][0], SIDE * place), y_low[part])
        y_high[part] = jnp.where(here, roll(tiles[x][1], SIDE * place + SIDE), y_high[part])
        column = lane % SIDE == x
        for h in range(2):
            z_low[h] = jnp.where(column, roll(tiles[x][h], x), z_low[h])
            z_high[h] = jnp.where(column, roll(tiles[x][h], x - (SIDE - 1)), z_high[h])
    return [tiles[0], tiles[SIDE - 1], y_low, y_high, z_low, z_high]


def store_faces(ref, faces):
    for f in range(FACES):
        for h in range(2):
            ref[:, (2 * f + h) * LANES : (2 * f + h + 1) * LANES] = faces[f][h]


def load_face(ref, f, h, *lead):
    return ref[(*lead, slice(None), slice((2 * f + h) * LANES, (2 * f + h + 1) * LANES))]


def pick_rows(tile, rows):
    return jnp.take_along_axis(tile, rows, axis=0)


def ghost_faces(links, base, before, own, after):
    ghosts, valid = [], []
    for d in range(FACES):
        link = jnp.broadcast_to(links[:, d : d + 1], (RANGE, LANES))
        local = link - base
        rows = link & (RANGE - 1)
        face = FLIPPED[d]
        halves = []
        for h in range(2):
            low = pick_rows(before(face, h), rows)
            mid = pick_rows(own(face, h), rows)
            high = pick_rows(after(face, h), rows)
            picked = jnp.where(local < 0, low, jnp.where(local >= RANGE, high, mid))
            halves.append(jnp.where(link >= 0, picked, 0.0))
        ghosts.append(halves)
        valid.append(link >= 0)
    return ghosts, valid


def beside(tiles, ghosts, x, h):
    lane = lanes()
    here = tiles[x][h]
    minus = tiles[x - 1][h] if x > 0 else ghosts[0][h]
    plus = tiles[x + 1][h] if x < SIDE - 1 else ghosts[1][h]
    total = minus + plus
    part, place = x // 8, x % 8
    if h == 0:
        outer_minus = roll(ghosts[2][part], -SIDE * place)
        outer_plus = roll(tiles[x][1], -SIDE)
    else:
        outer_minus = roll(tiles[x][0], SIDE)
        outer_plus = roll(ghosts[3][part], LANES - SIDE - SIDE * place)
    total = total + jnp.where(lane < SIDE, outer_minus, roll(here, SIDE))
    total = total + jnp.where(lane >= LANES - SIDE, outer_plus, roll(here, -SIDE))
    z = lane % SIDE
    total = total + jnp.where(z == 0, roll(ghosts[4][h], -x), roll(here, 1))
    total = total + jnp.where(z == SIDE - 1, roll(ghosts[5][h], SIDE - 1 - x), roll(here, -1))
    return total


def sweep(tiles, ghosts, source_ref, coefficient_ref):
    out = []
    for x in range(SIDE):
        out.append([])
        for h in range(2):
            weight = RELAXATION / (6.0 + coefficient_ref[2 * x + h])
            gathered = source_ref[2 * x + h] + beside(tiles, ghosts, x, h)
            out[x].append((1.0 - RELAXATION) * tiles[x][h] + weight * gathered)
    return out


def both(ref):
    return jnp.concatenate([ref[0], ref[1]], axis=0)


def range_base():
    return lax.axis_index("d") // 2 * RANGE


def reorder_kernel(slot_ref, p_ref, f_ref, c_ref, links_ref, p_out, f_out, c_out, links_out, faces_out):
    row = sublanes()
    rows = jnp.zeros((RANGE, LANES), jnp.int32)
    for i in range(RANGE):
        rows = jnp.where(row == slot_ref[i // 4, i % 4], i, rows)
    for source, target in ((p_ref, p_out), (f_ref, f_out), (c_ref, c_out)):
        for t in range(CELLS // LANES):
            span = slice(t * LANES, (t + 1) * LANES)
            tile = jnp.concatenate([source[0, :, span], source[1, :, span]], axis=0)
            target[t] = pick_rows(tile, rows)
    links_out[...] = both(links_ref)
    store_faces(faces_out, pack_faces(load(p_out)))


def window(pair_ref, faces_ref):
    before = lambda f, h: load_face(pair_ref, f, h, 1, 0)
    own = lambda f, h: load_face(faces_ref, f, h)
    after = lambda f, h: load_face(pair_ref, f, h, 0, 1)
    return before, own, after


def sweep_kernel(u_ref, f_ref, c_ref, links_ref, faces_ref, pair_ref, u_out, faces_out):
    ghosts, _ = ghost_faces(links_ref[...], range_base(), *window(pair_ref, faces_ref))
    tiles = sweep(load(u_ref), ghosts, f_ref, c_ref)
    store(u_out, tiles)
    store_faces(faces_out, pack_faces(tiles))


def lane_sum(tile):
    return jnp.sum(tile, axis=1, keepdims=True)


def face_sums(face):
    return [lane_sum(face(FLIPPED[d], 0) + face(FLIPPED[d], 1)) * (1.0 / CELLS) for d in range(FACES)]


def to_lanes(columns, range_index):
    at = lanes() == range_index % SLOTS * RANGE + sublanes()
    row = sublanes()
    tile = jnp.zeros((RANGE, LANES), jnp.float32)
    for i, column in enumerate(columns):
        spread = jnp.sum(jnp.where(at, column, 0.0), axis=0, keepdims=True)
        tile = jnp.where(row == i, spread, tile)
    return tile


def smooth_kernel(u_ref, f_ref, c_ref, links_ref, faces_ref, pair_ref, u_out, faces_out, coarse_out):
    links = links_ref[...]
    ghosts, _ = ghost_faces(links, range_base(), *window(pair_ref, faces_ref))
    tiles = sweep(load(u_ref), ghosts, f_ref, c_ref)
    store(u_out, tiles)
    faces = pack_faces(tiles)
    store_faces(faces_out, faces)
    defect = jnp.zeros((RANGE, LANES), jnp.float32)
    weights = jnp.zeros((RANGE, LANES), jnp.float32)
    for x in range(SIDE):
        for h in range(2):
            c = c_ref[2 * x + h]
            defect = defect + (f_ref[2 * x + h] - c * tiles[x][h])
            weights = weights + c
    sums = face_sums(lambda f, h: faces[f][h])
    inner = lane_sum(defect) * (1.0 / CELLS)
    for s in sums:
        inner = inner - s
    diag = 6.0 + lane_sum(weights) * (1.0 / CELLS)
    me = lax.axis_index("d") // 2
    values = to_lanes(sums + [inner, diag], me)
    names = to_lanes([links[:, d : d + 1].astype(jnp.float32) for d in range(FACES)], me)
    for i in range(ROW):
        coarse_out[i, 0:RANGE] = values
        coarse_out[i, RANGE : 2 * RANGE] = names


def row_kernel(coarse_ref, met_ref, out_ref):
    me = lax.axis_index("d")
    core, curve = me % 2, me // 2
    edge = jnp.where(core == 0, curve % ROW == ROW - 1, curve % ROW == 0)
    met = jnp.where(core == 0, curve + 1, curve + SLOTS - 1)
    sums = to_lanes(face_sums(lambda f, h: load_face(met_ref, f, h)), met)
    out_ref[0 : 2 * RANGE] = coarse_ref[0] + coarse_ref[1] + coarse_ref[2] + coarse_ref[3]
    out_ref[2 * RANGE : 3 * RANGE] = jnp.where(edge, sums, 0.0)


def final_kernel(u_ref, f_ref, c_ref, links_ref, faces_ref, met_ref, row_ref, rows_ref, out_ref):
    core, curve = lax.axis_index("d") % 2, lax.axis_index("d") // 2
    row = sublanes()
    spans = [slice(i * RANGE, (i + 1) * RANGE) for i in range(3)]
    values = row_ref[spans[0]] + rows_ref[0, 0, spans[0]] + rows_ref[1, 1, spans[0]]
    names = row_ref[spans[1]] + rows_ref[0, 0, spans[1]] + rows_ref[1, 1, spans[1]]
    sums = values + rows_ref[0, 0, spans[2]] + rows_ref[1, 1, spans[2]]
    valid = jnp.logical_and(names >= 0.0, row < FACES)
    at = names.astype(jnp.int32) & (LANES - 1)

    def named(tile):
        return jnp.where(valid, jnp.take_along_axis(tile, at, axis=1), 0.0)

    def total(tile):
        return jnp.broadcast_to(jnp.sum(tile, axis=0, keepdims=True), (RANGE, LANES))

    inner = jnp.broadcast_to(values[FACES : FACES + 1], (RANGE, LANES))
    diag = jnp.broadcast_to(values[FACES + 1 : FACES + 2], (RANGE, LANES))
    diag = jnp.where(diag > 0.0, diag, 1.0)
    residual = inner + total(named(sums))
    error = jnp.zeros((RANGE, LANES), jnp.float32)
    for step in range(COARSE_SWEEPS):
        near = total(named(error)) if step else 0.0
        error = error + RELAXATION * (residual - diag * error + near) / diag
    near = named(error)
    own = lanes() == curve % SLOTS * RANGE + row
    lift = lane_sum(jnp.where(own, error, 0.0))
    before = lambda f, h: load_face(met_ref, f, h, 1)
    mine = lambda f, h: load_face(faces_ref, f, h)
    after = lambda f, h: load_face(met_ref, f, h, 0)
    ghosts, _ = ghost_faces(links_ref[...], range_base(), before, mine, after)
    for d in range(FACES):
        raised = lane_sum(jnp.where(own, jnp.broadcast_to(near[d : d + 1], (RANGE, LANES)), 0.0))
        ghosts[d] = [half + raised for half in ghosts[d]]
    tiles = [[tile + lift for tile in pair] for pair in load(u_ref)]
    tiles = sweep(tiles, ghosts, f_ref, c_ref)
    for x in range(SIDE):
        for h in range(2):
            tile = tiles[x][h]
            half = jnp.where(core == 0, tile[0 : RANGE // 2], tile[RANGE // 2 :])
            t = 2 * x + h
            out_ref[:, t * LANES : (t + 1) * LANES] = half


def call(kernel, out_shape, name, *args, scalars=0):
    many = isinstance(out_shape, (list, tuple))
    return pl.pallas_call(
        kernel,
        out_shape=out_shape,
        in_specs=[SMEM] * scalars + [VMEM] * (len(args) - scalars),
        out_specs=[VMEM] * len(out_shape) if many else VMEM,
        name=name,
    )(*args)


def on_device(groups, pressure, source_term, coefficient, new_slot, face_links):
    cores, pairs, rows, row_pairs, exchange = groups
    gather = lambda array, members: lax.all_gather(array, "d", axis=0, axis_index_groups=members)
    field = f32(CELLS // LANES, RANGE, LANES)
    packed = f32(RANGE, FACES * 2 * LANES)
    p, f, c, slots, links = [
        gather(array, cores) for array in (pressure, source_term, coefficient, new_slot, face_links)
    ]
    u, f, c, links, faces = call(
        reorder_kernel,
        [field, field, field, jax.ShapeDtypeStruct((RANGE, FACES), jnp.int32), packed],
        "reorder",
        slots,
        p,
        f,
        c,
        links,
        scalars=1,
    )
    pair = gather(gather(faces, pairs), cores)
    u, faces = call(sweep_kernel, [field, packed], "sweep", u, f, c, links, faces, pair)
    pair = gather(gather(faces, pairs), cores)
    u, faces, coarse = call(
        smooth_kernel, [field, packed, f32(ROW, 2 * RANGE, LANES)], "smooth", u, f, c, links, faces, pair
    )
    met = lax.ppermute(faces, "d", exchange)
    coarse = lax.all_to_all(coarse, "d", 0, 0, axis_index_groups=rows, tiled=True)
    row = call(row_kernel, f32(3 * RANGE, LANES), "row", coarse, met)
    met, near_rows = gather(met, cores), gather(gather(row, row_pairs), cores)
    return call(
        final_kernel, f32(RANGE // 2, CELLS), "final", u, f, c, links, faces, met, row, near_rows
    )


def solution(mesh):
    devices = mesh.devices.reshape(-1)
    count = devices.size // 2
    cores = [[2 * i, 2 * i + 1] for i in range(count)]
    pairs = [[2 * i, 2 * i + 3] for i in range(count - 1)] + [[2 * count - 2, 1]]
    rows = [[2 * (i + k) + core for k in range(ROW)] for i in range(0, count, ROW) for core in range(2)]
    row_pairs = [[2 * i + 1, 2 * ((i + ROW) % count)] for i in range(count)]
    exchange = [pair for i in range(count - 1) for pair in ((2 * i, 2 * i + 3), (2 * i + 3, 2 * i))]
    split, line = P("d", None), P("d")
    return jax.shard_map(
        functools.partial(on_device, (cores, pairs, rows, row_pairs, exchange)),
        mesh=Mesh(devices, ("d",)),
        in_specs=(split, split, split, line, split),
        out_specs=split,
        check_vma=False,
    )
```

```python
import functools

import jax
import jax.numpy as jnp
from jax import lax
from jax.experimental import pallas as pl
from jax.experimental.pallas import tpu as pltpu
from jax.sharding import Mesh, PartitionSpec as P

PRE_SWEEPS = 2
COARSE_SWEEPS = 4
RELAXATION = 0.8

SIDE = 16
RANGE = 8
LANES = 128
CELLS = 4096
FACES = 6
FLIPPED = (1, 0, 3, 2, 5, 4)
GROUP = 16
PACKED = 3 * CELLS + LANES

VMEM = pl.BlockSpec(memory_space=pltpu.VMEM)
HBM = pl.BlockSpec(memory_space=pltpu.HBM)
GRANT = 4 * 1024 * 1024


def f32(*shape):
    return jax.ShapeDtypeStruct(shape, jnp.float32)


def lanes():
    return lax.broadcasted_iota(jnp.int32, (RANGE, LANES), 1)


def sublanes():
    return lax.broadcasted_iota(jnp.int32, (RANGE, LANES), 0)


def roll(tile, amount):
    amount = amount % LANES
    return tile if amount == 0 else pltpu.roll(tile, amount, 1)


def load(ref):
    return [[ref[2 * x + h] for h in range(2)] for x in range(SIDE)]


def store(ref, tiles):
    for x in range(SIDE):
        for h in range(2):
            ref[2 * x + h] = tiles[x][h]


def pack_faces(tiles):
    lane = lanes()
    zero = jnp.zeros((RANGE, LANES), jnp.float32)
    y_low, y_high, z_low, z_high = [[zero, zero] for _ in range(4)]
    for x in range(SIDE):
        part, place = x // 8, x % 8
        here = lane // SIDE == place
        y_low[part] = jnp.where(here, roll(tiles[x][0], SIDE * place), y_low[part])
        y_high[part] = jnp.where(here, roll(tiles[x][1], SIDE * place + SIDE), y_high[part])
        column = lane % SIDE == x
        for h in range(2):
            z_low[h] = jnp.where(column, roll(tiles[x][h], x), z_low[h])
            z_high[h] = jnp.where(column, roll(tiles[x][h], x - (SIDE - 1)), z_high[h])
    return [tiles[0], tiles[SIDE - 1], y_low, y_high, z_low, z_high]


def store_faces(ref, faces):
    for f in range(FACES):
        for h in range(2):
            ref[:, (2 * f + h) * LANES : (2 * f + h + 1) * LANES] = faces[f][h]


def load_face(ref, f, h, *lead):
    return ref[(*lead, slice(None), slice((2 * f + h) * LANES, (2 * f + h + 1) * LANES))]


def pick_rows(tile, rows):
    return jnp.take_along_axis(tile, rows, axis=0)


def ghost_faces(links, base, before, own, after):
    ghosts, valid = [], []
    for d in range(FACES):
        link = jnp.broadcast_to(links[:, d : d + 1], (RANGE, LANES))
        local = link - base
        rows = link & (RANGE - 1)
        face = FLIPPED[d]
        halves = []
        for h in range(2):
            low = pick_rows(before(face, h), rows)
            mid = pick_rows(own(face, h), rows)
            high = pick_rows(after(face, h), rows)
            picked = jnp.where(local < 0, low, jnp.where(local >= RANGE, high, mid))
            halves.append(jnp.where(link >= 0, picked, 0.0))
        ghosts.append(halves)
        valid.append(link >= 0)
    return ghosts, valid


def beside(tiles, ghosts, x, h):
    lane = lanes()
    here = tiles[x][h]
    minus = tiles[x - 1][h] if x > 0 else ghosts[0][h]
    plus = tiles[x + 1][h] if x < SIDE - 1 else ghosts[1][h]
    total = minus + plus
    part, place = x // 8, x % 8
    if h == 0:
        outer_minus = roll(ghosts[2][part], -SIDE * place)
        outer_plus = roll(tiles[x][1], -SIDE)
    else:
        outer_minus = roll(tiles[x][0], SIDE)
        outer_plus = roll(ghosts[3][part], LANES - SIDE - SIDE * place)
    total = total + jnp.where(lane < SIDE, outer_minus, roll(here, SIDE))
    total = total + jnp.where(lane >= LANES - SIDE, outer_plus, roll(here, -SIDE))
    z = lane % SIDE
    total = total + jnp.where(z == 0, roll(ghosts[4][h], -x), roll(here, 1))
    total = total + jnp.where(z == SIDE - 1, roll(ghosts[5][h], SIDE - 1 - x), roll(here, -1))
    return total


def sweep(tiles, ghosts, source_ref, coefficient_ref):
    out = []
    for x in range(SIDE):
        out.append([])
        for h in range(2):
            weight = RELAXATION / (6.0 + coefficient_ref[2 * x + h])
            gathered = source_ref[2 * x + h] + beside(tiles, ghosts, x, h)
            out[x].append((1.0 - RELAXATION) * tiles[x][h] + weight * gathered)
    return out


def range_base():
    return lax.axis_index("d") // 2 * RANGE


def pack_kernel(p_ref, f_ref, c_ref, slot_ref, links_ref, out_ref, slots, links, sems):
    small = [pltpu.make_async_copy(slot_ref, slots, sems.at[3]), pltpu.make_async_copy(links_ref, links, sems.at[4])]
    large = [
        pltpu.make_async_copy(ref, out_ref.at[:, i * CELLS : (i + 1) * CELLS], sems.at[i])
        for i, ref in enumerate((p_ref, f_ref, c_ref))
    ]
    for copy in small + large:
        copy.start()
    for copy in small:
        copy.wait()
    lane = lanes()[: RANGE // 2]
    row = sublanes()[: RANGE // 2]
    tile = jnp.zeros((RANGE // 2, LANES), jnp.int32)
    for d in range(FACES):
        tile = jnp.where(lane == d, links[:, d : d + 1], tile)
    for i in range(RANGE // 2):
        tile = jnp.where(jnp.logical_and(lane == FACES, row == i), slots[i], tile)
    out_ref[:, 3 * CELLS :] = tile.astype(jnp.float32)
    for copy in large:
        copy.wait()


def reorder_kernel(packed_ref, p_out, f_out, c_out, links_out, faces_out):
    def both(start):
        span = slice(start, start + LANES)
        return jnp.concatenate([packed_ref[0, :, span], packed_ref[1, :, span]], axis=0)

    lane, row = lanes(), sublanes()
    names = both(3 * CELLS)
    links_out[...] = names.astype(jnp.int32)
    slot = jnp.broadcast_to(names[:, FACES : FACES + 1], (RANGE, LANES)).astype(jnp.int32)
    placed = jnp.sum(jnp.where(slot == lane, row, 0).astype(jnp.float32), axis=0, keepdims=True)
    chosen = jnp.sum(jnp.where(lane == row, placed, 0.0), axis=1, keepdims=True)
    rows = jnp.broadcast_to(chosen, (RANGE, LANES)).astype(jnp.int32)
    for i, target in enumerate((p_out, f_out, c_out)):
        for t in range(CELLS // LANES):
            target[t] = pick_rows(both(i * CELLS + t * LANES), rows)
    store_faces(faces_out, pack_faces(load(p_out)))


def window(pair_ref, faces_ref):
    before = lambda f, h: load_face(pair_ref, f, h, 1, 0)
    own = lambda f, h: load_face(faces_ref, f, h)
    after = lambda f, h: load_face(pair_ref, f, h, 0, 1)
    return before, own, after


def sweep_kernel(u_ref, f_ref, c_ref, links_ref, faces_ref, pair_ref, u_out, faces_out):
    ghosts, _ = ghost_faces(links_ref[...], range_base(), *window(pair_ref, faces_ref))
    tiles = sweep(load(u_ref), ghosts, f_ref, c_ref)
    store(u_out, tiles)
    store_faces(faces_out, pack_faces(tiles))


def lane_sum(tile):
    return jnp.sum(tile, axis=1, keepdims=True)


def face_sums(face):
    return [lane_sum(face(FLIPPED[d], 0) + face(FLIPPED[d], 1)) * (1.0 / CELLS) for d in range(FACES)]


def smooth_kernel(u_ref, f_ref, c_ref, links_ref, faces_ref, pair_ref, u_out, faces_out, coarse_out):
    links = links_ref[...]
    ghosts, _ = ghost_faces(links, range_base(), *window(pair_ref, faces_ref))
    tiles = sweep(load(u_ref), ghosts, f_ref, c_ref)
    store(u_out, tiles)
    faces = pack_faces(tiles)
    store_faces(faces_out, faces)
    defect = jnp.zeros((RANGE, LANES), jnp.float32)
    weights = jnp.zeros((RANGE, LANES), jnp.float32)
    for x in range(SIDE):
        for h in range(2):
            c = c_ref[2 * x + h]
            defect = defect + (f_ref[2 * x + h] - c * tiles[x][h])
            weights = weights + c
    sums = face_sums(lambda f, h: faces[f][h])
    inner = lane_sum(defect) * (1.0 / CELLS)
    for s in sums:
        inner = inner - s
    diag = 6.0 + lane_sum(weights) * (1.0 / CELLS)
    lane = lanes()
    tile = jnp.zeros((RANGE, LANES), jnp.float32)
    for d in range(FACES):
        tile = jnp.where(lane == d, sums[d], tile)
        tile = jnp.where(lane == RANGE + d, links[:, d : d + 1].astype(jnp.float32), tile)
    tile = jnp.where(lane == FACES, inner, tile)
    tile = jnp.where(lane == FACES + 1, diag, tile)
    for i in range(GROUP):
        coarse_out[i] = tile


def final_kernel(u_ref, f_ref, c_ref, links_ref, faces_ref, met_ref, coarse_ref, out_ref):
    core, curve = lax.axis_index("d") % 2, lax.axis_index("d") // 2
    row = sublanes()
    nearest = []
    for i in range(GROUP):
        ahead = i - curve % GROUP
        aligned = jnp.logical_and(ahead >= -GROUP // 2, ahead < GROUP // 2)
        nearest.append(jnp.where(aligned, coarse_ref[0, i], coarse_ref[1, (i + GROUP // 2) % GROUP]))
    values = jnp.concatenate(nearest, axis=0).T
    sums, names = values[:RANGE], values[RANGE : 2 * RANGE]
    valid = jnp.logical_and(names >= 0.0, row < FACES)
    at = names.astype(jnp.int32) & (LANES - 1)

    def named(tile):
        return jnp.where(valid, jnp.take_along_axis(tile, at, axis=1), 0.0)

    def total(tile):
        return jnp.broadcast_to(jnp.sum(tile, axis=0, keepdims=True), (RANGE, LANES))

    inner = jnp.broadcast_to(sums[FACES : FACES + 1], (RANGE, LANES))
    diag = jnp.broadcast_to(sums[FACES + 1 : FACES + 2], (RANGE, LANES))
    diag = jnp.where(diag > 0.0, diag, 1.0)
    residual = inner + total(named(sums))
    error = jnp.zeros((RANGE, LANES), jnp.float32)
    for step in range(COARSE_SWEEPS):
        near = total(named(error)) if step else 0.0
        error = error + RELAXATION * (residual - diag * error + near) / diag
    near = named(error)
    own = lanes() == curve % GROUP * RANGE + row
    lift = lane_sum(jnp.where(own, error, 0.0))
    before = lambda f, h: load_face(met_ref, f, h, 1)
    mine = lambda f, h: load_face(faces_ref, f, h)
    after = lambda f, h: load_face(met_ref, f, h, 0)
    ghosts, _ = ghost_faces(links_ref[...], range_base(), before, mine, after)
    for d in range(FACES):
        raised = lane_sum(jnp.where(own, jnp.broadcast_to(near[d : d + 1], (RANGE, LANES)), 0.0))
        ghosts[d] = [half + raised for half in ghosts[d]]
    tiles = [[tile + lift for tile in pair] for pair in load(u_ref)]
    tiles = sweep(tiles, ghosts, f_ref, c_ref)
    for x in range(SIDE):
        for h in range(2):
            tile = tiles[x][h]
            half = jnp.where(core == 0, tile[0 : RANGE // 2], tile[RANGE // 2 :])
            t = 2 * x + h
            out_ref[:, t * LANES : (t + 1) * LANES] = half


def call(kernel, out_shape, name, *args, specs=None, scratch=()):
    many = isinstance(out_shape, (list, tuple))
    return pl.pallas_call(
        kernel,
        out_shape=out_shape,
        in_specs=specs or [VMEM] * len(args),
        out_specs=[VMEM] * len(out_shape) if many else VMEM,
        scratch_shapes=scratch,
        compiler_params=pltpu.CompilerParams(vmem_limit_bytes=GRANT),
        name=name,
    )(*args)


def on_device(groups, pressure, source_term, coefficient, new_slot, face_links):
    cores, pairs, groups16, exchange = groups
    gather = lambda array, members: lax.all_gather(array, "d", axis=0, axis_index_groups=members)
    field = f32(CELLS // LANES, RANGE, LANES)
    packed = f32(RANGE, FACES * 2 * LANES)
    whole = call(
        pack_kernel,
        f32(RANGE // 2, PACKED),
        "pack",
        *[
            pltpu.with_memory_space_constraint(array, pltpu.HBM)
            for array in (pressure, source_term, coefficient, new_slot, face_links)
        ],
        specs=[HBM] * 5,
        scratch=[
            pltpu.SMEM((RANGE // 2,), jnp.int32),
            pltpu.VMEM((RANGE // 2, FACES), jnp.int32),
            pltpu.SemaphoreType.DMA((5,)),
        ],
    )
    u, f, c, links, faces = call(
        reorder_kernel,
        [field, field, field, jax.ShapeDtypeStruct((RANGE, LANES), jnp.int32), packed],
        "reorder",
        gather(whole, cores),
    )
    pair = gather(gather(faces, pairs), cores)
    u, faces = call(sweep_kernel, [field, packed], "sweep", u, f, c, links, faces, pair)
    pair = gather(gather(faces, pairs), cores)
    u, faces, coarse = call(
        smooth_kernel, [field, packed, f32(GROUP, RANGE, LANES)], "smooth", u, f, c, links, faces, pair
    )
    met = lax.ppermute(faces, "d", exchange)
    coarse = lax.all_to_all(coarse, "d", 0, 0, axis_index_groups=groups16, tiled=True)
    met, coarse = gather(met, cores), gather(coarse, cores)
    return call(final_kernel, f32(RANGE // 2, CELLS), "final", u, f, c, links, faces, met, coarse)


def solution(mesh):
    devices = mesh.devices.reshape(-1)
    count = devices.size // 2
    cores = [[2 * i, 2 * i + 1] for i in range(count)]
    pairs = [[2 * i, 2 * i + 3] for i in range(count - 1)] + [[2 * count - 2, 1]]
    groups16 = [
        [2 * ((i + core * GROUP // 2 + k) % count) + core for k in range(GROUP)]
        for i in range(0, count, GROUP)
        for core in range(2)
    ]
    exchange = [pair for i in range(count - 1) for pair in ((2 * i, 2 * i + 3), (2 * i + 3, 2 * i))]
    split, line = P("d", None), P("d")
    return jax.shard_map(
        functools.partial(on_device, (cores, pairs, groups16, exchange)),
        mesh=Mesh(devices, ("d",)),
        in_specs=(split, split, split, line, split),
        out_specs=split,
        check_vma=False,
    )
```

```python
import functools

import jax
import jax.numpy as jnp
from jax import lax
from jax.experimental import pallas as pl
from jax.experimental.pallas import tpu as pltpu
from jax.sharding import Mesh, PartitionSpec as P

PRE_SWEEPS = 2
COARSE_SWEEPS = 4
RELAXATION = 0.8

SIDE = 16
RANGE = 8
LANES = 128
CELLS = 4096
FACES = 6
FLIPPED = (1, 0, 3, 2, 5, 4)
GROUP = 16
PACKED = 3 * CELLS + LANES

VMEM = pl.BlockSpec(memory_space=pltpu.VMEM)
HBM = pl.BlockSpec(memory_space=pltpu.HBM)
GRANT = 4 * 1024 * 1024


def f32(*shape):
    return jax.ShapeDtypeStruct(shape, jnp.float32)


def lanes():
    return lax.broadcasted_iota(jnp.int32, (RANGE, LANES), 1)


def sublanes():
    return lax.broadcasted_iota(jnp.int32, (RANGE, LANES), 0)


def roll(tile, amount):
    amount = amount % LANES
    return tile if amount == 0 else pltpu.roll(tile, amount, 1)


def load(ref):
    return [[ref[2 * x + h] for h in range(2)] for x in range(SIDE)]


def store(ref, tiles):
    for x in range(SIDE):
        for h in range(2):
            ref[2 * x + h] = tiles[x][h]


def pack_faces(tiles):
    lane = lanes()
    zero = jnp.zeros((RANGE, LANES), jnp.float32)
    y_low, y_high, z_low, z_high = [[zero, zero] for _ in range(4)]
    for x in range(SIDE):
        part, place = x // 8, x % 8
        here = lane // SIDE == place
        y_low[part] = jnp.where(here, roll(tiles[x][0], SIDE * place), y_low[part])
        y_high[part] = jnp.where(here, roll(tiles[x][1], SIDE * place + SIDE), y_high[part])
        column = lane % SIDE == x
        for h in range(2):
            z_low[h] = jnp.where(column, roll(tiles[x][h], x), z_low[h])
            z_high[h] = jnp.where(column, roll(tiles[x][h], x - (SIDE - 1)), z_high[h])
    return [tiles[0], tiles[SIDE - 1], y_low, y_high, z_low, z_high]


def store_faces(ref, faces):
    for f in range(FACES):
        for h in range(2):
            ref[:, (2 * f + h) * LANES : (2 * f + h + 1) * LANES] = faces[f][h]


def load_face(ref, f, h, *lead):
    return ref[(*lead, slice(None), slice((2 * f + h) * LANES, (2 * f + h + 1) * LANES))]


def load_coarse(ref, core, member):
    start = (2 * FACES + member) * LANES
    return ref[core, :, start : start + LANES]


def pick_rows(tile, rows):
    return jnp.take_along_axis(tile, rows, axis=0)


def ghost_faces(links, base, before, own, after):
    ghosts, valid = [], []
    for d in range(FACES):
        link = jnp.broadcast_to(links[:, d : d + 1], (RANGE, LANES))
        local = link - base
        rows = link & (RANGE - 1)
        face = FLIPPED[d]
        halves = []
        for h in range(2):
            low = pick_rows(before(face, h), rows)
            mid = pick_rows(own(face, h), rows)
            high = pick_rows(after(face, h), rows)
            picked = jnp.where(local < 0, low, jnp.where(local >= RANGE, high, mid))
            halves.append(jnp.where(link >= 0, picked, 0.0))
        ghosts.append(halves)
        valid.append(link >= 0)
    return ghosts, valid


def beside(tiles, ghosts, x, h):
    lane = lanes()
    here = tiles[x][h]
    minus = tiles[x - 1][h] if x > 0 else ghosts[0][h]
    plus = tiles[x + 1][h] if x < SIDE - 1 else ghosts[1][h]
    total = minus + plus
    part, place = x // 8, x % 8
    if h == 0:
        outer_minus = roll(ghosts[2][part], -SIDE * place)
        outer_plus = roll(tiles[x][1], -SIDE)
    else:
        outer_minus = roll(tiles[x][0], SIDE)
        outer_plus = roll(ghosts[3][part], LANES - SIDE - SIDE * place)
    total = total + jnp.where(lane < SIDE, outer_minus, roll(here, SIDE))
    total = total + jnp.where(lane >= LANES - SIDE, outer_plus, roll(here, -SIDE))
    z = lane % SIDE
    total = total + jnp.where(z == 0, roll(ghosts[4][h], -x), roll(here, 1))
    total = total + jnp.where(z == SIDE - 1, roll(ghosts[5][h], SIDE - 1 - x), roll(here, -1))
    return total


def sweep(tiles, ghosts, source_ref, coefficient_ref):
    out = []
    for x in range(SIDE):
        out.append([])
        for h in range(2):
            weight = RELAXATION / (6.0 + coefficient_ref[2 * x + h])
            gathered = source_ref[2 * x + h] + beside(tiles, ghosts, x, h)
            out[x].append((1.0 - RELAXATION) * tiles[x][h] + weight * gathered)
    return out


def range_base():
    return lax.axis_index("d") // 2 * RANGE


def pack_kernel(p_ref, f_ref, c_ref, slot_ref, links_ref, out_ref, slots, links, sems):
    small = [pltpu.make_async_copy(slot_ref, slots, sems.at[3]), pltpu.make_async_copy(links_ref, links, sems.at[4])]
    large = [
        pltpu.make_async_copy(ref, out_ref.at[:, i * CELLS : (i + 1) * CELLS], sems.at[i])
        for i, ref in enumerate((p_ref, f_ref, c_ref))
    ]
    for copy in small + large:
        copy.start()
    for copy in small:
        copy.wait()
    lane = lanes()[: RANGE // 2]
    row = sublanes()[: RANGE // 2]
    tile = jnp.zeros((RANGE // 2, LANES), jnp.int32)
    for d in range(FACES):
        tile = jnp.where(lane == d, links[:, d : d + 1], tile)
    for i in range(RANGE // 2):
        tile = jnp.where(jnp.logical_and(lane == FACES, row == i), slots[i], tile)
    out_ref[:, 3 * CELLS :] = tile.astype(jnp.float32)
    for copy in large:
        copy.wait()


def reorder_kernel(packed_ref, p_out, f_out, c_out, links_out, faces_out):
    def both(start):
        span = slice(start, start + LANES)
        return jnp.concatenate([packed_ref[0, :, span], packed_ref[1, :, span]], axis=0)

    lane, row = lanes(), sublanes()
    names = both(3 * CELLS)
    links_out[...] = names.astype(jnp.int32)
    slot = jnp.broadcast_to(names[:, FACES : FACES + 1], (RANGE, LANES)).astype(jnp.int32)
    placed = jnp.sum(jnp.where(slot == lane, row, 0).astype(jnp.float32), axis=0, keepdims=True)
    chosen = jnp.sum(jnp.where(lane == row, placed, 0.0), axis=1, keepdims=True)
    rows = jnp.broadcast_to(chosen, (RANGE, LANES)).astype(jnp.int32)
    for i, target in enumerate((p_out, f_out, c_out)):
        for t in range(CELLS // LANES):
            target[t] = pick_rows(both(i * CELLS + t * LANES), rows)
    store_faces(faces_out, pack_faces(load(p_out)))


def window(met_ref, faces_ref):
    before = lambda f, h: load_face(met_ref, f, h, 1)
    own = lambda f, h: load_face(faces_ref, f, h)
    after = lambda f, h: load_face(met_ref, f, h, 0)
    return before, own, after


def sweep_kernel(u_ref, f_ref, c_ref, links_ref, faces_ref, met_ref, u_out, faces_out):
    ghosts, _ = ghost_faces(links_ref[...], range_base(), *window(met_ref, faces_ref))
    tiles = sweep(load(u_ref), ghosts, f_ref, c_ref)
    store(u_out, tiles)
    store_faces(faces_out, pack_faces(tiles))


def lane_sum(tile):
    return jnp.sum(tile, axis=1, keepdims=True)


def face_sums(face):
    return [lane_sum(face(FLIPPED[d], 0) + face(FLIPPED[d], 1)) * (1.0 / CELLS) for d in range(FACES)]


def smooth_kernel(u_ref, f_ref, c_ref, links_ref, faces_ref, met_ref, u_out, faces_out, coarse_out):
    links = links_ref[...]
    ghosts, _ = ghost_faces(links, range_base(), *window(met_ref, faces_ref))
    tiles = sweep(load(u_ref), ghosts, f_ref, c_ref)
    store(u_out, tiles)
    faces = pack_faces(tiles)
    store_faces(faces_out, faces)
    defect = jnp.zeros((RANGE, LANES), jnp.float32)
    weights = jnp.zeros((RANGE, LANES), jnp.float32)
    for x in range(SIDE):
        for h in range(2):
            c = c_ref[2 * x + h]
            defect = defect + (f_ref[2 * x + h] - c * tiles[x][h])
            weights = weights + c
    sums = face_sums(lambda f, h: faces[f][h])
    inner = lane_sum(defect) * (1.0 / CELLS)
    for s in sums:
        inner = inner - s
    diag = 6.0 + lane_sum(weights) * (1.0 / CELLS)
    lane = lanes()
    tile = jnp.zeros((RANGE, LANES), jnp.float32)
    for d in range(FACES):
        tile = jnp.where(lane == d, sums[d], tile)
        tile = jnp.where(lane == RANGE + d, links[:, d : d + 1].astype(jnp.float32), tile)
    tile = jnp.where(lane == FACES, inner, tile)
    tile = jnp.where(lane == FACES + 1, diag, tile)
    for i in range(GROUP):
        coarse_out[i] = tile


def join_kernel(met_ref, coarse_ref, out_ref):
    width = FACES * 2 * LANES
    out_ref[:, :width] = met_ref[...]
    for i in range(GROUP):
        out_ref[:, width + i * LANES : width + (i + 1) * LANES] = coarse_ref[i]


def final_kernel(u_ref, f_ref, c_ref, links_ref, faces_ref, met_ref, out_ref):
    core, curve = lax.axis_index("d") % 2, lax.axis_index("d") // 2
    row = sublanes()
    nearest = []
    for i in range(GROUP):
        ahead = i - curve % GROUP
        aligned = jnp.logical_and(ahead >= -GROUP // 2, ahead < GROUP // 2)
        first = load_coarse(met_ref, 0, i)
        second = load_coarse(met_ref, 1, (i + GROUP // 2) % GROUP)
        nearest.append(jnp.where(aligned, first, second))
    values = jnp.concatenate(nearest, axis=0).T
    sums, names = values[:RANGE], values[RANGE : 2 * RANGE]
    valid = jnp.logical_and(names >= 0.0, row < FACES)
    at = names.astype(jnp.int32) & (LANES - 1)

    def named(tile):
        return jnp.where(valid, jnp.take_along_axis(tile, at, axis=1), 0.0)

    def total(tile):
        return jnp.broadcast_to(jnp.sum(tile, axis=0, keepdims=True), (RANGE, LANES))

    inner = jnp.broadcast_to(sums[FACES : FACES + 1], (RANGE, LANES))
    diag = jnp.broadcast_to(sums[FACES + 1 : FACES + 2], (RANGE, LANES))
    diag = jnp.where(diag > 0.0, diag, 1.0)
    residual = inner + total(named(sums))
    error = jnp.zeros((RANGE, LANES), jnp.float32)
    for step in range(COARSE_SWEEPS):
        near = total(named(error)) if step else 0.0
        error = error + RELAXATION * (residual - diag * error + near) / diag
    near = named(error)
    own = lanes() == curve % GROUP * RANGE + row
    lift = lane_sum(jnp.where(own, error, 0.0))
    ghosts, _ = ghost_faces(links_ref[...], range_base(), *window(met_ref, faces_ref))
    for d in range(FACES):
        raised = lane_sum(jnp.where(own, jnp.broadcast_to(near[d : d + 1], (RANGE, LANES)), 0.0))
        ghosts[d] = [half + raised for half in ghosts[d]]
    tiles = [[tile + lift for tile in pair] for pair in load(u_ref)]
    tiles = sweep(tiles, ghosts, f_ref, c_ref)
    for x in range(SIDE):
        for h in range(2):
            tile = tiles[x][h]
            half = jnp.where(core == 0, tile[0 : RANGE // 2], tile[RANGE // 2 :])
            t = 2 * x + h
            out_ref[:, t * LANES : (t + 1) * LANES] = half


def call(kernel, out_shape, name, *args, specs=None, scratch=()):
    many = isinstance(out_shape, (list, tuple))
    return pl.pallas_call(
        kernel,
        out_shape=out_shape,
        in_specs=specs or [VMEM] * len(args),
        out_specs=[VMEM] * len(out_shape) if many else VMEM,
        scratch_shapes=scratch,
        compiler_params=pltpu.CompilerParams(vmem_limit_bytes=GRANT),
        name=name,
    )(*args)


def on_device(groups, pressure, source_term, coefficient, new_slot, face_links):
    cores, groups16, exchange = groups
    meet = lambda array: lax.ppermute(array, "d", exchange)
    gather = lambda array, members: lax.all_gather(array, "d", axis=0, axis_index_groups=members)
    field = f32(CELLS // LANES, RANGE, LANES)
    packed = f32(RANGE, FACES * 2 * LANES)
    whole = call(
        pack_kernel,
        f32(RANGE // 2, PACKED),
        "pack",
        *[
            pltpu.with_memory_space_constraint(array, pltpu.HBM)
            for array in (pressure, source_term, coefficient, new_slot, face_links)
        ],
        specs=[HBM] * 5,
        scratch=[
            pltpu.SMEM((RANGE // 2,), jnp.int32),
            pltpu.VMEM((RANGE // 2, FACES), jnp.int32),
            pltpu.SemaphoreType.DMA((5,)),
        ],
    )
    u, f, c, links, faces = call(
        reorder_kernel,
        [field, field, field, jax.ShapeDtypeStruct((RANGE, LANES), jnp.int32), packed],
        "reorder",
        gather(whole, cores),
    )
    met = gather(meet(faces), cores)
    u, faces = call(sweep_kernel, [field, packed], "sweep", u, f, c, links, faces, met)
    met = gather(meet(faces), cores)
    u, faces, coarse = call(
        smooth_kernel, [field, packed, f32(GROUP, RANGE, LANES)], "smooth", u, f, c, links, faces, met
    )
    met = meet(faces)
    coarse = lax.all_to_all(coarse, "d", 0, 0, axis_index_groups=groups16, tiled=True)
    joined = call(join_kernel, f32(RANGE, (2 * FACES + GROUP) * LANES), "join", met, coarse)
    return call(final_kernel, f32(RANGE // 2, CELLS), "final", u, f, c, links, faces, gather(joined, cores))


def solution(mesh):
    devices = mesh.devices.reshape(-1)
    count = devices.size // 2
    cores = [[2 * i, 2 * i + 1] for i in range(count)]
    groups16 = [
        [2 * ((i + core * GROUP // 2 + k) % count) + core for k in range(GROUP)]
        for i in range(0, count, GROUP)
        for core in range(2)
    ]
    exchange = [pair for i in range(count - 1) for pair in ((2 * i, 2 * i + 3), (2 * i + 3, 2 * i))]
    split, line = P("d", None), P("d")
    return jax.shard_map(
        functools.partial(on_device, (cores, groups16, exchange)),
        mesh=Mesh(devices, ("d",)),
        in_specs=(split, split, split, line, split),
        out_specs=split,
        check_vma=False,
    )
```

```python
import functools

import jax
import jax.numpy as jnp
from jax import lax
from jax.experimental import pallas as pl
from jax.experimental.pallas import tpu as pltpu
from jax.sharding import Mesh, PartitionSpec as P


COARSE_SWEEPS = 4
RELAXATION = 0.8

SIDE = 16
RANGE = 8
LANES = 128
CELLS = 4096
FACES = 6
FLIPPED = (1, 0, 3, 2, 5, 4)
GROUP = 16
PACKED = 3 * CELLS + LANES

VMEM = pl.BlockSpec(memory_space=pltpu.VMEM)
HBM = pl.BlockSpec(memory_space=pltpu.HBM)
GRANT = 4 * 1024 * 1024


def f32(*shape):
    return jax.ShapeDtypeStruct(shape, jnp.float32)


def lanes():
    return lax.broadcasted_iota(jnp.int32, (RANGE, LANES), 1)


def sublanes():
    return lax.broadcasted_iota(jnp.int32, (RANGE, LANES), 0)


def roll(tile, amount):
    amount = amount % LANES
    return tile if amount == 0 else pltpu.roll(tile, amount, 1)


def load(ref):
    return [[ref[2 * x + h] for h in range(2)] for x in range(SIDE)]


def store(ref, tiles):
    for x in range(SIDE):
        for h in range(2):
            ref[2 * x + h] = tiles[x][h]


def pack_faces(tiles):
    lane = lanes()
    zero = jnp.zeros((RANGE, LANES), jnp.float32)
    y_low, y_high, z_low, z_high = [[zero, zero] for _ in range(4)]
    for x in range(SIDE):
        part, place = x // 8, x % 8
        here = lane // SIDE == place
        y_low[part] = jnp.where(here, roll(tiles[x][0], SIDE * place), y_low[part])
        y_high[part] = jnp.where(here, roll(tiles[x][1], SIDE * place + SIDE), y_high[part])
        column = lane % SIDE == x
        for h in range(2):
            z_low[h] = jnp.where(column, roll(tiles[x][h], x), z_low[h])
            z_high[h] = jnp.where(column, roll(tiles[x][h], x - (SIDE - 1)), z_high[h])
    return [tiles[0], tiles[SIDE - 1], y_low, y_high, z_low, z_high]


def store_faces(ref, faces):
    for f in range(FACES):
        for h in range(2):
            ref[:, (2 * f + h) * LANES : (2 * f + h + 1) * LANES] = faces[f][h]


def load_face(ref, f, h, *lead):
    return ref[(*lead, slice(None), slice((2 * f + h) * LANES, (2 * f + h + 1) * LANES))]


def load_coarse(ref, core, member):
    start = (2 * FACES + member) * LANES
    return ref[core, :, start : start + LANES]


def pick_rows(tile, rows):
    return jnp.take_along_axis(tile, rows, axis=0)


def ghost_faces(links, base, before, own, after):
    ghosts, valid = [], []
    for d in range(FACES):
        link = jnp.broadcast_to(links[:, d : d + 1], (RANGE, LANES))
        local = link - base
        rows = link & (RANGE - 1)
        face = FLIPPED[d]
        halves = []
        for h in range(2):
            low = pick_rows(before(face, h), rows)
            mid = pick_rows(own(face, h), rows)
            high = pick_rows(after(face, h), rows)
            picked = jnp.where(local < 0, low, jnp.where(local >= RANGE, high, mid))
            halves.append(jnp.where(link >= 0, picked, 0.0))
        ghosts.append(halves)
        valid.append(link >= 0)
    return ghosts, valid


def beside(tiles, ghosts, x, h):
    lane = lanes()
    here = tiles[x][h]
    minus = tiles[x - 1][h] if x > 0 else ghosts[0][h]
    plus = tiles[x + 1][h] if x < SIDE - 1 else ghosts[1][h]
    total = minus + plus
    part, place = x // 8, x % 8
    if h == 0:
        outer_minus = roll(ghosts[2][part], -SIDE * place)
        outer_plus = roll(tiles[x][1], -SIDE)
    else:
        outer_minus = roll(tiles[x][0], SIDE)
        outer_plus = roll(ghosts[3][part], LANES - SIDE - SIDE * place)
    total = total + jnp.where(lane < SIDE, outer_minus, roll(here, SIDE))
    total = total + jnp.where(lane >= LANES - SIDE, outer_plus, roll(here, -SIDE))
    z = lane % SIDE
    total = total + jnp.where(z == 0, roll(ghosts[4][h], -x), roll(here, 1))
    total = total + jnp.where(z == SIDE - 1, roll(ghosts[5][h], SIDE - 1 - x), roll(here, -1))
    return total


def sweep(tiles, ghosts, source_ref, coefficient_ref):
    out = []
    for x in range(SIDE):
        out.append([])
        for h in range(2):
            weight = RELAXATION / (6.0 + coefficient_ref[2 * x + h])
            gathered = source_ref[2 * x + h] + beside(tiles, ghosts, x, h)
            out[x].append((1.0 - RELAXATION) * tiles[x][h] + weight * gathered)
    return out


def range_base():
    return lax.axis_index("d") // 2 * RANGE


def pack_kernel(p_ref, f_ref, c_ref, slot_ref, links_ref, out_ref, slots, links, sems):
    small = [pltpu.make_async_copy(slot_ref, slots, sems.at[3]), pltpu.make_async_copy(links_ref, links, sems.at[4])]
    large = [
        pltpu.make_async_copy(ref, out_ref.at[:, i * CELLS : (i + 1) * CELLS], sems.at[i])
        for i, ref in enumerate((p_ref, f_ref, c_ref))
    ]
    for copy in small + large:
        copy.start()
    for copy in small:
        copy.wait()
    lane = lanes()[: RANGE // 2]
    row = sublanes()[: RANGE // 2]
    tile = jnp.zeros((RANGE // 2, LANES), jnp.int32)
    for d in range(FACES):
        tile = jnp.where(lane == d, links[:, d : d + 1], tile)
    for i in range(RANGE // 2):
        tile = jnp.where(jnp.logical_and(lane == FACES, row == i), slots[i], tile)
    out_ref[:, 3 * CELLS :] = tile.astype(jnp.float32)
    for copy in large:
        copy.wait()


def reorder_kernel(packed_ref, p_out, f_out, c_out, links_out, faces_out):
    def both(start):
        span = slice(start, start + LANES)
        return jnp.concatenate([packed_ref[0, :, span], packed_ref[1, :, span]], axis=0)

    lane, row = lanes(), sublanes()
    names = both(3 * CELLS)
    links_out[...] = names.astype(jnp.int32)
    slot = jnp.broadcast_to(names[:, FACES : FACES + 1], (RANGE, LANES)).astype(jnp.int32)
    placed = jnp.sum(jnp.where(slot == lane, row, 0).astype(jnp.float32), axis=0, keepdims=True)
    chosen = jnp.sum(jnp.where(lane == row, placed, 0.0), axis=1, keepdims=True)
    rows = jnp.broadcast_to(chosen, (RANGE, LANES)).astype(jnp.int32)
    for i, target in enumerate((p_out, f_out, c_out)):
        for t in range(CELLS // LANES):
            target[t] = pick_rows(both(i * CELLS + t * LANES), rows)
    store_faces(faces_out, pack_faces(load(p_out)))


def window(met_ref, faces_ref):
    before = lambda f, h: load_face(met_ref, f, h, 1)
    own = lambda f, h: load_face(faces_ref, f, h)
    after = lambda f, h: load_face(met_ref, f, h, 0)
    return before, own, after


def sweep_kernel(u_ref, f_ref, c_ref, links_ref, faces_ref, met_ref, u_out, faces_out):
    ghosts, _ = ghost_faces(links_ref[...], range_base(), *window(met_ref, faces_ref))
    tiles = sweep(load(u_ref), ghosts, f_ref, c_ref)
    store(u_out, tiles)
    store_faces(faces_out, pack_faces(tiles))


def lane_sum(tile):
    return jnp.sum(tile, axis=1, keepdims=True)


def face_sums(face):
    return [lane_sum(face(FLIPPED[d], 0) + face(FLIPPED[d], 1)) * (1.0 / CELLS) for d in range(FACES)]


def coarse_kernel(u_ref, f_ref, c_ref, links_ref, faces_ref, coarse_out):
    links = links_ref[...]
    defect = jnp.zeros((RANGE, LANES), jnp.float32)
    weights = jnp.zeros((RANGE, LANES), jnp.float32)
    for t in range(CELLS // LANES):
        c = c_ref[t]
        defect = defect + (f_ref[t] - c * u_ref[t])
        weights = weights + c
    sums = face_sums(lambda f, h: load_face(faces_ref, f, h))
    inner = lane_sum(defect) * (1.0 / CELLS)
    for s in sums:
        inner = inner - s
    diag = 6.0 + lane_sum(weights) * (1.0 / CELLS)
    lane = lanes()
    tile = jnp.zeros((RANGE, LANES), jnp.float32)
    for d in range(FACES):
        tile = jnp.where(lane == d, sums[d], tile)
        tile = jnp.where(lane == RANGE + d, links[:, d : d + 1].astype(jnp.float32), tile)
    tile = jnp.where(lane == FACES, inner, tile)
    tile = jnp.where(lane == FACES + 1, diag, tile)
    for i in range(GROUP):
        coarse_out[i] = tile


def join_kernel(met_ref, coarse_ref, out_ref):
    width = FACES * 2 * LANES
    out_ref[:, :width] = met_ref[...]
    for i in range(GROUP):
        out_ref[:, width + i * LANES : width + (i + 1) * LANES] = coarse_ref[i]


def final_kernel(u_ref, f_ref, c_ref, links_ref, faces_ref, met_ref, out_ref):
    core, curve = lax.axis_index("d") % 2, lax.axis_index("d") // 2
    row = sublanes()
    nearest = []
    for i in range(GROUP):
        ahead = i - curve % GROUP
        aligned = jnp.logical_and(ahead >= -GROUP // 2, ahead < GROUP // 2)
        first = load_coarse(met_ref, 0, i)
        second = load_coarse(met_ref, 1, (i + GROUP // 2) % GROUP)
        nearest.append(jnp.where(aligned, first, second))
    values = jnp.concatenate(nearest, axis=0).T
    sums, names = values[:RANGE], values[RANGE : 2 * RANGE]
    valid = jnp.logical_and(names >= 0.0, row < FACES)
    at = names.astype(jnp.int32) & (LANES - 1)

    def named(tile):
        return jnp.where(valid, jnp.take_along_axis(tile, at, axis=1), 0.0)

    def total(tile):
        return jnp.broadcast_to(jnp.sum(tile, axis=0, keepdims=True), (RANGE, LANES))

    inner = jnp.broadcast_to(sums[FACES : FACES + 1], (RANGE, LANES))
    diag = jnp.broadcast_to(sums[FACES + 1 : FACES + 2], (RANGE, LANES))
    diag = jnp.where(diag > 0.0, diag, 1.0)
    residual = inner + total(named(sums))
    error = jnp.zeros((RANGE, LANES), jnp.float32)
    for step in range(COARSE_SWEEPS):
        near = total(named(error)) if step else 0.0
        error = error + RELAXATION * (residual - diag * error + near) / diag
    near = named(error)
    own = lanes() == curve % GROUP * RANGE + row
    lift = lane_sum(jnp.where(own, error, 0.0))
    ghosts, _ = ghost_faces(links_ref[...], range_base(), *window(met_ref, faces_ref))
    for d in range(FACES):
        raised = lane_sum(jnp.where(own, jnp.broadcast_to(near[d : d + 1], (RANGE, LANES)), 0.0))
        ghosts[d] = [half + raised for half in ghosts[d]]
    tiles = [[tile + lift for tile in pair] for pair in load(u_ref)]
    tiles = sweep(tiles, ghosts, f_ref, c_ref)
    for x in range(SIDE):
        for h in range(2):
            tile = tiles[x][h]
            half = jnp.where(core == 0, tile[0 : RANGE // 2], tile[RANGE // 2 :])
            t = 2 * x + h
            out_ref[:, t * LANES : (t + 1) * LANES] = half


def call(kernel, out_shape, *args, specs=None, scratch=()):
    many = isinstance(out_shape, (list, tuple))
    return pl.pallas_call(
        kernel,
        out_shape=out_shape,
        in_specs=specs or [VMEM] * len(args),
        out_specs=[VMEM] * len(out_shape) if many else VMEM,
        scratch_shapes=scratch,
        compiler_params=pltpu.CompilerParams(vmem_limit_bytes=GRANT),
    )(*args)


def on_device(groups, pressure, source_term, coefficient, new_slot, face_links):
    cores, groups16, exchange = groups
    meet = lambda array: lax.ppermute(array, "d", exchange)
    gather = lambda array, members: lax.all_gather(array, "d", axis=0, axis_index_groups=members)
    field = f32(CELLS // LANES, RANGE, LANES)
    packed = f32(RANGE, FACES * 2 * LANES)
    whole = call(
        pack_kernel,
        f32(RANGE // 2, PACKED),
        *[
            pltpu.with_memory_space_constraint(array, pltpu.HBM)
            for array in (pressure, source_term, coefficient, new_slot, face_links)
        ],
        specs=[HBM] * 5,
        scratch=[
            pltpu.SMEM((RANGE // 2,), jnp.int32),
            pltpu.VMEM((RANGE // 2, FACES), jnp.int32),
            pltpu.SemaphoreType.DMA((5,)),
        ],
    )
    u, f, c, links, faces = call(
        reorder_kernel,
        [field, field, field, jax.ShapeDtypeStruct((RANGE, LANES), jnp.int32), packed],
        gather(whole, cores),
    )
    met = gather(meet(faces), cores)
    u, faces = call(sweep_kernel, [field, packed], u, f, c, links, faces, met)
    met = gather(meet(faces), cores)
    u, faces = call(sweep_kernel, [field, packed], u, f, c, links, faces, met)
    met = meet(faces)
    coarse = call(coarse_kernel, pltpu.VMEM((GROUP, RANGE, LANES), jnp.float32), u, f, c, links, faces)
    coarse = lax.all_to_all(coarse, "d", 0, 0, axis_index_groups=groups16, tiled=True)
    joined = call(join_kernel, f32(RANGE, (2 * FACES + GROUP) * LANES), met, coarse)
    return call(final_kernel, f32(RANGE // 2, CELLS), u, f, c, links, faces, gather(joined, cores))


def solution(mesh):
    devices = mesh.devices.reshape(-1)
    count = devices.size // 2
    cores = [[2 * i, 2 * i + 1] for i in range(count)]
    groups16 = [
        [2 * ((i + core * GROUP // 2 + k) % count) + core for k in range(GROUP)]
        for i in range(0, count, GROUP)
        for core in range(2)
    ]
    exchange = [pair for i in range(count - 1) for pair in ((2 * i, 2 * i + 3), (2 * i + 3, 2 * i))]
    split, line = P("d", None), P("d")
    return jax.shard_map(
        functools.partial(on_device, (cores, groups16, exchange)),
        mesh=Mesh(devices, ("d",)),
        in_specs=(split, split, split, line, split),
        out_specs=split,
        check_vma=False,
    )
```

```python
import functools

import jax
import jax.numpy as jnp
from jax import lax
from jax.experimental import pallas as pl
from jax.experimental.pallas import tpu as pltpu
from jax.sharding import Mesh, PartitionSpec as P


COARSE_SWEEPS = 4
RELAXATION = 0.8

SIDE = 16
RANGE = 8
LANES = 128
CELLS = 4096
FACES = 6
FLIPPED = (1, 0, 3, 2, 5, 4)
GROUP = 16
PACKED = 3 * CELLS + LANES

VMEM = pl.BlockSpec(memory_space=pltpu.VMEM)
HBM = pl.BlockSpec(memory_space=pltpu.HBM)
GRANT = 4 * 1024 * 1024


def f32(*shape):
    return jax.ShapeDtypeStruct(shape, jnp.float32)


def lanes():
    return lax.broadcasted_iota(jnp.int32, (RANGE, LANES), 1)


def sublanes():
    return lax.broadcasted_iota(jnp.int32, (RANGE, LANES), 0)


def roll(tile, amount):
    amount = amount % LANES
    return tile if amount == 0 else pltpu.roll(tile, amount, 1)


def load(ref):
    return [[ref[2 * x + h] for h in range(2)] for x in range(SIDE)]


def store(ref, tiles):
    for x in range(SIDE):
        for h in range(2):
            ref[2 * x + h] = tiles[x][h]


def pack_faces(tiles):
    lane = lanes()
    zero = jnp.zeros((RANGE, LANES), jnp.float32)
    y_low, y_high, z_low, z_high = [[zero, zero] for _ in range(4)]
    for x in range(SIDE):
        part, place = x // 8, x % 8
        here = lane // SIDE == place
        y_low[part] = jnp.where(here, roll(tiles[x][0], SIDE * place), y_low[part])
        y_high[part] = jnp.where(here, roll(tiles[x][1], SIDE * place + SIDE), y_high[part])
        column = lane % SIDE == x
        for h in range(2):
            z_low[h] = jnp.where(column, roll(tiles[x][h], x), z_low[h])
            z_high[h] = jnp.where(column, roll(tiles[x][h], x - (SIDE - 1)), z_high[h])
    return [tiles[0], tiles[SIDE - 1], y_low, y_high, z_low, z_high]


def store_faces(ref, faces):
    for f in range(FACES):
        for h in range(2):
            ref[:, (2 * f + h) * LANES : (2 * f + h + 1) * LANES] = faces[f][h]


def load_face(ref, f, h, *lead):
    return ref[(*lead, slice(None), slice((2 * f + h) * LANES, (2 * f + h + 1) * LANES))]


def pick_rows(tile, rows):
    return jnp.take_along_axis(tile, rows, axis=0)


def ghost_faces(links, base, before, own, after):
    ghosts, valid = [], []
    for d in range(FACES):
        link = jnp.broadcast_to(links[:, d : d + 1], (RANGE, LANES))
        local = link - base
        rows = link & (RANGE - 1)
        face = FLIPPED[d]
        halves = []
        for h in range(2):
            low = pick_rows(before(face, h), rows)
            mid = pick_rows(own(face, h), rows)
            high = pick_rows(after(face, h), rows)
            picked = jnp.where(local < 0, low, jnp.where(local >= RANGE, high, mid))
            halves.append(jnp.where(link >= 0, picked, 0.0))
        ghosts.append(halves)
        valid.append(link >= 0)
    return ghosts, valid


def beside(tiles, ghosts, x, h):
    lane = lanes()
    here = tiles[x][h]
    minus = tiles[x - 1][h] if x > 0 else ghosts[0][h]
    plus = tiles[x + 1][h] if x < SIDE - 1 else ghosts[1][h]
    total = minus + plus
    part, place = x // 8, x % 8
    if h == 0:
        outer_minus = roll(ghosts[2][part], -SIDE * place)
        outer_plus = roll(tiles[x][1], -SIDE)
    else:
        outer_minus = roll(tiles[x][0], SIDE)
        outer_plus = roll(ghosts[3][part], LANES - SIDE - SIDE * place)
    total = total + jnp.where(lane < SIDE, outer_minus, roll(here, SIDE))
    total = total + jnp.where(lane >= LANES - SIDE, outer_plus, roll(here, -SIDE))
    z = lane % SIDE
    total = total + jnp.where(z == 0, roll(ghosts[4][h], -x), roll(here, 1))
    total = total + jnp.where(z == SIDE - 1, roll(ghosts[5][h], SIDE - 1 - x), roll(here, -1))
    return total


def sweep(tiles, ghosts, source_ref, coefficient_ref):
    out = []
    for x in range(SIDE):
        out.append([])
        for h in range(2):
            weight = RELAXATION / (6.0 + coefficient_ref[2 * x + h])
            gathered = source_ref[2 * x + h] + beside(tiles, ghosts, x, h)
            out[x].append((1.0 - RELAXATION) * tiles[x][h] + weight * gathered)
    return out


def range_base():
    return lax.axis_index("d") // 2 * RANGE


def pack_kernel(p_ref, f_ref, c_ref, slot_ref, links_ref, out_ref, slots, links, sems):
    small = [pltpu.make_async_copy(slot_ref, slots, sems.at[3]), pltpu.make_async_copy(links_ref, links, sems.at[4])]
    large = [
        pltpu.make_async_copy(ref, out_ref.at[:, i * CELLS : (i + 1) * CELLS], sems.at[i])
        for i, ref in enumerate((p_ref, f_ref, c_ref))
    ]
    for copy in small + large:
        copy.start()
    for copy in small:
        copy.wait()
    lane = lanes()[: RANGE // 2]
    row = sublanes()[: RANGE // 2]
    tile = jnp.zeros((RANGE // 2, LANES), jnp.int32)
    for d in range(FACES):
        tile = jnp.where(lane == d, links[:, d : d + 1], tile)
    for i in range(RANGE // 2):
        tile = jnp.where(jnp.logical_and(lane == FACES, row == i), slots[i], tile)
    out_ref[:, 3 * CELLS :] = tile.astype(jnp.float32)
    for copy in large:
        copy.wait()


def reorder_kernel(packed_ref, p_out, f_out, c_out, links_out, faces_out):
    def both(start):
        span = slice(start, start + LANES)
        return jnp.concatenate([packed_ref[0, :, span], packed_ref[1, :, span]], axis=0)

    lane, row = lanes(), sublanes()
    names = both(3 * CELLS)
    links_out[...] = names.astype(jnp.int32)
    slot = jnp.broadcast_to(names[:, FACES : FACES + 1], (RANGE, LANES)).astype(jnp.int32)
    placed = jnp.sum(jnp.where(slot == lane, row, 0).astype(jnp.float32), axis=0, keepdims=True)
    chosen = jnp.sum(jnp.where(lane == row, placed, 0.0), axis=1, keepdims=True)
    rows = jnp.broadcast_to(chosen, (RANGE, LANES)).astype(jnp.int32)
    for i, target in enumerate((p_out, f_out, c_out)):
        for t in range(CELLS // LANES):
            target[t] = pick_rows(both(i * CELLS + t * LANES), rows)
    store_faces(faces_out, pack_faces(load(p_out)))


def window(met_ref, faces_ref):
    before = lambda f, h: load_face(met_ref, f, h, 1)
    own = lambda f, h: load_face(faces_ref, f, h)
    after = lambda f, h: load_face(met_ref, f, h, 0)
    return before, own, after


def sweep_kernel(u_ref, f_ref, c_ref, links_ref, faces_ref, met_ref, u_out, faces_out):
    ghosts, _ = ghost_faces(links_ref[...], range_base(), *window(met_ref, faces_ref))
    tiles = sweep(load(u_ref), ghosts, f_ref, c_ref)
    store(u_out, tiles)
    store_faces(faces_out, pack_faces(tiles))


def lane_sum(tile):
    return jnp.sum(tile, axis=1, keepdims=True)


def face_sums(face):
    return [lane_sum(face(FLIPPED[d], 0) + face(FLIPPED[d], 1)) * (1.0 / CELLS) for d in range(FACES)]


def coarse_kernel(u_ref, f_ref, c_ref, links_ref, faces_ref, coarse_out):
    links = links_ref[...]
    defect = jnp.zeros((RANGE, LANES), jnp.float32)
    weights = jnp.zeros((RANGE, LANES), jnp.float32)
    for t in range(CELLS // LANES):
        c = c_ref[t]
        defect = defect + (f_ref[t] - c * u_ref[t])
        weights = weights + c
    sums = face_sums(lambda f, h: load_face(faces_ref, f, h))
    inner = lane_sum(defect) * (1.0 / CELLS)
    for s in sums:
        inner = inner - s
    diag = 6.0 + lane_sum(weights) * (1.0 / CELLS)
    lane = lanes()
    tile = jnp.zeros((RANGE, LANES), jnp.float32)
    for d in range(FACES):
        tile = jnp.where(lane == d, sums[d], tile)
        tile = jnp.where(lane == RANGE + d, links[:, d : d + 1].astype(jnp.float32), tile)
    tile = jnp.where(lane == FACES, inner, tile)
    tile = jnp.where(lane == FACES + 1, diag, tile)
    for i in range(GROUP):
        coarse_out[i] = tile


def turn_kernel(coarse_ref, out_ref):
    values = jnp.concatenate([coarse_ref[i] for i in range(GROUP)], axis=0).T
    out_ref[:, :LANES] = values[:RANGE]
    out_ref[:, LANES:] = values[RANGE : 2 * RANGE]


def join_kernel(met_ref, turned_ref, out_ref):
    width = FACES * 2 * LANES
    out_ref[:, :width] = met_ref[...]
    out_ref[:, width:] = turned_ref[...]


def final_kernel(u_ref, f_ref, c_ref, links_ref, faces_ref, met_ref, out_ref):
    core, curve = lax.axis_index("d") % 2, lax.axis_index("d") // 2
    row = sublanes()
    ahead = lanes() // RANGE - curve % GROUP
    aligned = jnp.logical_and(ahead >= -GROUP // 2, ahead < GROUP // 2)
    sums, names = [
        jnp.where(aligned, load_face(met_ref, FACES, h, 0), roll(load_face(met_ref, FACES, h, 1), LANES // 2))
        for h in range(2)
    ]
    valid = jnp.logical_and(names >= 0.0, row < FACES)
    at = names.astype(jnp.int32) & (LANES - 1)

    def named(tile):
        return jnp.where(valid, jnp.take_along_axis(tile, at, axis=1), 0.0)

    def total(tile):
        return jnp.broadcast_to(jnp.sum(tile, axis=0, keepdims=True), (RANGE, LANES))

    inner = jnp.broadcast_to(sums[FACES : FACES + 1], (RANGE, LANES))
    diag = jnp.broadcast_to(sums[FACES + 1 : FACES + 2], (RANGE, LANES))
    diag = jnp.where(diag > 0.0, diag, 1.0)
    residual = inner + total(named(sums))
    error = jnp.zeros((RANGE, LANES), jnp.float32)
    for step in range(COARSE_SWEEPS):
        near = total(named(error)) if step else 0.0
        error = error + RELAXATION * (residual - diag * error + near) / diag
    near = named(error)
    own = lanes() == curve % GROUP * RANGE + row
    lift = lane_sum(jnp.where(own, error, 0.0))
    ghosts, _ = ghost_faces(links_ref[...], range_base(), *window(met_ref, faces_ref))
    for d in range(FACES):
        raised = lane_sum(jnp.where(own, jnp.broadcast_to(near[d : d + 1], (RANGE, LANES)), 0.0))
        ghosts[d] = [half + raised for half in ghosts[d]]
    tiles = [[tile + lift for tile in pair] for pair in load(u_ref)]
    tiles = sweep(tiles, ghosts, f_ref, c_ref)
    for x in range(SIDE):
        for h in range(2):
            tile = tiles[x][h]
            half = jnp.where(core == 0, tile[0 : RANGE // 2], tile[RANGE // 2 :])
            t = 2 * x + h
            out_ref[:, t * LANES : (t + 1) * LANES] = half


def call(kernel, out_shape, *args, specs=None, scratch=()):
    many = isinstance(out_shape, (list, tuple))
    return pl.pallas_call(
        kernel,
        out_shape=out_shape,
        in_specs=specs or [VMEM] * len(args),
        out_specs=[VMEM] * len(out_shape) if many else VMEM,
        scratch_shapes=scratch,
        compiler_params=pltpu.CompilerParams(vmem_limit_bytes=GRANT),
    )(*args)


def on_device(groups, pressure, source_term, coefficient, new_slot, face_links):
    cores, groups16, exchange = groups
    meet = lambda array: lax.ppermute(array, "d", exchange)
    gather = lambda array, members: lax.all_gather(array, "d", axis=0, axis_index_groups=members)
    field = f32(CELLS // LANES, RANGE, LANES)
    packed = f32(RANGE, FACES * 2 * LANES)
    whole = call(
        pack_kernel,
        f32(RANGE // 2, PACKED),
        *[
            pltpu.with_memory_space_constraint(array, pltpu.HBM)
            for array in (pressure, source_term, coefficient, new_slot, face_links)
        ],
        specs=[HBM] * 5,
        scratch=[
            pltpu.SMEM((RANGE // 2,), jnp.int32),
            pltpu.VMEM((RANGE // 2, FACES), jnp.int32),
            pltpu.SemaphoreType.DMA((5,)),
        ],
    )
    u, f, c, links, faces = call(
        reorder_kernel,
        [field, field, field, jax.ShapeDtypeStruct((RANGE, LANES), jnp.int32), packed],
        gather(whole, cores),
    )
    met = gather(meet(faces), cores)
    u, faces = call(sweep_kernel, [field, packed], u, f, c, links, faces, met)
    met = gather(meet(faces), cores)
    u, faces = call(sweep_kernel, [field, packed], u, f, c, links, faces, met)
    met = meet(faces)
    coarse = call(coarse_kernel, pltpu.VMEM((GROUP, RANGE, LANES), jnp.float32), u, f, c, links, faces)
    coarse = lax.all_to_all(coarse, "d", 0, 0, axis_index_groups=groups16, tiled=True)
    turned = call(turn_kernel, f32(RANGE, 2 * LANES), coarse)
    joined = call(join_kernel, f32(RANGE, (FACES + 1) * 2 * LANES), met, turned)
    return call(final_kernel, f32(RANGE // 2, CELLS), u, f, c, links, faces, gather(joined, cores))


def solution(mesh):
    devices = mesh.devices.reshape(-1)
    count = devices.size // 2
    cores = [[2 * i, 2 * i + 1] for i in range(count)]
    groups16 = [
        [2 * ((i + core * GROUP // 2 + k) % count) + core for k in range(GROUP)]
        for i in range(0, count, GROUP)
        for core in range(2)
    ]
    exchange = [pair for i in range(count - 1) for pair in ((2 * i, 2 * i + 3), (2 * i + 3, 2 * i))]
    split, line = P("d", None), P("d")
    return jax.shard_map(
        functools.partial(on_device, (cores, groups16, exchange)),
        mesh=Mesh(devices, ("d",)),
        in_specs=(split, split, split, line, split),
        out_specs=split,
        check_vma=False,
    )
```

```python
import functools

import jax
import jax.numpy as jnp
from jax import lax
from jax.experimental import pallas as pl
from jax.experimental.pallas import tpu as pltpu
from jax.sharding import Mesh, PartitionSpec as P

COARSE_SWEEPS = 4
RELAXATION = 0.8

SIDE = 16
RANGE = 8
LANES = 128
CELLS = 4096
FACES = 6
FLIPPED = (1, 0, 3, 2, 5, 4)
ROW = 4
SLOTS = 16
PACKED = 3 * CELLS + LANES

VMEM = pl.BlockSpec(memory_space=pltpu.VMEM)
HBM = pl.BlockSpec(memory_space=pltpu.HBM)
GRANT = 4 * 1024 * 1024


def f32(*shape):
    return jax.ShapeDtypeStruct(shape, jnp.float32)


def lanes():
    return lax.broadcasted_iota(jnp.int32, (RANGE, LANES), 1)


def sublanes():
    return lax.broadcasted_iota(jnp.int32, (RANGE, LANES), 0)


def roll(tile, amount):
    amount = amount % LANES
    return tile if amount == 0 else pltpu.roll(tile, amount, 1)


def load(ref):
    return [[ref[2 * x + h] for h in range(2)] for x in range(SIDE)]


def store(ref, tiles):
    for x in range(SIDE):
        for h in range(2):
            ref[2 * x + h] = tiles[x][h]


def pack_faces(tiles):
    lane = lanes()
    zero = jnp.zeros((RANGE, LANES), jnp.float32)
    y_low, y_high, z_low, z_high = [[zero, zero] for _ in range(4)]
    for x in range(SIDE):
        part, place = x // 8, x % 8
        here = lane // SIDE == place
        y_low[part] = jnp.where(here, roll(tiles[x][0], SIDE * place), y_low[part])
        y_high[part] = jnp.where(here, roll(tiles[x][1], SIDE * place + SIDE), y_high[part])
        column = lane % SIDE == x
        for h in range(2):
            z_low[h] = jnp.where(column, roll(tiles[x][h], x), z_low[h])
            z_high[h] = jnp.where(column, roll(tiles[x][h], x - (SIDE - 1)), z_high[h])
    return [tiles[0], tiles[SIDE - 1], y_low, y_high, z_low, z_high]


def store_faces(ref, faces):
    for f in range(FACES):
        for h in range(2):
            ref[:, (2 * f + h) * LANES : (2 * f + h + 1) * LANES] = faces[f][h]


def load_face(ref, f, h, *lead):
    return ref[(*lead, slice(None), slice((2 * f + h) * LANES, (2 * f + h + 1) * LANES))]


def pick_rows(tile, rows):
    return jnp.take_along_axis(tile, rows, axis=0)


def ghost_faces(links, base, before, own, after):
    ghosts, valid = [], []
    for d in range(FACES):
        link = jnp.broadcast_to(links[:, d : d + 1], (RANGE, LANES))
        local = link - base
        rows = link & (RANGE - 1)
        face = FLIPPED[d]
        halves = []
        for h in range(2):
            low = pick_rows(before(face, h), rows)
            mid = pick_rows(own(face, h), rows)
            high = pick_rows(after(face, h), rows)
            picked = jnp.where(local < 0, low, jnp.where(local >= RANGE, high, mid))
            halves.append(jnp.where(link >= 0, picked, 0.0))
        ghosts.append(halves)
        valid.append(link >= 0)
    return ghosts, valid


def beside(tiles, ghosts, x, h):
    lane = lanes()
    here = tiles[x][h]
    minus = tiles[x - 1][h] if x > 0 else ghosts[0][h]
    plus = tiles[x + 1][h] if x < SIDE - 1 else ghosts[1][h]
    total = minus + plus
    part, place = x // 8, x % 8
    if h == 0:
        outer_minus = roll(ghosts[2][part], -SIDE * place)
        outer_plus = roll(tiles[x][1], -SIDE)
    else:
        outer_minus = roll(tiles[x][0], SIDE)
        outer_plus = roll(ghosts[3][part], LANES - SIDE - SIDE * place)
    total = total + jnp.where(lane < SIDE, outer_minus, roll(here, SIDE))
    total = total + jnp.where(lane >= LANES - SIDE, outer_plus, roll(here, -SIDE))
    z = lane % SIDE
    total = total + jnp.where(z == 0, roll(ghosts[4][h], -x), roll(here, 1))
    total = total + jnp.where(z == SIDE - 1, roll(ghosts[5][h], SIDE - 1 - x), roll(here, -1))
    return total


def sweep(tiles, ghosts, source_ref, coefficient_ref):
    out = []
    for x in range(SIDE):
        out.append([])
        for h in range(2):
            weight = RELAXATION / (6.0 + coefficient_ref[2 * x + h])
            gathered = source_ref[2 * x + h] + beside(tiles, ghosts, x, h)
            out[x].append((1.0 - RELAXATION) * tiles[x][h] + weight * gathered)
    return out


def range_base():
    return lax.axis_index("d") // 2 * RANGE


def pack_kernel(p_ref, f_ref, c_ref, slot_ref, links_ref, out_ref, slots, links, sems):
    small = [pltpu.make_async_copy(slot_ref, slots, sems.at[3]), pltpu.make_async_copy(links_ref, links, sems.at[4])]
    large = [
        pltpu.make_async_copy(ref, out_ref.at[:, i * CELLS : (i + 1) * CELLS], sems.at[i])
        for i, ref in enumerate((p_ref, f_ref, c_ref))
    ]
    for copy in small + large:
        copy.start()
    for copy in small:
        copy.wait()
    lane = lanes()[: RANGE // 2]
    row = sublanes()[: RANGE // 2]
    tile = jnp.zeros((RANGE // 2, LANES), jnp.int32)
    for d in range(FACES):
        tile = jnp.where(lane == d, links[:, d : d + 1], tile)
    for i in range(RANGE // 2):
        tile = jnp.where(jnp.logical_and(lane == FACES, row == i), slots[i], tile)
    out_ref[:, 3 * CELLS :] = tile.astype(jnp.float32)
    for copy in large:
        copy.wait()


def reorder_kernel(packed_ref, p_out, f_out, c_out, links_out, faces_out):
    def both(start):
        span = slice(start, start + LANES)
        return jnp.concatenate([packed_ref[0, :, span], packed_ref[1, :, span]], axis=0)

    lane, row = lanes(), sublanes()
    names = both(3 * CELLS)
    links_out[...] = names.astype(jnp.int32)
    slot = jnp.broadcast_to(names[:, FACES : FACES + 1], (RANGE, LANES)).astype(jnp.int32)
    placed = jnp.sum(jnp.where(slot == lane, row, 0).astype(jnp.float32), axis=0, keepdims=True)
    chosen = jnp.sum(jnp.where(lane == row, placed, 0.0), axis=1, keepdims=True)
    rows = jnp.broadcast_to(chosen, (RANGE, LANES)).astype(jnp.int32)
    for i, target in enumerate((p_out, f_out, c_out)):
        for t in range(CELLS // LANES):
            target[t] = pick_rows(both(i * CELLS + t * LANES), rows)
    store_faces(faces_out, pack_faces(load(p_out)))


def window(met_ref, faces_ref):
    before = lambda f, h: load_face(met_ref, f, h, 1)
    own = lambda f, h: load_face(faces_ref, f, h)
    after = lambda f, h: load_face(met_ref, f, h, 0)
    return before, own, after


def sweep_kernel(u_ref, f_ref, c_ref, links_ref, faces_ref, met_ref, u_out, faces_out):
    ghosts, _ = ghost_faces(links_ref[...], range_base(), *window(met_ref, faces_ref))
    tiles = sweep(load(u_ref), ghosts, f_ref, c_ref)
    store(u_out, tiles)
    store_faces(faces_out, pack_faces(tiles))


def lane_sum(tile):
    return jnp.sum(tile, axis=1, keepdims=True)


def face_sums(face):
    return [lane_sum(face(FLIPPED[d], 0) + face(FLIPPED[d], 1)) * (1.0 / CELLS) for d in range(FACES)]


def coarse_kernel(u_ref, f_ref, c_ref, links_ref, faces_ref, coarse_out):
    links = links_ref[...]
    defect = jnp.zeros((RANGE, LANES), jnp.float32)
    weights = jnp.zeros((RANGE, LANES), jnp.float32)
    for t in range(CELLS // LANES):
        c = c_ref[t]
        defect = defect + (f_ref[t] - c * u_ref[t])
        weights = weights + c
    sums = face_sums(lambda f, h: load_face(faces_ref, f, h))
    inner = lane_sum(defect) * (1.0 / CELLS)
    for s in sums:
        inner = inner - s
    diag = 6.0 + lane_sum(weights) * (1.0 / CELLS)
    lane = lanes()
    tile = jnp.zeros((RANGE, LANES), jnp.float32)
    for d in range(FACES):
        tile = jnp.where(lane == d, sums[d], tile)
        tile = jnp.where(lane == RANGE + d, links[:, d : d + 1].astype(jnp.float32), tile)
    tile = jnp.where(lane == FACES, inner, tile)
    tile = jnp.where(lane == FACES + 1, diag, tile)
    coarse_out[...] = tile


def row_kernel(row_ref, met_ref, out_ref):
    core, curve = lax.axis_index("d") % 2, lax.axis_index("d") // 2
    met = jnp.where(core == 0, curve + 1, curve + SLOTS - 1) % SLOTS
    lane = lanes()
    edge = jnp.zeros((RANGE, LANES), jnp.float32)
    for d, column in enumerate(face_sums(lambda f, h: load_face(met_ref, f, h))):
        edge = jnp.where(lane == d, column, edge)
    tiles = []
    for slot in range(SLOTS):
        place = slot % ROW
        own = slot // ROW == curve // ROW % (SLOTS // ROW)
        other = jnp.where(slot == met, edge, 0.0)
        tiles.append(jnp.where(own, row_ref[place // 2, place % 2], other))
    values = jnp.concatenate(tiles, axis=0).T
    out_ref[:, :LANES] = values[:RANGE]
    out_ref[:, LANES:] = values[RANGE : 2 * RANGE]


def join_kernel(met_ref, far_ref, out_ref):
    width = FACES * 2 * LANES
    out_ref[:, :width] = met_ref[...]
    out_ref[:, width:] = far_ref[...]


def final_kernel(u_ref, f_ref, c_ref, links_ref, faces_ref, row_ref, met_ref, out_ref):
    core, curve = lax.axis_index("d") % 2, lax.axis_index("d") // 2
    row = sublanes()
    part = (lanes() // (ROW * RANGE) + SLOTS // ROW - curve // ROW % (SLOTS // ROW)) % (SLOTS // ROW)
    first = jnp.logical_or(part == 3, jnp.logical_and(part == 2, curve % ROW == 0))
    sums, names = [
        jnp.where(
            part == 0,
            row_ref[:, h * LANES : (h + 1) * LANES],
            jnp.where(first, load_face(met_ref, FACES, h, 0), load_face(met_ref, FACES, h, 1)),
        )
        for h in range(2)
    ]
    valid = jnp.logical_and(names >= 0.0, row < FACES)
    at = names.astype(jnp.int32) & (LANES - 1)

    def named(tile):
        return jnp.where(valid, jnp.take_along_axis(tile, at, axis=1), 0.0)

    def total(tile):
        return jnp.broadcast_to(jnp.sum(tile, axis=0, keepdims=True), (RANGE, LANES))

    inner = jnp.broadcast_to(sums[FACES : FACES + 1], (RANGE, LANES))
    diag = jnp.broadcast_to(sums[FACES + 1 : FACES + 2], (RANGE, LANES))
    diag = jnp.where(diag > 0.0, diag, 1.0)
    residual = inner + total(named(sums))
    error = jnp.zeros((RANGE, LANES), jnp.float32)
    for step in range(COARSE_SWEEPS):
        near = total(named(error)) if step else 0.0
        error = error + RELAXATION * (residual - diag * error + near) / diag
    near = named(error)
    own = lanes() == curve % SLOTS * RANGE + row
    lift = lane_sum(jnp.where(own, error, 0.0))
    ghosts, _ = ghost_faces(links_ref[...], range_base(), *window(met_ref, faces_ref))
    for d in range(FACES):
        raised = lane_sum(jnp.where(own, jnp.broadcast_to(near[d : d + 1], (RANGE, LANES)), 0.0))
        ghosts[d] = [half + raised for half in ghosts[d]]
    tiles = [[tile + lift for tile in pair] for pair in load(u_ref)]
    tiles = sweep(tiles, ghosts, f_ref, c_ref)
    for x in range(SIDE):
        for h in range(2):
            tile = tiles[x][h]
            half = jnp.where(core == 0, tile[0 : RANGE // 2], tile[RANGE // 2 :])
            t = 2 * x + h
            out_ref[:, t * LANES : (t + 1) * LANES] = half


def call(kernel, out_shape, *args, specs=None, scratch=()):
    many = isinstance(out_shape, (list, tuple))
    return pl.pallas_call(
        kernel,
        out_shape=out_shape,
        in_specs=specs or [VMEM] * len(args),
        out_specs=[VMEM] * len(out_shape) if many else VMEM,
        scratch_shapes=scratch,
        compiler_params=pltpu.CompilerParams(vmem_limit_bytes=GRANT),
    )(*args)


def on_device(groups, pressure, source_term, coefficient, new_slot, face_links):
    cores, along, across, exchange, far = groups
    gather = lambda array, members: lax.all_gather(array, "d", axis=0, axis_index_groups=members)
    meet = lambda array: lax.ppermute(array, "d", exchange)
    field = f32(CELLS // LANES, RANGE, LANES)
    packed = f32(RANGE, FACES * 2 * LANES)
    whole = call(
        pack_kernel,
        f32(RANGE // 2, PACKED),
        *[
            pltpu.with_memory_space_constraint(array, pltpu.HBM)
            for array in (pressure, source_term, coefficient, new_slot, face_links)
        ],
        specs=[HBM] * 5,
        scratch=[
            pltpu.SMEM((RANGE // 2,), jnp.int32),
            pltpu.VMEM((RANGE // 2, FACES), jnp.int32),
            pltpu.SemaphoreType.DMA((5,)),
        ],
    )
    u, f, c, links, faces = call(
        reorder_kernel,
        [field, field, field, jax.ShapeDtypeStruct((RANGE, LANES), jnp.int32), packed],
        gather(whole, cores),
    )
    met = gather(meet(faces), cores)
    u, faces = call(sweep_kernel, [field, packed], u, f, c, links, faces, met)
    met = gather(meet(faces), cores)
    u, faces = call(sweep_kernel, [field, packed], u, f, c, links, faces, met)
    met = meet(faces)
    coarse = call(coarse_kernel, f32(RANGE, LANES), u, f, c, links, faces)
    coarse = gather(coarse, along)
    coarse = gather(coarse, across)
    row = call(row_kernel, f32(RANGE, 2 * LANES), coarse, met)
    joined = call(join_kernel, f32(RANGE, (FACES + 1) * 2 * LANES), met, lax.ppermute(row, "d", far))
    return call(final_kernel, f32(RANGE // 2, CELLS), u, f, c, links, faces, row, gather(joined, cores))


def solution(mesh):
    devices = mesh.devices.reshape(-1)
    count = devices.size // 2
    cores = [[2 * i, 2 * i + 1] for i in range(count)]
    firsts = [2 * i + core for i in range(0, count, ROW) for core in range(2)]
    along = [[i + k, i + k + 2] for i in firsts for k in (0, 4)]
    across = [[i + k, i + 6 - k] for i in firsts for k in (0, 2)]
    far = [
        pair
        for i in range(count - ROW)
        for pair in ((2 * i + 1, 2 * (i + ROW)), (2 * (i + ROW), 2 * i + 1))
    ]
    exchange = [pair for i in range(count - 1) for pair in ((2 * i, 2 * i + 3), (2 * i + 3, 2 * i))]
    split, line = P("d", None), P("d")
    return jax.shard_map(
        functools.partial(on_device, (cores, along, across, exchange, far)),
        mesh=Mesh(devices, ("d",)),
        in_specs=(split, split, split, line, split),
        out_specs=split,
        check_vma=False,
    )
```

```python
import functools

import jax
import jax.numpy as jnp
from jax import lax
from jax.experimental import pallas as pl
from jax.experimental.pallas import tpu as pltpu
from jax.sharding import Mesh, PartitionSpec as P

PRE_SWEEPS = 2
COARSE_SWEEPS = 4
RELAXATION = 0.8

SIDE = 16
RANGE = 8
LANES = 128
CELLS = 4096
FACES = 6
FLIPPED = (1, 0, 3, 2, 5, 4)
ROW = 4
SLOTS = 16
PACKED = CELLS + LANES

VMEM = pl.BlockSpec(memory_space=pltpu.VMEM)
HBM = pl.BlockSpec(memory_space=pltpu.HBM)
GRANT = 4 * 1024 * 1024


def f32(*shape):
    return jax.ShapeDtypeStruct(shape, jnp.float32)


def lanes():
    return lax.broadcasted_iota(jnp.int32, (RANGE, LANES), 1)


def sublanes():
    return lax.broadcasted_iota(jnp.int32, (RANGE, LANES), 0)


def roll(tile, amount):
    amount = amount % LANES
    return tile if amount == 0 else pltpu.roll(tile, amount, 1)


def load(ref):
    return [[ref[2 * x + h] for h in range(2)] for x in range(SIDE)]


def store(ref, tiles):
    for x in range(SIDE):
        for h in range(2):
            ref[2 * x + h] = tiles[x][h]


def pack_faces(tiles):
    lane = lanes()
    zero = jnp.zeros((RANGE, LANES), jnp.float32)
    y_low, y_high, z_low, z_high = [[zero, zero] for _ in range(4)]
    for x in range(SIDE):
        part, place = x // 8, x % 8
        here = lane // SIDE == place
        y_low[part] = jnp.where(here, roll(tiles[x][0], SIDE * place), y_low[part])
        y_high[part] = jnp.where(here, roll(tiles[x][1], SIDE * place + SIDE), y_high[part])
        column = lane % SIDE == x
        for h in range(2):
            z_low[h] = jnp.where(column, roll(tiles[x][h], x), z_low[h])
            z_high[h] = jnp.where(column, roll(tiles[x][h], x - (SIDE - 1)), z_high[h])
    return [tiles[0], tiles[SIDE - 1], y_low, y_high, z_low, z_high]


def store_faces(ref, faces):
    for f in range(FACES):
        for h in range(2):
            ref[:, (2 * f + h) * LANES : (2 * f + h + 1) * LANES] = faces[f][h]


def load_face(ref, f, h, *lead):
    return ref[(*lead, slice(None), slice((2 * f + h) * LANES, (2 * f + h + 1) * LANES))]


def pick_rows(tile, rows):
    return jnp.take_along_axis(tile, rows, axis=0)


def ghost_faces(links, base, before, own, after):
    ghosts, valid = [], []
    for d in range(FACES):
        link = jnp.broadcast_to(links[:, d : d + 1], (RANGE, LANES))
        local = link - base
        rows = link & (RANGE - 1)
        face = FLIPPED[d]
        halves = []
        for h in range(2):
            low = pick_rows(before(face, h), rows)
            mid = pick_rows(own(face, h), rows)
            high = pick_rows(after(face, h), rows)
            picked = jnp.where(local < 0, low, jnp.where(local >= RANGE, high, mid))
            halves.append(jnp.where(link >= 0, picked, 0.0))
        ghosts.append(halves)
        valid.append(link >= 0)
    return ghosts, valid


def beside(tiles, ghosts, x, h):
    lane = lanes()
    here = tiles[x][h]
    minus = tiles[x - 1][h] if x > 0 else ghosts[0][h]
    plus = tiles[x + 1][h] if x < SIDE - 1 else ghosts[1][h]
    total = minus + plus
    part, place = x // 8, x % 8
    if h == 0:
        outer_minus = roll(ghosts[2][part], -SIDE * place)
        outer_plus = roll(tiles[x][1], -SIDE)
    else:
        outer_minus = roll(tiles[x][0], SIDE)
        outer_plus = roll(ghosts[3][part], LANES - SIDE - SIDE * place)
    total = total + jnp.where(lane < SIDE, outer_minus, roll(here, SIDE))
    total = total + jnp.where(lane >= LANES - SIDE, outer_plus, roll(here, -SIDE))
    z = lane % SIDE
    total = total + jnp.where(z == 0, roll(ghosts[4][h], -x), roll(here, 1))
    total = total + jnp.where(z == SIDE - 1, roll(ghosts[5][h], SIDE - 1 - x), roll(here, -1))
    return total


def sweep(tiles, ghosts, source_ref, coefficient_ref):
    out = []
    for x in range(SIDE):
        out.append([])
        for h in range(2):
            weight = RELAXATION / (6.0 + coefficient_ref[2 * x + h])
            gathered = source_ref[2 * x + h] + beside(tiles, ghosts, x, h)
            out[x].append((1.0 - RELAXATION) * tiles[x][h] + weight * gathered)
    return out


def range_base():
    return lax.axis_index("d") // 2 * RANGE


def pack_kernel(p_ref, f_ref, c_ref, slot_ref, links_ref, p_out, rest_out, slots, links, sems):
    targets = (p_out.at[:, :CELLS], rest_out.at[:, :CELLS], rest_out.at[:, CELLS:], slots, links)
    copies = [
        pltpu.make_async_copy(ref, target, sems.at[i])
        for i, (ref, target) in enumerate(zip((p_ref, f_ref, c_ref, slot_ref, links_ref), targets))
    ]
    for copy in copies[3:] + copies[:3]:
        copy.start()
    for copy in copies[3:]:
        copy.wait()
    lane = lanes()[: RANGE // 2]
    row = sublanes()[: RANGE // 2]
    tile = jnp.zeros((RANGE // 2, LANES), jnp.int32)
    for d in range(FACES):
        tile = jnp.where(lane == d, links[:, d : d + 1], tile)
    for i in range(RANGE // 2):
        tile = jnp.where(jnp.logical_and(lane == FACES, row == i), slots[i], tile)
    p_out[:, CELLS:] = tile.astype(jnp.float32)
    for copy in copies[:3]:
        copy.wait()


def both(ref, start):
    span = slice(start, start + LANES)
    return jnp.concatenate([ref[0, :, span], ref[1, :, span]], axis=0)


def reorder(ref, start, rows, target):
    for t in range(CELLS // LANES):
        target[t] = pick_rows(both(ref, start + t * LANES), rows)


def reorder_kernel(packed_ref, p_out, links_out, rows_out, faces_out):
    lane, row = lanes(), sublanes()
    names = both(packed_ref, CELLS)
    links_out[...] = names.astype(jnp.int32)
    slot = jnp.broadcast_to(names[:, FACES : FACES + 1], (RANGE, LANES)).astype(jnp.int32)
    placed = jnp.sum(jnp.where(slot == lane, row, 0).astype(jnp.float32), axis=0, keepdims=True)
    chosen = jnp.sum(jnp.where(lane == row, placed, 0.0), axis=1, keepdims=True)
    rows = jnp.broadcast_to(chosen, (RANGE, LANES)).astype(jnp.int32)
    rows_out[...] = rows
    reorder(packed_ref, 0, rows, p_out)
    store_faces(faces_out, pack_faces(load(p_out)))


def reorder_rest_kernel(rest_ref, rows_ref, f_out, c_out):
    rows = rows_ref[...]
    reorder(rest_ref, 0, rows, f_out)
    reorder(rest_ref, CELLS, rows, c_out)


def choose_kernel(pair_ref, out_ref):
    core = lax.axis_index("d") % 2
    out_ref[...] = jnp.where(core == 0, pair_ref[1], pair_ref[0])


def window(met_ref, faces_ref):
    before = lambda f, h: load_face(met_ref, f, h, 1)
    own = lambda f, h: load_face(faces_ref, f, h)
    after = lambda f, h: load_face(met_ref, f, h, 0)
    return before, own, after


def sweep_kernel(u_ref, f_ref, c_ref, links_ref, faces_ref, met_ref, u_out, faces_out):
    ghosts, _ = ghost_faces(links_ref[...], range_base(), *window(met_ref, faces_ref))
    tiles = sweep(load(u_ref), ghosts, f_ref, c_ref)
    store(u_out, tiles)
    store_faces(faces_out, pack_faces(tiles))


def lane_sum(tile):
    return jnp.sum(tile, axis=1, keepdims=True)


def face_sums(face):
    return [lane_sum(face(FLIPPED[d], 0) + face(FLIPPED[d], 1)) * (1.0 / CELLS) for d in range(FACES)]


def coarse_kernel(u_ref, f_ref, c_ref, links_ref, faces_ref, coarse_out):
    links = links_ref[...]
    defect = jnp.zeros((RANGE, LANES), jnp.float32)
    weights = jnp.zeros((RANGE, LANES), jnp.float32)
    for t in range(CELLS // LANES):
        c = c_ref[t]
        defect = defect + (f_ref[t] - c * u_ref[t])
        weights = weights + c
    sums = face_sums(lambda f, h: load_face(faces_ref, f, h))
    inner = lane_sum(defect) * (1.0 / CELLS)
    for s in sums:
        inner = inner - s
    diag = 6.0 + lane_sum(weights) * (1.0 / CELLS)
    lane = lanes()
    tile = jnp.zeros((RANGE, LANES), jnp.float32)
    for d in range(FACES):
        tile = jnp.where(lane == d, sums[d], tile)
        tile = jnp.where(lane == RANGE + d, links[:, d : d + 1].astype(jnp.float32), tile)
    tile = jnp.where(lane == FACES, inner, tile)
    tile = jnp.where(lane == FACES + 1, diag, tile)
    coarse_out[...] = tile


def row_kernel(row_ref, met_ref, out_ref):
    core, curve = lax.axis_index("d") % 2, lax.axis_index("d") // 2
    met = jnp.where(core == 0, curve + 1, curve + SLOTS - 1) % SLOTS
    lane = lanes()
    edge = jnp.zeros((RANGE, LANES), jnp.float32)
    for d, column in enumerate(face_sums(lambda f, h: load_face(met_ref, f, h))):
        edge = jnp.where(lane == d, column, edge)
    tiles = []
    for slot in range(SLOTS):
        place = slot % ROW
        own = slot // ROW == curve // ROW % (SLOTS // ROW)
        other = jnp.where(slot == met, edge, 0.0)
        tiles.append(jnp.where(own, row_ref[place // 2, place % 2], other))
    values = jnp.concatenate(tiles, axis=0).T
    out_ref[:, :LANES] = values[:RANGE]
    out_ref[:, LANES:] = values[RANGE : 2 * RANGE]


def join_kernel(met_ref, far_ref, out_ref):
    width = FACES * 2 * LANES
    core = lax.axis_index("d") % 2
    out_ref[:, :width] = met_ref[...]
    out_ref[:, width:] = jnp.where(core == 0, far_ref[0], far_ref[1])


def final_kernel(u_ref, f_ref, c_ref, links_ref, faces_ref, row_ref, met_ref, out_ref):
    core, curve = lax.axis_index("d") % 2, lax.axis_index("d") // 2
    row = sublanes()
    part = (lanes() // (ROW * RANGE) + SLOTS // ROW - curve // ROW % (SLOTS // ROW)) % (SLOTS // ROW)
    first = jnp.logical_or(part == 3, jnp.logical_and(part == 2, curve % ROW == 0))
    sums, names = [
        jnp.where(
            part == 0,
            row_ref[:, h * LANES : (h + 1) * LANES],
            jnp.where(first, load_face(met_ref, FACES, h, 0), load_face(met_ref, FACES, h, 1)),
        )
        for h in range(2)
    ]
    valid = jnp.logical_and(names >= 0.0, row < FACES)
    at = names.astype(jnp.int32) & (LANES - 1)

    def named(tile):
        return jnp.where(valid, jnp.take_along_axis(tile, at, axis=1), 0.0)

    def total(tile):
        return jnp.broadcast_to(jnp.sum(tile, axis=0, keepdims=True), (RANGE, LANES))

    inner = jnp.broadcast_to(sums[FACES : FACES + 1], (RANGE, LANES))
    diag = jnp.broadcast_to(sums[FACES + 1 : FACES + 2], (RANGE, LANES))
    diag = jnp.where(diag > 0.0, diag, 1.0)
    residual = inner + total(named(sums))
    error = jnp.zeros((RANGE, LANES), jnp.float32)
    for step in range(COARSE_SWEEPS):
        near = total(named(error)) if step else 0.0
        error = error + RELAXATION * (residual - diag * error + near) / diag
    near = named(error)
    own = lanes() == curve % SLOTS * RANGE + row
    lift = lane_sum(jnp.where(own, error, 0.0))
    ghosts, _ = ghost_faces(links_ref[...], range_base(), *window(met_ref, faces_ref))
    for d in range(FACES):
        raised = lane_sum(jnp.where(own, jnp.broadcast_to(near[d : d + 1], (RANGE, LANES)), 0.0))
        ghosts[d] = [half + raised for half in ghosts[d]]
    tiles = [[tile + lift for tile in pair] for pair in load(u_ref)]
    tiles = sweep(tiles, ghosts, f_ref, c_ref)
    for x in range(SIDE):
        for h in range(2):
            tile = tiles[x][h]
            half = jnp.where(core == 0, tile[0 : RANGE // 2], tile[RANGE // 2 :])
            t = 2 * x + h
            out_ref[:, t * LANES : (t + 1) * LANES] = half


def call(kernel, out_shape, name, *args, specs=None, scratch=()):
    many = isinstance(out_shape, (list, tuple))
    return pl.pallas_call(
        kernel,
        out_shape=out_shape,
        in_specs=specs or [VMEM] * len(args),
        out_specs=[VMEM] * len(out_shape) if many else VMEM,
        scratch_shapes=scratch,
        compiler_params=pltpu.CompilerParams(vmem_limit_bytes=GRANT),
        name=name,
    )(*args)


def on_device(groups, pressure, source_term, coefficient, new_slot, face_links):
    cores, pairs, along, across, exchange, far = groups
    gather = lambda array, members: lax.all_gather(array, "d", axis=0, axis_index_groups=members)
    meet = lambda array: lax.ppermute(array, "d", exchange)
    field = f32(CELLS // LANES, RANGE, LANES)
    packed = f32(RANGE, FACES * 2 * LANES)
    index = jax.ShapeDtypeStruct((RANGE, LANES), jnp.int32)
    whole, rest = call(
        pack_kernel,
        [f32(RANGE // 2, PACKED), f32(RANGE // 2, 2 * CELLS)],
        "pack",
        *[
            pltpu.with_memory_space_constraint(array, pltpu.HBM)
            for array in (pressure, source_term, coefficient, new_slot, face_links)
        ],
        specs=[HBM] * 5,
        scratch=[
            pltpu.SMEM((RANGE // 2,), jnp.int32),
            pltpu.VMEM((RANGE // 2, FACES), jnp.int32),
            pltpu.SemaphoreType.DMA((5,)),
        ],
    )
    u, links, rows, faces = call(
        reorder_kernel, [field, index, index, packed], "reorder", gather(whole, cores)
    )
    met = meet(faces)
    rest, _ = lax.optimization_barrier((rest, faces))
    f, c = call(reorder_rest_kernel, [field, field], "rest", gather(rest, cores), rows)
    u, faces = call(sweep_kernel, [field, packed], "sweep", u, f, c, links, faces, gather(met, cores))
    met = call(choose_kernel, packed, "choose", gather(faces, pairs))
    u, faces = call(sweep_kernel, [field, packed], "smooth", u, f, c, links, faces, gather(met, cores))
    met = meet(faces)
    coarse = call(coarse_kernel, f32(RANGE, LANES), "coarse", u, f, c, links, faces)
    coarse = gather(gather(coarse, along), across)
    row = call(row_kernel, f32(RANGE, 2 * LANES), "row", coarse, met)
    joined = call(join_kernel, f32(RANGE, (FACES + 1) * 2 * LANES), "join", met, gather(row, far))
    return call(
        final_kernel, f32(RANGE // 2, CELLS), "final", u, f, c, links, faces, row, gather(joined, cores)
    )


def solution(mesh):
    devices = mesh.devices.reshape(-1)
    count = devices.size // 2
    cores = [[2 * i, 2 * i + 1] for i in range(count)]
    firsts = [2 * i + core for i in range(0, count, ROW) for core in range(2)]
    along = [[i + k, i + k + 2] for i in firsts for k in (0, 4)]
    across = [[i + k, i + 6 - k] for i in firsts for k in (0, 2)]
    far = [[2 * i + 1, 2 * (i + ROW)] for i in range(count - ROW)]
    for i in range(0, ROW, 2):
        far += [[2 * i, 2 * i + 2], [2 * (count - 1 - i) - 1, 2 * (count - 1 - i) + 1]]
    pairs = [[2 * i, 2 * i + 3] for i in range(count - 1)] + [[2 * count - 2, 1]]
    exchange = [pair for i in range(count - 1) for pair in ((2 * i, 2 * i + 3), (2 * i + 3, 2 * i))]
    split, line = P("d", None), P("d")
    return jax.shard_map(
        functools.partial(on_device, (cores, pairs, along, across, exchange, far)),
        mesh=Mesh(devices, ("d",)),
        in_specs=(split, split, split, line, split),
        out_specs=split,
        check_vma=False,
    )
```

```python
import functools

import jax
import jax.numpy as jnp
from jax import lax
from jax.experimental import pallas as pl
from jax.experimental.pallas import tpu as pltpu
from jax.sharding import Mesh, PartitionSpec as P

PRE_SWEEPS = 2
COARSE_SWEEPS = 4
RELAXATION = 0.8

SIDE = 16
RANGE = 8
LANES = 128
CELLS = 4096
FACES = 6
FLIPPED = (1, 0, 3, 2, 5, 4)
ROW = 4
SLOTS = 16
PARTS = 4
PACKED = CELLS + LANES

VMEM = pl.BlockSpec(memory_space=pltpu.VMEM)
HBM = pl.BlockSpec(memory_space=pltpu.HBM)
GRANT = 4 * 1024 * 1024


def f32(*shape):
    return jax.ShapeDtypeStruct(shape, jnp.float32)


def lanes():
    return lax.broadcasted_iota(jnp.int32, (RANGE, LANES), 1)


def sublanes():
    return lax.broadcasted_iota(jnp.int32, (RANGE, LANES), 0)


def roll(tile, amount):
    amount = amount % LANES
    return tile if amount == 0 else pltpu.roll(tile, amount, 1)


def load(ref):
    return [[ref[2 * x + h] for h in range(2)] for x in range(SIDE)]


def store(ref, tiles):
    for x in range(SIDE):
        for h in range(2):
            ref[2 * x + h] = tiles[x][h]


def pack_faces(tiles):
    lane = lanes()
    zero = jnp.zeros((RANGE, LANES), jnp.float32)
    y_low, y_high, z_low, z_high = [[zero, zero] for _ in range(4)]
    for x in range(SIDE):
        part, place = x // 8, x % 8
        here = lane // SIDE == place
        y_low[part] = jnp.where(here, roll(tiles[x][0], SIDE * place), y_low[part])
        y_high[part] = jnp.where(here, roll(tiles[x][1], SIDE * place + SIDE), y_high[part])
        column = lane % SIDE == x
        for h in range(2):
            z_low[h] = jnp.where(column, roll(tiles[x][h], x), z_low[h])
            z_high[h] = jnp.where(column, roll(tiles[x][h], x - (SIDE - 1)), z_high[h])
    return [tiles[0], tiles[SIDE - 1], y_low, y_high, z_low, z_high]


def store_faces(ref, faces):
    for f in range(FACES):
        for h in range(2):
            ref[:, (2 * f + h) * LANES : (2 * f + h + 1) * LANES] = faces[f][h]


def load_face(ref, f, h, *lead):
    return ref[(*lead, slice(None), slice((2 * f + h) * LANES, (2 * f + h + 1) * LANES))]


def pick_rows(tile, rows):
    return jnp.take_along_axis(tile, rows, axis=0)


def ghost_faces(links, base, before, own, after):
    ghosts, valid = [], []
    for d in range(FACES):
        link = jnp.broadcast_to(links[:, d : d + 1], (RANGE, LANES))
        local = link - base
        rows = link & (RANGE - 1)
        face = FLIPPED[d]
        halves = []
        for h in range(2):
            low = pick_rows(before(face, h), rows)
            mid = pick_rows(own(face, h), rows)
            high = pick_rows(after(face, h), rows)
            picked = jnp.where(local < 0, low, jnp.where(local >= RANGE, high, mid))
            halves.append(jnp.where(link >= 0, picked, 0.0))
        ghosts.append(halves)
        valid.append(link >= 0)
    return ghosts, valid


def beside(tiles, ghosts, x, h):
    lane = lanes()
    here = tiles[x][h]
    minus = tiles[x - 1][h] if x > 0 else ghosts[0][h]
    plus = tiles[x + 1][h] if x < SIDE - 1 else ghosts[1][h]
    total = minus + plus
    part, place = x // 8, x % 8
    if h == 0:
        outer_minus = roll(ghosts[2][part], -SIDE * place)
        outer_plus = roll(tiles[x][1], -SIDE)
    else:
        outer_minus = roll(tiles[x][0], SIDE)
        outer_plus = roll(ghosts[3][part], LANES - SIDE - SIDE * place)
    total = total + jnp.where(lane < SIDE, outer_minus, roll(here, SIDE))
    total = total + jnp.where(lane >= LANES - SIDE, outer_plus, roll(here, -SIDE))
    z = lane % SIDE
    total = total + jnp.where(z == 0, roll(ghosts[4][h], -x), roll(here, 1))
    total = total + jnp.where(z == SIDE - 1, roll(ghosts[5][h], SIDE - 1 - x), roll(here, -1))
    return total


def relax(tiles, ghosts, source_ref, coefficient_ref, x, h):
    weight = RELAXATION / (6.0 + coefficient_ref[2 * x + h])
    gathered = source_ref[2 * x + h] + beside(tiles, ghosts, x, h)
    return (1.0 - RELAXATION) * tiles[x][h] + weight * gathered


def sweep(tiles, ghosts, source_ref, coefficient_ref):
    return [[relax(tiles, ghosts, source_ref, coefficient_ref, x, h) for h in range(2)] for x in range(SIDE)]


def range_base():
    return lax.axis_index("d") // 2 * RANGE


def pack_kernel(p_ref, f_ref, c_ref, slot_ref, links_ref, p_out, rest_out, slots, links, sems):
    targets = (p_out.at[:, :CELLS], rest_out.at[:, :CELLS], rest_out.at[:, CELLS:], slots, links)
    copies = [
        pltpu.make_async_copy(ref, target, sems.at[i])
        for i, (ref, target) in enumerate(zip((p_ref, f_ref, c_ref, slot_ref, links_ref), targets))
    ]
    for copy in copies[3:] + copies[:3]:
        copy.start()
    for copy in copies[3:]:
        copy.wait()
    lane = lanes()[: RANGE // 2]
    row = sublanes()[: RANGE // 2]
    tile = jnp.zeros((RANGE // 2, LANES), jnp.int32)
    for d in range(FACES):
        tile = jnp.where(lane == d, links[:, d : d + 1], tile)
    for i in range(RANGE // 2):
        tile = jnp.where(jnp.logical_and(lane == FACES, row == i), slots[i], tile)
    p_out[:, CELLS:] = tile.astype(jnp.float32)
    for copy in copies[:3]:
        copy.wait()


def both(ref, start):
    span = slice(start, start + LANES)
    return jnp.concatenate([ref[0, :, span], ref[1, :, span]], axis=0)


def reorder(ref, start, rows, target):
    for t in range(CELLS // LANES):
        target[t] = pick_rows(both(ref, start + t * LANES), rows)


def reorder_kernel(packed_ref, p_out, links_out, rows_out, faces_out):
    lane, row = lanes(), sublanes()
    names = both(packed_ref, CELLS)
    links_out[...] = names.astype(jnp.int32)
    slot = jnp.broadcast_to(names[:, FACES : FACES + 1], (RANGE, LANES)).astype(jnp.int32)
    placed = jnp.sum(jnp.where(slot == lane, row, 0).astype(jnp.float32), axis=0, keepdims=True)
    chosen = jnp.sum(jnp.where(lane == row, placed, 0.0), axis=1, keepdims=True)
    rows = jnp.broadcast_to(chosen, (RANGE, LANES)).astype(jnp.int32)
    rows_out[...] = rows
    reorder(packed_ref, 0, rows, p_out)
    store_faces(faces_out, pack_faces(load(p_out)))


def reorder_rest_kernel(rest_ref, rows_ref, f_out, c_out):
    rows = rows_ref[...]
    reorder(rest_ref, 0, rows, f_out)
    reorder(rest_ref, CELLS, rows, c_out)


def window(met_ref, faces_ref):
    before = lambda f, h: load_face(met_ref, f, h, 1)
    own = lambda f, h: load_face(faces_ref, f, h)
    after = lambda f, h: load_face(met_ref, f, h, 0)
    return before, own, after


def sweep_kernel(u_ref, f_ref, c_ref, links_ref, faces_ref, met_ref, u_out, faces_out):
    ghosts, _ = ghost_faces(links_ref[...], range_base(), *window(met_ref, faces_ref))
    tiles = sweep(load(u_ref), ghosts, f_ref, c_ref)
    store(u_out, tiles)
    store_faces(faces_out, pack_faces(tiles))


def lane_sum(tile):
    return jnp.sum(tile, axis=1, keepdims=True)


def face_sums(face):
    return [lane_sum(face(FLIPPED[d], 0) + face(FLIPPED[d], 1)) * (1.0 / CELLS) for d in range(FACES)]


def coarse_kernel(u_ref, f_ref, c_ref, links_ref, faces_ref, coarse_out):
    links = links_ref[...]
    defect = jnp.zeros((RANGE, LANES), jnp.float32)
    weights = jnp.zeros((RANGE, LANES), jnp.float32)
    for t in range(CELLS // LANES):
        c = c_ref[t]
        defect = defect + (f_ref[t] - c * u_ref[t])
        weights = weights + c
    sums = face_sums(lambda f, h: load_face(faces_ref, f, h))
    inner = lane_sum(defect) * (1.0 / CELLS)
    for s in sums:
        inner = inner - s
    diag = 6.0 + lane_sum(weights) * (1.0 / CELLS)
    lane = lanes()
    tile = jnp.zeros((RANGE, LANES), jnp.float32)
    for d in range(FACES):
        tile = jnp.where(lane == d, sums[d], tile)
        tile = jnp.where(lane == RANGE + d, links[:, d : d + 1].astype(jnp.float32), tile)
    tile = jnp.where(lane == FACES, inner, tile)
    tile = jnp.where(lane == FACES + 1, diag, tile)
    coarse_out[...] = tile


def row_kernel(row_ref, met_ref, out_ref):
    core, curve = lax.axis_index("d") % 2, lax.axis_index("d") // 2
    met = jnp.where(core == 0, curve + 1, curve + SLOTS - 1) % SLOTS
    lane = lanes()
    edge = jnp.zeros((RANGE, LANES), jnp.float32)
    for d, column in enumerate(face_sums(lambda f, h: load_face(met_ref, f, h))):
        edge = jnp.where(lane == d, column, edge)
    tiles = []
    for slot in range(SLOTS):
        place = slot % ROW
        own = slot // ROW == curve // ROW % (SLOTS // ROW)
        other = jnp.where(slot == met, edge, 0.0)
        tiles.append(jnp.where(own, row_ref[place // 2, place % 2], other))
    values = jnp.concatenate(tiles, axis=0).T
    out_ref[:, :LANES] = values[:RANGE]
    out_ref[:, LANES:] = values[RANGE : 2 * RANGE]


def join_kernel(met_ref, far_ref, out_ref):
    width = FACES * 2 * LANES
    core = lax.axis_index("d") % 2
    out_ref[:, :width] = met_ref[...]
    out_ref[:, width:] = jnp.where(core == 0, far_ref[0], far_ref[1])


def final_kernel(u_ref, f_ref, c_ref, links_ref, faces_ref, row_ref, met_ref, out_ref, held, sems):
    core, curve = lax.axis_index("d") % 2, lax.axis_index("d") // 2
    row = sublanes()
    part = (lanes() // (ROW * RANGE) + SLOTS // ROW - curve // ROW % (SLOTS // ROW)) % (SLOTS // ROW)
    first = jnp.logical_or(part == 3, jnp.logical_and(part == 2, curve % ROW == 0))
    sums, names = [
        jnp.where(
            part == 0,
            row_ref[:, h * LANES : (h + 1) * LANES],
            jnp.where(first, load_face(met_ref, FACES, h, 0), load_face(met_ref, FACES, h, 1)),
        )
        for h in range(2)
    ]
    valid = jnp.logical_and(names >= 0.0, row < FACES)
    at = names.astype(jnp.int32) & (LANES - 1)

    def named(tile):
        return jnp.where(valid, jnp.take_along_axis(tile, at, axis=1), 0.0)

    def total(tile):
        return jnp.broadcast_to(jnp.sum(tile, axis=0, keepdims=True), (RANGE, LANES))

    inner = jnp.broadcast_to(sums[FACES : FACES + 1], (RANGE, LANES))
    diag = jnp.broadcast_to(sums[FACES + 1 : FACES + 2], (RANGE, LANES))
    diag = jnp.where(diag > 0.0, diag, 1.0)
    residual = inner + total(named(sums))
    error = jnp.zeros((RANGE, LANES), jnp.float32)
    for step in range(COARSE_SWEEPS):
        near = total(named(error)) if step else 0.0
        error = error + RELAXATION * (residual - diag * error + near) / diag
    near = named(error)
    own = lanes() == curve % SLOTS * RANGE + row
    lift = lane_sum(jnp.where(own, error, 0.0))
    ghosts, _ = ghost_faces(links_ref[...], range_base(), *window(met_ref, faces_ref))
    for d in range(FACES):
        raised = lane_sum(jnp.where(own, jnp.broadcast_to(near[d : d + 1], (RANGE, LANES)), 0.0))
        ghosts[d] = [half + raised for half in ghosts[d]]
    tiles = [[tile + lift for tile in pair] for pair in load(u_ref)]
    copies = []
    for x in range(SIDE):
        for h in range(2):
            t = 2 * x + h
            tile = relax(tiles, ghosts, f_ref, c_ref, x, h)
            half = jnp.where(core == 0, tile[0 : RANGE // 2], tile[RANGE // 2 :])
            held[:, t * LANES : (t + 1) * LANES] = half
        if x % (SIDE // PARTS) == SIDE // PARTS - 1:
            part = len(copies)
            span = slice(part * CELLS // PARTS, (part + 1) * CELLS // PARTS)
            copies.append(pltpu.make_async_copy(held.at[:, span], out_ref.at[:, span], sems.at[part]))
            copies[-1].start()
    for copy in copies:
        copy.wait()


def call(kernel, out_shape, name, *args, specs=None, out=VMEM, scratch=()):
    many = isinstance(out_shape, (list, tuple))
    return pl.pallas_call(
        kernel,
        out_shape=out_shape,
        in_specs=specs or [VMEM] * len(args),
        out_specs=[out] * len(out_shape) if many else out,
        scratch_shapes=scratch,
        compiler_params=pltpu.CompilerParams(vmem_limit_bytes=GRANT),
        name=name,
    )(*args)


def on_device(groups, pressure, source_term, coefficient, new_slot, face_links):
    cores, along, across, exchange, far = groups
    gather = lambda array, members: lax.all_gather(array, "d", axis=0, axis_index_groups=members)
    meet = lambda array: lax.ppermute(array, "d", exchange)
    field = f32(CELLS // LANES, RANGE, LANES)
    packed = f32(RANGE, FACES * 2 * LANES)
    index = jax.ShapeDtypeStruct((RANGE, LANES), jnp.int32)
    whole, rest = call(
        pack_kernel,
        [f32(RANGE // 2, PACKED), f32(RANGE // 2, 2 * CELLS)],
        "pack",
        *[
            pltpu.with_memory_space_constraint(array, pltpu.HBM)
            for array in (pressure, source_term, coefficient, new_slot, face_links)
        ],
        specs=[HBM] * 5,
        scratch=[
            pltpu.SMEM((RANGE // 2,), jnp.int32),
            pltpu.VMEM((RANGE // 2, FACES), jnp.int32),
            pltpu.SemaphoreType.DMA((5,)),
        ],
    )
    u, links, rows, faces = call(
        reorder_kernel, [field, index, index, packed], "reorder", gather(whole, cores)
    )
    met = meet(faces)
    rest, _ = lax.optimization_barrier((rest, faces))
    f, c = call(reorder_rest_kernel, [field, field], "rest", gather(rest, cores), rows)
    u, faces = call(sweep_kernel, [field, packed], "sweep", u, f, c, links, faces, gather(met, cores))
    u, faces = call(sweep_kernel, [field, packed], "smooth", u, f, c, links, faces, gather(meet(faces), cores))
    met = meet(faces)
    coarse = call(coarse_kernel, f32(RANGE, LANES), "coarse", u, f, c, links, faces)
    coarse = gather(gather(coarse, along), across)
    row = call(row_kernel, f32(RANGE, 2 * LANES), "row", coarse, met)
    joined = call(join_kernel, f32(RANGE, (FACES + 1) * 2 * LANES), "join", met, gather(row, far))
    return call(
        final_kernel,
        f32(RANGE // 2, CELLS),
        "final",
        u,
        f,
        c,
        links,
        faces,
        row,
        gather(joined, cores),
        out=HBM,
        scratch=[pltpu.VMEM((RANGE // 2, CELLS), jnp.float32), pltpu.SemaphoreType.DMA((PARTS,))],
    )


def solution(mesh):
    devices = mesh.devices.reshape(-1)
    count = devices.size // 2
    cores = [[2 * i, 2 * i + 1] for i in range(count)]
    firsts = [2 * i + core for i in range(0, count, ROW) for core in range(2)]
    along = [[i + k, i + k + 2] for i in firsts for k in (0, 4)]
    across = [[i + k, i + 6 - k] for i in firsts for k in (0, 2)]
    far = [[2 * i + 1, 2 * (i + ROW)] for i in range(count - ROW)]
    for i in range(0, ROW, 2):
        far += [[2 * i, 2 * i + 2], [2 * (count - 1 - i) - 1, 2 * (count - 1 - i) + 1]]
    exchange = [pair for i in range(count - 1) for pair in ((2 * i, 2 * i + 3), (2 * i + 3, 2 * i))]
    split, line = P("d", None), P("d")
    return jax.shard_map(
        functools.partial(on_device, (cores, along, across, exchange, far)),
        mesh=Mesh(devices, ("d",)),
        in_specs=(split, split, split, line, split),
        out_specs=split,
        check_vma=False,
    )
```

```python
import functools

import jax
import jax.numpy as jnp
from jax import lax
from jax.experimental import pallas as pl
from jax.experimental.pallas import tpu as pltpu
from jax.sharding import Mesh, PartitionSpec as P

PRE_SWEEPS = 2
COARSE_SWEEPS = 4
RELAXATION = 0.8

SIDE = 16
RANGE = 8
LANES = 128
CELLS = 4096
FACES = 6
FLIPPED = (1, 0, 3, 2, 5, 4)
ROW = 4
BROKEN = 2
SLOTS = 16
PACKED = CELLS + LANES

VMEM = pl.BlockSpec(memory_space=pltpu.VMEM)
HBM = pl.BlockSpec(memory_space=pltpu.HBM)
GRANT = 4 * 1024 * 1024


def f32(*shape):
    return jax.ShapeDtypeStruct(shape, jnp.float32)


def lanes():
    return lax.broadcasted_iota(jnp.int32, (RANGE, LANES), 1)


def sublanes():
    return lax.broadcasted_iota(jnp.int32, (RANGE, LANES), 0)


def roll(tile, amount):
    amount = amount % LANES
    return tile if amount == 0 else pltpu.roll(tile, amount, 1)


def load(ref):
    return [[ref[2 * x + h] for h in range(2)] for x in range(SIDE)]


def store(ref, tiles):
    for x in range(SIDE):
        for h in range(2):
            ref[2 * x + h] = tiles[x][h]


def pack_faces(tiles):
    lane = lanes()
    zero = jnp.zeros((RANGE, LANES), jnp.float32)
    y_low, y_high, z_low, z_high = [[zero, zero] for _ in range(4)]
    for x in range(SIDE):
        part, place = x // 8, x % 8
        here = lane // SIDE == place
        y_low[part] = jnp.where(here, roll(tiles[x][0], SIDE * place), y_low[part])
        y_high[part] = jnp.where(here, roll(tiles[x][1], SIDE * place + SIDE), y_high[part])
        column = lane % SIDE == x
        for h in range(2):
            z_low[h] = jnp.where(column, roll(tiles[x][h], x), z_low[h])
            z_high[h] = jnp.where(column, roll(tiles[x][h], x - (SIDE - 1)), z_high[h])
    return [tiles[0], tiles[SIDE - 1], y_low, y_high, z_low, z_high]


def store_faces(ref, faces):
    for f in range(FACES):
        for h in range(2):
            ref[:, (2 * f + h) * LANES : (2 * f + h + 1) * LANES] = faces[f][h]


def load_face(ref, f, h, *lead):
    return ref[(*lead, slice(None), slice((2 * f + h) * LANES, (2 * f + h + 1) * LANES))]


def pick_rows(tile, rows):
    return jnp.take_along_axis(tile, rows, axis=0)


def ghost_faces(links, base, before, own, after):
    ghosts, valid = [], []
    for d in range(FACES):
        link = jnp.broadcast_to(links[:, d : d + 1], (RANGE, LANES))
        local = link - base
        rows = link & (RANGE - 1)
        face = FLIPPED[d]
        halves = []
        for h in range(2):
            low = pick_rows(before(face, h), rows)
            mid = pick_rows(own(face, h), rows)
            high = pick_rows(after(face, h), rows)
            picked = jnp.where(local < 0, low, jnp.where(local >= RANGE, high, mid))
            halves.append(jnp.where(link >= 0, picked, 0.0))
        ghosts.append(halves)
        valid.append(link >= 0)
    return ghosts, valid


def beside(tiles, ghosts, x, h):
    lane = lanes()
    here = tiles[x][h]
    minus = tiles[x - 1][h] if x > 0 else ghosts[0][h]
    plus = tiles[x + 1][h] if x < SIDE - 1 else ghosts[1][h]
    total = minus + plus
    part, place = x // 8, x % 8
    if h == 0:
        outer_minus = roll(ghosts[2][part], -SIDE * place)
        outer_plus = roll(tiles[x][1], -SIDE)
    else:
        outer_minus = roll(tiles[x][0], SIDE)
        outer_plus = roll(ghosts[3][part], LANES - SIDE - SIDE * place)
    total = total + jnp.where(lane < SIDE, outer_minus, roll(here, SIDE))
    total = total + jnp.where(lane >= LANES - SIDE, outer_plus, roll(here, -SIDE))
    z = lane % SIDE
    total = total + jnp.where(z == 0, roll(ghosts[4][h], -x), roll(here, 1))
    total = total + jnp.where(z == SIDE - 1, roll(ghosts[5][h], SIDE - 1 - x), roll(here, -1))
    return total


def relax(tiles, ghosts, source_ref, coefficient_ref, x, h):
    weight = RELAXATION / (6.0 + coefficient_ref[2 * x + h])
    gathered = source_ref[2 * x + h] + beside(tiles, ghosts, x, h)
    return (1.0 - RELAXATION) * tiles[x][h] + weight * gathered


def sweep(tiles, ghosts, source_ref, coefficient_ref):
    return [[relax(tiles, ghosts, source_ref, coefficient_ref, x, h) for h in range(2)] for x in range(SIDE)]


def range_base():
    return lax.axis_index("d") // 2 * RANGE


def pack_kernel(p_ref, f_ref, c_ref, slot_ref, links_ref, p_out, rest_out, slots, links, sems):
    targets = (p_out.at[:, :CELLS], rest_out.at[:, :CELLS], rest_out.at[:, CELLS:], slots, links)
    copies = [
        pltpu.make_async_copy(ref, target, sems.at[i])
        for i, (ref, target) in enumerate(zip((p_ref, f_ref, c_ref, slot_ref, links_ref), targets))
    ]
    for copy in copies[3:] + copies[:3]:
        copy.start()
    for copy in copies[3:]:
        copy.wait()
    lane = lanes()[: RANGE // 2]
    row = sublanes()[: RANGE // 2]
    tile = jnp.zeros((RANGE // 2, LANES), jnp.int32)
    for d in range(FACES):
        tile = jnp.where(lane == d, links[:, d : d + 1], tile)
    for i in range(RANGE // 2):
        tile = jnp.where(jnp.logical_and(lane == FACES, row == i), slots[i], tile)
    p_out[:, CELLS:] = tile.astype(jnp.float32)
    for copy in copies[:3]:
        copy.wait()


def both(ref, start):
    span = slice(start, start + LANES)
    return jnp.concatenate([ref[0, :, span], ref[1, :, span]], axis=0)


def reorder(ref, start, rows, target):
    for t in range(CELLS // LANES):
        target[t] = pick_rows(both(ref, start + t * LANES), rows)


def reorder_kernel(packed_ref, p_out, links_out, rows_out, faces_out):
    lane, row = lanes(), sublanes()
    names = both(packed_ref, CELLS)
    links_out[...] = names.astype(jnp.int32)
    slot = jnp.broadcast_to(names[:, FACES : FACES + 1], (RANGE, LANES)).astype(jnp.int32)
    placed = jnp.sum(jnp.where(slot == lane, row, 0).astype(jnp.float32), axis=0, keepdims=True)
    chosen = jnp.sum(jnp.where(lane == row, placed, 0.0), axis=1, keepdims=True)
    rows = jnp.broadcast_to(chosen, (RANGE, LANES)).astype(jnp.int32)
    rows_out[...] = rows
    reorder(packed_ref, 0, rows, p_out)
    store_faces(faces_out, pack_faces(load(p_out)))


def reorder_rest_kernel(rest_ref, rows_ref, f_out, c_out):
    rows = rows_ref[...]
    reorder(rest_ref, 0, rows, f_out)
    reorder(rest_ref, CELLS, rows, c_out)


def choose_kernel(pair_ref, single_ref, out_ref):
    me = lax.axis_index("d")
    single = jnp.logical_or(me == 2 * BROKEN, me == 2 * BROKEN + 3)
    out_ref[...] = jnp.where(single, single_ref[...], jnp.where(me % 2 == 0, pair_ref[1], pair_ref[0]))


def window(met_ref, faces_ref):
    before = lambda f, h: load_face(met_ref, f, h, 1)
    own = lambda f, h: load_face(faces_ref, f, h)
    after = lambda f, h: load_face(met_ref, f, h, 0)
    return before, own, after


def sweep_kernel(u_ref, f_ref, c_ref, links_ref, faces_ref, met_ref, u_out, faces_out):
    ghosts, _ = ghost_faces(links_ref[...], range_base(), *window(met_ref, faces_ref))
    tiles = sweep(load(u_ref), ghosts, f_ref, c_ref)
    store(u_out, tiles)
    store_faces(faces_out, pack_faces(tiles))


def lane_sum(tile):
    return jnp.sum(tile, axis=1, keepdims=True)


def face_sums(face):
    return [lane_sum(face(FLIPPED[d], 0) + face(FLIPPED[d], 1)) * (1.0 / CELLS) for d in range(FACES)]


def coarse_kernel(u_ref, f_ref, c_ref, links_ref, faces_ref, coarse_out):
    links = links_ref[...]
    defect = jnp.zeros((RANGE, LANES), jnp.float32)
    weights = jnp.zeros((RANGE, LANES), jnp.float32)
    for t in range(CELLS // LANES):
        c = c_ref[t]
        defect = defect + (f_ref[t] - c * u_ref[t])
        weights = weights + c
    sums = face_sums(lambda f, h: load_face(faces_ref, f, h))
    inner = lane_sum(defect) * (1.0 / CELLS)
    for s in sums:
        inner = inner - s
    diag = 6.0 + lane_sum(weights) * (1.0 / CELLS)
    lane = lanes()
    tile = jnp.zeros((RANGE, LANES), jnp.float32)
    for d in range(FACES):
        tile = jnp.where(lane == d, sums[d], tile)
        tile = jnp.where(lane == RANGE + d, links[:, d : d + 1].astype(jnp.float32), tile)
    tile = jnp.where(lane == FACES, inner, tile)
    tile = jnp.where(lane == FACES + 1, diag, tile)
    coarse_out[...] = tile


def row_kernel(row_ref, met_ref, out_ref):
    core, curve = lax.axis_index("d") % 2, lax.axis_index("d") // 2
    met = jnp.where(core == 0, curve + 1, curve + SLOTS - 1) % SLOTS
    lane = lanes()
    edge = jnp.zeros((RANGE, LANES), jnp.float32)
    for d, column in enumerate(face_sums(lambda f, h: load_face(met_ref, f, h))):
        edge = jnp.where(lane == d, column, edge)
    tiles = []
    for slot in range(SLOTS):
        place = slot % ROW
        own = slot // ROW == curve // ROW % (SLOTS // ROW)
        other = jnp.where(slot == met, edge, 0.0)
        tiles.append(jnp.where(own, row_ref[place // 2, place % 2], other))
    values = jnp.concatenate(tiles, axis=0).T
    out_ref[:, :LANES] = values[:RANGE]
    out_ref[:, LANES:] = values[RANGE : 2 * RANGE]


def join_kernel(met_ref, far_ref, out_ref):
    width = FACES * 2 * LANES
    core = lax.axis_index("d") % 2
    out_ref[:, :width] = met_ref[...]
    out_ref[:, width:] = jnp.where(core == 0, far_ref[0], far_ref[1])


def final_kernel(u_ref, f_ref, c_ref, links_ref, faces_ref, row_ref, met_ref, out_ref):
    core, curve = lax.axis_index("d") % 2, lax.axis_index("d") // 2
    row = sublanes()
    part = (lanes() // (ROW * RANGE) + SLOTS // ROW - curve // ROW % (SLOTS // ROW)) % (SLOTS // ROW)
    first = jnp.logical_or(part == 3, jnp.logical_and(part == 2, curve % ROW == 0))
    sums, names = [
        jnp.where(
            part == 0,
            row_ref[:, h * LANES : (h + 1) * LANES],
            jnp.where(first, load_face(met_ref, FACES, h, 0), load_face(met_ref, FACES, h, 1)),
        )
        for h in range(2)
    ]
    valid = jnp.logical_and(names >= 0.0, row < FACES)
    at = names.astype(jnp.int32) & (LANES - 1)

    def named(tile):
        return jnp.where(valid, jnp.take_along_axis(tile, at, axis=1), 0.0)

    def total(tile):
        return jnp.broadcast_to(jnp.sum(tile, axis=0, keepdims=True), (RANGE, LANES))

    inner = jnp.broadcast_to(sums[FACES : FACES + 1], (RANGE, LANES))
    diag = jnp.broadcast_to(sums[FACES + 1 : FACES + 2], (RANGE, LANES))
    diag = jnp.where(diag > 0.0, diag, 1.0)
    residual = inner + total(named(sums))
    weight = RELAXATION / diag
    error = weight * residual
    for step in range(COARSE_SWEEPS - 1):
        error = (1.0 - RELAXATION) * error + weight * (residual + total(named(error)))
    near = named(error)
    own = lanes() == curve % SLOTS * RANGE + row
    lift = lane_sum(jnp.where(own, error, 0.0))
    ghosts, _ = ghost_faces(links_ref[...], range_base(), *window(met_ref, faces_ref))
    raised = []
    for d in range(FACES):
        raised.append(lane_sum(jnp.where(own, jnp.broadcast_to(near[d : d + 1], (RANGE, LANES)), 0.0)))
    lane = lanes()
    z = lane % SIDE
    around = []
    for h in range(2):
        low_y = jnp.where(lane < SIDE, raised[2], lift) if h == 0 else lift
        high_y = jnp.where(lane >= LANES - SIDE, raised[3], lift) if h == 1 else lift
        around.append(low_y + high_y + jnp.where(z == 0, raised[4], lift) + jnp.where(z == SIDE - 1, raised[5], lift))
    tiles = load(u_ref)
    for x in range(SIDE):
        for h in range(2):
            t = 2 * x + h
            weight = RELAXATION / (6.0 + c_ref[t])
            near = around[h] + (lift if x else raised[0]) + (lift if x < SIDE - 1 else raised[1])
            tile = relax(tiles, ghosts, f_ref, c_ref, x, h) + ((1.0 - RELAXATION) * lift + weight * near)
            half = jnp.where(core == 0, tile[0 : RANGE // 2], tile[RANGE // 2 :])
            out_ref[:, t * LANES : (t + 1) * LANES] = half


def call(kernel, out_shape, name, *args, specs=None, scratch=()):
    many = isinstance(out_shape, (list, tuple))
    return pl.pallas_call(
        kernel,
        out_shape=out_shape,
        in_specs=specs or [VMEM] * len(args),
        out_specs=[VMEM] * len(out_shape) if many else VMEM,
        scratch_shapes=scratch,
        compiler_params=pltpu.CompilerParams(vmem_limit_bytes=GRANT),
        name=name,
    )(*args)


def on_device(groups, pressure, source_term, coefficient, new_slot, face_links):
    cores, pairs, single, along, across, exchange, far = groups
    gather = lambda array, members: lax.all_gather(array, "d", axis=0, axis_index_groups=members)
    meet = lambda array: lax.ppermute(array, "d", exchange)
    field = f32(CELLS // LANES, RANGE, LANES)
    packed = f32(RANGE, FACES * 2 * LANES)
    index = jax.ShapeDtypeStruct((RANGE, LANES), jnp.int32)
    whole, rest = call(
        pack_kernel,
        [f32(RANGE // 2, PACKED), f32(RANGE // 2, 2 * CELLS)],
        "pack",
        *[
            pltpu.with_memory_space_constraint(array, pltpu.HBM)
            for array in (pressure, source_term, coefficient, new_slot, face_links)
        ],
        specs=[HBM] * 5,
        scratch=[
            pltpu.SMEM((RANGE // 2,), jnp.int32),
            pltpu.VMEM((RANGE // 2, FACES), jnp.int32),
            pltpu.SemaphoreType.DMA((5,)),
        ],
    )
    u, links, rows, faces = call(
        reorder_kernel, [field, index, index, packed], "reorder", gather(whole, cores)
    )
    met = meet(faces)
    rest, _ = lax.optimization_barrier((rest, faces))
    f, c = call(reorder_rest_kernel, [field, field], "rest", gather(rest, cores), rows)
    u, faces = call(sweep_kernel, [field, packed], "sweep", u, f, c, links, faces, gather(met, cores))
    met = call(choose_kernel, packed, "choose", gather(faces, pairs), lax.ppermute(faces, "d", single))
    u, faces = call(sweep_kernel, [field, packed], "smooth", u, f, c, links, faces, gather(met, cores))
    met = meet(faces)
    coarse = call(coarse_kernel, f32(RANGE, LANES), "coarse", u, f, c, links, faces)
    coarse = gather(gather(coarse, along), across)
    row = call(row_kernel, f32(RANGE, 2 * LANES), "row", coarse, met)
    joined = call(join_kernel, f32(RANGE, (FACES + 1) * 2 * LANES), "join", met, gather(row, far))
    return call(
        final_kernel,
        f32(RANGE // 2, CELLS),
        "final",
        u,
        f,
        c,
        links,
        faces,
        row,
        gather(joined, cores),
    )


def solution(mesh):
    devices = mesh.devices.reshape(-1)
    count = devices.size // 2
    cores = [[2 * i, 2 * i + 1] for i in range(count)]
    firsts = [2 * i + core for i in range(0, count, ROW) for core in range(2)]
    along = [[i + k, i + k + 2] for i in firsts for k in (0, 4)]
    across = [[i + k, i + 6 - k] for i in firsts for k in (0, 2)]
    far = [[2 * i + 1, 2 * (i + ROW)] for i in range(count - ROW)]
    for i in range(0, ROW, 2):
        far += [[2 * i, 2 * i + 2], [2 * (count - 1 - i) - 1, 2 * (count - 1 - i) + 1]]
    pairs = [[2 * i, 2 * i + 3] for i in range(count - 1) if i != BROKEN]
    pairs += [[2 * BROKEN, 1], [2 * count - 2, 2 * BROKEN + 3]]
    single = [(2 * BROKEN, 2 * BROKEN + 3), (2 * BROKEN + 3, 2 * BROKEN)]
    exchange = [pair for i in range(count - 1) for pair in ((2 * i, 2 * i + 3), (2 * i + 3, 2 * i))]
    split, line = P("d", None), P("d")
    return jax.shard_map(
        functools.partial(on_device, (cores, pairs, single, along, across, exchange, far)),
        mesh=Mesh(devices, ("d",)),
        in_specs=(split, split, split, line, split),
        out_specs=split,
        check_vma=False,
    )
```

```python
import functools

import jax
import jax.numpy as jnp
from jax import lax
from jax.experimental import pallas as pl
from jax.experimental.pallas import tpu as pltpu
from jax.sharding import Mesh, PartitionSpec as P

PRE_SWEEPS = 2
COARSE_SWEEPS = 4
RELAXATION = 0.8

SIDE = 16
RANGE = 8
LANES = 128
CELLS = 4096
FACES = 6
FLIPPED = (1, 0, 3, 2, 5, 4)
ROW = 4
BROKEN = 2
SLOTS = 16
PACKED = CELLS + LANES

VMEM = pl.BlockSpec(memory_space=pltpu.VMEM)
HBM = pl.BlockSpec(memory_space=pltpu.HBM)
GRANT = 4 * 1024 * 1024


def f32(*shape):
    return jax.ShapeDtypeStruct(shape, jnp.float32)


def lanes():
    return lax.broadcasted_iota(jnp.int32, (RANGE, LANES), 1)


def sublanes():
    return lax.broadcasted_iota(jnp.int32, (RANGE, LANES), 0)


def roll(tile, amount):
    amount = amount % LANES
    return tile if amount == 0 else pltpu.roll(tile, amount, 1)


def load(ref):
    return [[ref[2 * x + h] for h in range(2)] for x in range(SIDE)]


def store(ref, tiles):
    for x in range(SIDE):
        for h in range(2):
            ref[2 * x + h] = tiles[x][h]


def pack_faces(tiles):
    lane = lanes()
    zero = jnp.zeros((RANGE, LANES), jnp.float32)
    y_low, y_high, z_low, z_high = [[zero, zero] for _ in range(4)]
    for x in range(SIDE):
        part, place = x // 8, x % 8
        here = lane // SIDE == place
        y_low[part] = jnp.where(here, roll(tiles[x][0], SIDE * place), y_low[part])
        y_high[part] = jnp.where(here, roll(tiles[x][1], SIDE * place + SIDE), y_high[part])
        for h in range(2):
            turned = roll(tiles[x][h], x)
            z_low[h] = jnp.where(lane % SIDE == x, turned, z_low[h])
            z_high[h] = jnp.where(lane % SIDE == (x + SIDE - 1) % SIDE, turned, z_high[h])
    return [tiles[0], tiles[SIDE - 1], y_low, y_high, z_low, z_high]


def store_faces(ref, faces):
    for f in range(FACES):
        for h in range(2):
            ref[:, (2 * f + h) * LANES : (2 * f + h + 1) * LANES] = faces[f][h]


def load_face(ref, f, h, *lead):
    return ref[(*lead, slice(None), slice((2 * f + h) * LANES, (2 * f + h + 1) * LANES))]


def pick_rows(tile, rows):
    return jnp.take_along_axis(tile, rows, axis=0)


def ghost_faces(links, base, before, own, after):
    ghosts, valid = [], []
    for d in range(FACES):
        link = jnp.broadcast_to(links[:, d : d + 1], (RANGE, LANES))
        local = link - base
        rows = link & (RANGE - 1)
        face = FLIPPED[d]
        halves = []
        for h in range(2):
            low = pick_rows(before(face, h), rows)
            mid = pick_rows(own(face, h), rows)
            high = pick_rows(after(face, h), rows)
            picked = jnp.where(local < 0, low, jnp.where(local >= RANGE, high, mid))
            halves.append(jnp.where(link >= 0, picked, 0.0))
        ghosts.append(halves)
        valid.append(link >= 0)
    return ghosts, valid


def beside(tiles, ghosts, x, h):
    lane = lanes()
    here = tiles[x][h]
    minus = tiles[x - 1][h] if x > 0 else ghosts[0][h]
    plus = tiles[x + 1][h] if x < SIDE - 1 else ghosts[1][h]
    total = minus + plus
    part, place = x // 8, x % 8
    if h == 0:
        outer_minus = roll(ghosts[2][part], -SIDE * place)
        outer_plus = roll(tiles[x][1], -SIDE)
    else:
        outer_minus = roll(tiles[x][0], SIDE)
        outer_plus = roll(ghosts[3][part], LANES - SIDE - SIDE * place)
    total = total + jnp.where(lane < SIDE, outer_minus, roll(here, SIDE))
    total = total + jnp.where(lane >= LANES - SIDE, outer_plus, roll(here, -SIDE))
    z = lane % SIDE
    total = total + jnp.where(z == 0, roll(ghosts[4][h], 1 - SIDE - x), roll(here, 1))
    total = total + jnp.where(z == SIDE - 1, roll(ghosts[5][h], SIDE - 1 - x), roll(here, -1))
    return total


def relax(tiles, ghosts, source_ref, weight_ref, x, h):
    weight = weight_ref[2 * x + h]
    gathered = source_ref[2 * x + h] + beside(tiles, ghosts, x, h)
    return (1.0 - RELAXATION) * tiles[x][h] + weight * gathered


def sweep(tiles, ghosts, source_ref, weight_ref):
    return [[relax(tiles, ghosts, source_ref, weight_ref, x, h) for h in range(2)] for x in range(SIDE)]


def range_base():
    return lax.axis_index("d") // 2 * RANGE


def pack_kernel(p_ref, f_ref, c_ref, slot_ref, links_ref, p_out, rest_out, slots, links, sems):
    targets = (p_out.at[:, :CELLS], rest_out.at[:, :CELLS], rest_out.at[:, CELLS:], slots, links)
    copies = [
        pltpu.make_async_copy(ref, target, sems.at[i])
        for i, (ref, target) in enumerate(zip((p_ref, f_ref, c_ref, slot_ref, links_ref), targets))
    ]
    for copy in copies[3:] + copies[:3]:
        copy.start()
    for copy in copies[3:]:
        copy.wait()
    lane = lanes()[: RANGE // 2]
    row = sublanes()[: RANGE // 2]
    tile = jnp.zeros((RANGE // 2, LANES), jnp.int32)
    for d in range(FACES):
        tile = jnp.where(lane == d, links[:, d : d + 1], tile)
    for i in range(RANGE // 2):
        tile = jnp.where(jnp.logical_and(lane == FACES, row == i), slots[i], tile)
    p_out[:, CELLS:] = tile.astype(jnp.float32)
    for copy in copies[:3]:
        copy.wait()


def both(ref, start):
    span = slice(start, start + LANES)
    return jnp.concatenate([ref[0, :, span], ref[1, :, span]], axis=0)


def reorder(ref, start, rows, target):
    for t in range(CELLS // LANES):
        target[t] = pick_rows(both(ref, start + t * LANES), rows)


def reorder_kernel(packed_ref, p_out, links_out, rows_out, faces_out):
    lane, row = lanes(), sublanes()
    names = both(packed_ref, CELLS)
    links_out[...] = names.astype(jnp.int32)
    slot = jnp.broadcast_to(names[:, FACES : FACES + 1], (RANGE, LANES)).astype(jnp.int32)
    placed = jnp.sum(jnp.where(slot == lane, row, 0).astype(jnp.float32), axis=0, keepdims=True)
    chosen = jnp.sum(jnp.where(lane == row, placed, 0.0), axis=1, keepdims=True)
    rows = jnp.broadcast_to(chosen, (RANGE, LANES)).astype(jnp.int32)
    rows_out[...] = rows
    reorder(packed_ref, 0, rows, p_out)
    store_faces(faces_out, pack_faces(load(p_out)))


def reorder_rest_kernel(rest_ref, rows_ref, f_out, c_out, weight_out):
    rows = rows_ref[...]
    reorder(rest_ref, 0, rows, f_out)
    reorder(rest_ref, CELLS, rows, c_out)
    for t in range(CELLS // LANES):
        weight_out[t] = RELAXATION / (6.0 + c_out[t])


def choose_kernel(pair_ref, single_ref, out_ref):
    me = lax.axis_index("d")
    single = jnp.logical_or(me == 2 * BROKEN, me == 2 * BROKEN + 3)
    out_ref[...] = jnp.where(single, single_ref[...], jnp.where(me % 2 == 0, pair_ref[1], pair_ref[0]))


def window(met_ref, faces_ref):
    before = lambda f, h: load_face(met_ref, f, h, 1)
    own = lambda f, h: load_face(faces_ref, f, h)
    after = lambda f, h: load_face(met_ref, f, h, 0)
    return before, own, after


def sweep_kernel(u_ref, f_ref, weight_ref, links_ref, faces_ref, met_ref, u_out, faces_out):
    ghosts, _ = ghost_faces(links_ref[...], range_base(), *window(met_ref, faces_ref))
    tiles = sweep(load(u_ref), ghosts, f_ref, weight_ref)
    store(u_out, tiles)
    store_faces(faces_out, pack_faces(tiles))


def lane_sum(tile):
    return jnp.sum(tile, axis=1, keepdims=True)


def face_sums(face):
    return [lane_sum(face(FLIPPED[d], 0) + face(FLIPPED[d], 1)) * (1.0 / CELLS) for d in range(FACES)]


def coarse_kernel(u_ref, f_ref, c_ref, links_ref, faces_ref, coarse_out):
    links = links_ref[...]
    defect = jnp.zeros((RANGE, LANES), jnp.float32)
    weights = jnp.zeros((RANGE, LANES), jnp.float32)
    for t in range(CELLS // LANES):
        c = c_ref[t]
        defect = defect + (f_ref[t] - c * u_ref[t])
        weights = weights + c
    sums = face_sums(lambda f, h: load_face(faces_ref, f, h))
    inner = lane_sum(defect) * (1.0 / CELLS)
    for s in sums:
        inner = inner - s
    diag = 6.0 + lane_sum(weights) * (1.0 / CELLS)
    lane = lanes()
    tile = jnp.zeros((RANGE, LANES), jnp.float32)
    for d in range(FACES):
        tile = jnp.where(lane == d, sums[d], tile)
        tile = jnp.where(lane == RANGE + d, links[:, d : d + 1].astype(jnp.float32), tile)
    tile = jnp.where(lane == FACES, inner, tile)
    tile = jnp.where(lane == FACES + 1, diag, tile)
    coarse_out[...] = tile


def row_kernel(row_ref, met_ref, out_ref):
    core, curve = lax.axis_index("d") % 2, lax.axis_index("d") // 2
    met = jnp.where(core == 0, curve + 1, curve + SLOTS - 1) % SLOTS
    lane = lanes()
    edge = jnp.zeros((RANGE, LANES), jnp.float32)
    for d, column in enumerate(face_sums(lambda f, h: load_face(met_ref, f, h))):
        edge = jnp.where(lane == d, column, edge)
    tiles = []
    for slot in range(SLOTS):
        place = slot % ROW
        own = slot // ROW == curve // ROW % (SLOTS // ROW)
        other = jnp.where(slot == met, edge, 0.0)
        tiles.append(jnp.where(own, row_ref[place // 2, place % 2], other))
    values = jnp.concatenate(tiles, axis=0).T
    out_ref[:, :LANES] = values[:RANGE]
    out_ref[:, LANES:] = values[RANGE : 2 * RANGE]


def join_kernel(met_ref, far_ref, out_ref):
    width = FACES * 2 * LANES
    core = lax.axis_index("d") % 2
    out_ref[:, :width] = met_ref[...]
    out_ref[:, width:] = jnp.where(core == 0, far_ref[0], far_ref[1])


def final_kernel(u_ref, f_ref, weight_ref, links_ref, faces_ref, row_ref, met_ref, out_ref):
    core, curve = lax.axis_index("d") % 2, lax.axis_index("d") // 2
    row = sublanes()
    part = (lanes() // (ROW * RANGE) + SLOTS // ROW - curve // ROW % (SLOTS // ROW)) % (SLOTS // ROW)
    first = jnp.logical_or(part == 3, jnp.logical_and(part == 2, curve % ROW == 0))
    sums, names = [
        jnp.where(
            part == 0,
            row_ref[:, h * LANES : (h + 1) * LANES],
            jnp.where(first, load_face(met_ref, FACES, h, 0), load_face(met_ref, FACES, h, 1)),
        )
        for h in range(2)
    ]
    valid = jnp.logical_and(names >= 0.0, row < FACES)
    at = names.astype(jnp.int32) & (LANES - 1)

    def named(tile):
        return jnp.where(valid, jnp.take_along_axis(tile, at, axis=1), 0.0)

    def total(tile):
        return jnp.broadcast_to(jnp.sum(tile, axis=0, keepdims=True), (RANGE, LANES))

    inner = jnp.broadcast_to(sums[FACES : FACES + 1], (RANGE, LANES))
    diag = jnp.broadcast_to(sums[FACES + 1 : FACES + 2], (RANGE, LANES))
    diag = jnp.where(diag > 0.0, diag, 1.0)
    residual = inner + total(named(sums))
    weight = RELAXATION / diag
    error = weight * residual
    for step in range(COARSE_SWEEPS - 1):
        error = (1.0 - RELAXATION) * error + weight * (residual + total(named(error)))
    near = named(error)
    own = lanes() == curve % SLOTS * RANGE + row
    lift = lane_sum(jnp.where(own, error, 0.0))
    ghosts, _ = ghost_faces(links_ref[...], range_base(), *window(met_ref, faces_ref))
    raised = []
    for d in range(FACES):
        raised.append(lane_sum(jnp.where(own, jnp.broadcast_to(near[d : d + 1], (RANGE, LANES)), 0.0)))
    lane = lanes()
    z = lane % SIDE
    around = []
    for h in range(2):
        low_y = jnp.where(lane < SIDE, raised[2], lift) if h == 0 else lift
        high_y = jnp.where(lane >= LANES - SIDE, raised[3], lift) if h == 1 else lift
        around.append(low_y + high_y + jnp.where(z == 0, raised[4], lift) + jnp.where(z == SIDE - 1, raised[5], lift))
    tiles = load(u_ref)
    for x in range(SIDE):
        for h in range(2):
            t = 2 * x + h
            near = around[h] + (lift if x else raised[0]) + (lift if x < SIDE - 1 else raised[1])
            tile = relax(tiles, ghosts, f_ref, weight_ref, x, h) + ((1.0 - RELAXATION) * lift + weight_ref[t] * near)
            half = jnp.where(core == 0, tile[0 : RANGE // 2], tile[RANGE // 2 :])
            out_ref[:, t * LANES : (t + 1) * LANES] = half


def call(kernel, out_shape, name, *args, specs=None, scratch=()):
    many = isinstance(out_shape, (list, tuple))
    return pl.pallas_call(
        kernel,
        out_shape=out_shape,
        in_specs=specs or [VMEM] * len(args),
        out_specs=[VMEM] * len(out_shape) if many else VMEM,
        scratch_shapes=scratch,
        compiler_params=pltpu.CompilerParams(vmem_limit_bytes=GRANT),
        name=name,
    )(*args)


def on_device(groups, pressure, source_term, coefficient, new_slot, face_links):
    cores, pairs, single, along, across, exchange, far = groups
    gather = lambda array, members: lax.all_gather(array, "d", axis=0, axis_index_groups=members)
    meet = lambda array: lax.ppermute(array, "d", exchange)
    field = f32(CELLS // LANES, RANGE, LANES)
    packed = f32(RANGE, FACES * 2 * LANES)
    index = jax.ShapeDtypeStruct((RANGE, LANES), jnp.int32)
    whole, rest = call(
        pack_kernel,
        [f32(RANGE // 2, PACKED), f32(RANGE // 2, 2 * CELLS)],
        "pack",
        *[
            pltpu.with_memory_space_constraint(array, pltpu.HBM)
            for array in (pressure, source_term, coefficient, new_slot, face_links)
        ],
        specs=[HBM] * 5,
        scratch=[
            pltpu.SMEM((RANGE // 2,), jnp.int32),
            pltpu.VMEM((RANGE // 2, FACES), jnp.int32),
            pltpu.SemaphoreType.DMA((5,)),
        ],
    )
    u, links, rows, faces = call(
        reorder_kernel, [field, index, index, packed], "reorder", gather(whole, cores)
    )
    met = meet(faces)
    rest, _ = lax.optimization_barrier((rest, faces))
    f, c, w = call(reorder_rest_kernel, [field] * 3, "rest", gather(rest, cores), rows)
    u, faces = call(sweep_kernel, [field, packed], "sweep", u, f, w, links, faces, gather(met, cores))
    met = call(choose_kernel, packed, "choose", gather(faces, pairs), lax.ppermute(faces, "d", single))
    u, faces = call(sweep_kernel, [field, packed], "smooth", u, f, w, links, faces, gather(met, cores))
    met = meet(faces)
    coarse = call(coarse_kernel, f32(RANGE, LANES), "coarse", u, f, c, links, faces)
    coarse = gather(gather(coarse, along), across)
    row = call(row_kernel, f32(RANGE, 2 * LANES), "row", coarse, met)
    joined = call(join_kernel, f32(RANGE, (FACES + 1) * 2 * LANES), "join", met, gather(row, far))
    return call(
        final_kernel,
        f32(RANGE // 2, CELLS),
        "final",
        u,
        f,
        w,
        links,
        faces,
        row,
        gather(joined, cores),
    )


def solution(mesh):
    devices = mesh.devices.reshape(-1)
    count = devices.size // 2
    cores = [[2 * i, 2 * i + 1] for i in range(count)]
    firsts = [2 * i + core for i in range(0, count, ROW) for core in range(2)]
    along = [[i + k, i + k + 2] for i in firsts for k in (0, 4)]
    across = [[i + k, i + 6 - k] for i in firsts for k in (0, 2)]
    far = [[2 * i + 1, 2 * (i + ROW)] for i in range(count - ROW)]
    for i in range(0, ROW, 2):
        far += [[2 * i, 2 * i + 2], [2 * (count - 1 - i) - 1, 2 * (count - 1 - i) + 1]]
    pairs = [[2 * i, 2 * i + 3] for i in range(count - 1) if i != BROKEN]
    pairs += [[2 * BROKEN, 1], [2 * count - 2, 2 * BROKEN + 3]]
    single = [(2 * BROKEN, 2 * BROKEN + 3), (2 * BROKEN + 3, 2 * BROKEN)]
    exchange = [pair for i in range(count - 1) for pair in ((2 * i, 2 * i + 3), (2 * i + 3, 2 * i))]
    split, line = P("d", None), P("d")
    return jax.shard_map(
        functools.partial(on_device, (cores, pairs, single, along, across, exchange, far)),
        mesh=Mesh(devices, ("d",)),
        in_specs=(split, split, split, line, split),
        out_specs=split,
        check_vma=False,
    )
```

```python
import functools

import jax
import jax.numpy as jnp
from jax import lax
from jax.experimental import pallas as pl
from jax.experimental.pallas import tpu as pltpu
from jax.sharding import Mesh, PartitionSpec as P

PRE_SWEEPS = 2
COARSE_SWEEPS = 4
RELAXATION = 0.8

SIDE = 16
RANGE = 8
LANES = 128
CELLS = 4096
FACES = 6
FLIPPED = (1, 0, 3, 2, 5, 4)
TURN = {3: LANES - SIDE, 5: 2 * SIDE - 2}
ROW = 4
BROKEN = 2
SLOTS = 16
PACKED = CELLS + LANES

VMEM = pl.BlockSpec(memory_space=pltpu.VMEM)
HBM = pl.BlockSpec(memory_space=pltpu.HBM)
GRANT = 4 * 1024 * 1024


def f32(*shape):
    return jax.ShapeDtypeStruct(shape, jnp.float32)


def lanes():
    return lax.broadcasted_iota(jnp.int32, (RANGE, LANES), 1)


def sublanes():
    return lax.broadcasted_iota(jnp.int32, (RANGE, LANES), 0)


def roll(tile, amount):
    amount = amount % LANES
    return tile if amount == 0 else pltpu.roll(tile, amount, 1)


def load(ref):
    return [[ref[2 * x + h] for h in range(2)] for x in range(SIDE)]


def store(ref, tiles):
    for x in range(SIDE):
        for h in range(2):
            ref[2 * x + h] = tiles[x][h]


def pack_faces(tiles):
    lane = lanes()
    zero = jnp.zeros((RANGE, LANES), jnp.float32)
    y_low, y_high, z_low, z_high = [[zero, zero] for _ in range(4)]
    for x in range(SIDE):
        part, place = x // 8, x % 8
        here = lane // SIDE == place
        y_low[part] = jnp.where(here, roll(tiles[x][0], SIDE * place), y_low[part])
        y_high[part] = jnp.where(here, roll(tiles[x][1], SIDE * place + SIDE), y_high[part])
        for h in range(2):
            turned = roll(tiles[x][h], x)
            z_low[h] = jnp.where(lane % SIDE == x, turned, z_low[h])
            z_high[h] = jnp.where(lane % SIDE == (x + SIDE - 1) % SIDE, turned, z_high[h])
    return [tiles[0], tiles[SIDE - 1], y_low, y_high, z_low, z_high]


def store_faces(ref, faces):
    for f in range(FACES):
        for h in range(2):
            ref[:, (2 * f + h) * LANES : (2 * f + h + 1) * LANES] = faces[f][h]


def load_face(ref, f, h, *lead):
    return ref[(*lead, slice(None), slice((2 * f + h) * LANES, (2 * f + h + 1) * LANES))]


def pick_rows(tile, rows):
    return jnp.take_along_axis(tile, rows, axis=0)


def ghost_faces(links, base, before, own, after):
    ghosts, valid = [], []
    for d in range(FACES):
        link = jnp.broadcast_to(links[:, d : d + 1], (RANGE, LANES))
        local = link - base
        rows = link & (RANGE - 1)
        face = FLIPPED[d]
        halves = []
        for h in range(2):
            low = pick_rows(before(face, h), rows)
            mid = pick_rows(own(face, h), rows)
            high = pick_rows(after(face, h), rows)
            picked = jnp.where(local < 0, low, jnp.where(local >= RANGE, high, mid))
            halves.append(roll(jnp.where(link >= 0, picked, 0.0), TURN.get(d, 0)))
        ghosts.append(halves)
        valid.append(link >= 0)
    return ghosts, valid


def beside(tiles, ghosts, x, h):
    lane = lanes()
    here = tiles[x][h]
    minus = tiles[x - 1][h] if x > 0 else ghosts[0][h]
    plus = tiles[x + 1][h] if x < SIDE - 1 else ghosts[1][h]
    total = minus + plus
    part, place = x // 8, x % 8
    outer_y = roll(jnp.where(lane // SIDE == place, ghosts[2][part], ghosts[3][part]), -SIDE * place)
    if h == 0:
        outer_minus, outer_plus = outer_y, roll(tiles[x][1], -SIDE)
    else:
        outer_minus, outer_plus = roll(tiles[x][0], SIDE), outer_y
    total = total + jnp.where(lane < SIDE, outer_minus, roll(here, SIDE))
    total = total + jnp.where(lane >= LANES - SIDE, outer_plus, roll(here, -SIDE))
    z = lane % SIDE
    column = (x + SIDE - 1) % SIDE
    outer_z = roll(jnp.where(z == column, ghosts[4][h], ghosts[5][h]), 1 - SIDE - x)
    total = total + jnp.where(z == 0, outer_z, roll(here, 1))
    total = total + jnp.where(z == SIDE - 1, outer_z, roll(here, -1))
    return total


def relax(tiles, ghosts, source_ref, weight_ref, x, h):
    weight = weight_ref[2 * x + h]
    gathered = source_ref[2 * x + h] + beside(tiles, ghosts, x, h)
    return (1.0 - RELAXATION) * tiles[x][h] + weight * gathered


def sweep(tiles, ghosts, source_ref, weight_ref):
    return [[relax(tiles, ghosts, source_ref, weight_ref, x, h) for h in range(2)] for x in range(SIDE)]


def range_base():
    return lax.axis_index("d") // 2 * RANGE


def pack_kernel(p_ref, f_ref, c_ref, slot_ref, links_ref, p_out, rest_out, slots, links, sems):
    targets = (p_out.at[:, :CELLS], rest_out.at[:, :CELLS], rest_out.at[:, CELLS:], slots, links)
    copies = [
        pltpu.make_async_copy(ref, target, sems.at[i])
        for i, (ref, target) in enumerate(zip((p_ref, f_ref, c_ref, slot_ref, links_ref), targets))
    ]
    for copy in copies[3:] + copies[:3]:
        copy.start()
    for copy in copies[3:]:
        copy.wait()
    lane = lanes()[: RANGE // 2]
    row = sublanes()[: RANGE // 2]
    tile = jnp.zeros((RANGE // 2, LANES), jnp.int32)
    for d in range(FACES):
        tile = jnp.where(lane == d, links[:, d : d + 1], tile)
    for i in range(RANGE // 2):
        tile = jnp.where(jnp.logical_and(lane == FACES, row == i), slots[i], tile)
    p_out[:, CELLS:] = tile.astype(jnp.float32)
    for copy in copies[:3]:
        copy.wait()


def both(ref, start):
    span = slice(start, start + LANES)
    return jnp.concatenate([ref[0, :, span], ref[1, :, span]], axis=0)


def reorder(ref, start, rows, target):
    for t in range(CELLS // LANES):
        target[t] = pick_rows(both(ref, start + t * LANES), rows)


def reorder_kernel(packed_ref, p_out, links_out, rows_out, faces_out):
    lane, row = lanes(), sublanes()
    names = both(packed_ref, CELLS)
    links_out[...] = names.astype(jnp.int32)
    slot = jnp.broadcast_to(names[:, FACES : FACES + 1], (RANGE, LANES)).astype(jnp.int32)
    placed = jnp.sum(jnp.where(slot == lane, row, 0).astype(jnp.float32), axis=0, keepdims=True)
    chosen = jnp.sum(jnp.where(lane == row, placed, 0.0), axis=1, keepdims=True)
    rows = jnp.broadcast_to(chosen, (RANGE, LANES)).astype(jnp.int32)
    rows_out[...] = rows
    reorder(packed_ref, 0, rows, p_out)
    store_faces(faces_out, pack_faces(load(p_out)))


def reorder_rest_kernel(rest_ref, rows_ref, f_out, c_out, weight_out):
    rows = rows_ref[...]
    reorder(rest_ref, 0, rows, f_out)
    reorder(rest_ref, CELLS, rows, c_out)
    for t in range(CELLS // LANES):
        weight_out[t] = RELAXATION / (6.0 + c_out[t])


def choose_kernel(pair_ref, single_ref, out_ref):
    me = lax.axis_index("d")
    single = jnp.logical_or(me == 2 * BROKEN, me == 2 * BROKEN + 3)
    out_ref[...] = jnp.where(single, single_ref[...], jnp.where(me % 2 == 0, pair_ref[1], pair_ref[0]))


def window(met_ref, faces_ref):
    before = lambda f, h: load_face(met_ref, f, h, 1)
    own = lambda f, h: load_face(faces_ref, f, h)
    after = lambda f, h: load_face(met_ref, f, h, 0)
    return before, own, after


def sweep_kernel(u_ref, f_ref, weight_ref, links_ref, faces_ref, met_ref, u_out, faces_out):
    ghosts, _ = ghost_faces(links_ref[...], range_base(), *window(met_ref, faces_ref))
    tiles = sweep(load(u_ref), ghosts, f_ref, weight_ref)
    store(u_out, tiles)
    store_faces(faces_out, pack_faces(tiles))


def lane_sum(tile):
    return jnp.sum(tile, axis=1, keepdims=True)


def face_sums(face):
    return [lane_sum(face(FLIPPED[d], 0) + face(FLIPPED[d], 1)) * (1.0 / CELLS) for d in range(FACES)]


def coarse_kernel(u_ref, f_ref, c_ref, links_ref, faces_ref, coarse_out):
    links = links_ref[...]
    defect = jnp.zeros((RANGE, LANES), jnp.float32)
    weights = jnp.zeros((RANGE, LANES), jnp.float32)
    for t in range(CELLS // LANES):
        c = c_ref[t]
        defect = defect + (f_ref[t] - c * u_ref[t])
        weights = weights + c
    sums = face_sums(lambda f, h: load_face(faces_ref, f, h))
    inner = lane_sum(defect) * (1.0 / CELLS)
    for s in sums:
        inner = inner - s
    diag = 6.0 + lane_sum(weights) * (1.0 / CELLS)
    lane = lanes()
    tile = jnp.zeros((RANGE, LANES), jnp.float32)
    for d in range(FACES):
        tile = jnp.where(lane == d, sums[d], tile)
        tile = jnp.where(lane == RANGE + d, links[:, d : d + 1].astype(jnp.float32), tile)
    tile = jnp.where(lane == FACES, inner, tile)
    tile = jnp.where(lane == FACES + 1, diag, tile)
    coarse_out[...] = tile


def row_kernel(row_ref, met_ref, out_ref):
    core, curve = lax.axis_index("d") % 2, lax.axis_index("d") // 2
    met = jnp.where(core == 0, curve + 1, curve + SLOTS - 1) % SLOTS
    lane = lanes()
    edge = jnp.zeros((RANGE, LANES), jnp.float32)
    for d, column in enumerate(face_sums(lambda f, h: load_face(met_ref, f, h))):
        edge = jnp.where(lane == d, column, edge)
    tiles = []
    for slot in range(SLOTS):
        place = slot % ROW
        own = slot // ROW == curve // ROW % (SLOTS // ROW)
        other = jnp.where(slot == met, edge, 0.0)
        tiles.append(jnp.where(own, row_ref[place // 2, place % 2], other))
    values = jnp.concatenate(tiles, axis=0).T
    out_ref[:, :LANES] = values[:RANGE]
    out_ref[:, LANES:] = values[RANGE : 2 * RANGE]


def join_kernel(met_ref, far_ref, out_ref):
    width = FACES * 2 * LANES
    core = lax.axis_index("d") % 2
    out_ref[:, :width] = met_ref[...]
    out_ref[:, width:] = jnp.where(core == 0, far_ref[0], far_ref[1])


def final_kernel(u_ref, f_ref, weight_ref, links_ref, faces_ref, row_ref, met_ref, out_ref):
    core, curve = lax.axis_index("d") % 2, lax.axis_index("d") // 2
    row = sublanes()
    part = (lanes() // (ROW * RANGE) + SLOTS // ROW - curve // ROW % (SLOTS // ROW)) % (SLOTS // ROW)
    first = jnp.logical_or(part == 3, jnp.logical_and(part == 2, curve % ROW == 0))
    sums, names = [
        jnp.where(
            part == 0,
            row_ref[:, h * LANES : (h + 1) * LANES],
            jnp.where(first, load_face(met_ref, FACES, h, 0), load_face(met_ref, FACES, h, 1)),
        )
        for h in range(2)
    ]
    valid = jnp.logical_and(names >= 0.0, row < FACES)
    at = names.astype(jnp.int32) & (LANES - 1)

    def named(tile):
        return jnp.where(valid, jnp.take_along_axis(tile, at, axis=1), 0.0)

    def total(tile):
        return jnp.broadcast_to(jnp.sum(tile, axis=0, keepdims=True), (RANGE, LANES))

    inner = jnp.broadcast_to(sums[FACES : FACES + 1], (RANGE, LANES))
    diag = jnp.broadcast_to(sums[FACES + 1 : FACES + 2], (RANGE, LANES))
    diag = jnp.where(diag > 0.0, diag, 1.0)
    residual = inner + total(named(sums))
    weight = RELAXATION / diag
    error = weight * residual
    for step in range(COARSE_SWEEPS - 1):
        error = (1.0 - RELAXATION) * error + weight * (residual + total(named(error)))
    near = named(error)
    own = lanes() == curve % SLOTS * RANGE + row
    lift = lane_sum(jnp.where(own, error, 0.0))
    ghosts, _ = ghost_faces(links_ref[...], range_base(), *window(met_ref, faces_ref))
    raised = []
    for d in range(FACES):
        raised.append(lane_sum(jnp.where(own, jnp.broadcast_to(near[d : d + 1], (RANGE, LANES)), 0.0)))
    lane = lanes()
    z = lane % SIDE
    around = []
    for h in range(2):
        low_y = jnp.where(lane < SIDE, raised[2], lift) if h == 0 else lift
        high_y = jnp.where(lane >= LANES - SIDE, raised[3], lift) if h == 1 else lift
        around.append(low_y + high_y + jnp.where(z == 0, raised[4], lift) + jnp.where(z == SIDE - 1, raised[5], lift))
    tiles = load(u_ref)
    for x in range(SIDE):
        for h in range(2):
            t = 2 * x + h
            near = around[h] + (lift if x else raised[0]) + (lift if x < SIDE - 1 else raised[1])
            tile = relax(tiles, ghosts, f_ref, weight_ref, x, h) + ((1.0 - RELAXATION) * lift + weight_ref[t] * near)
            half = jnp.where(core == 0, tile[0 : RANGE // 2], tile[RANGE // 2 :])
            out_ref[:, t * LANES : (t + 1) * LANES] = half


def call(kernel, out_shape, name, *args, specs=None, scratch=()):
    many = isinstance(out_shape, (list, tuple))
    return pl.pallas_call(
        kernel,
        out_shape=out_shape,
        in_specs=specs or [VMEM] * len(args),
        out_specs=[VMEM] * len(out_shape) if many else VMEM,
        scratch_shapes=scratch,
        compiler_params=pltpu.CompilerParams(vmem_limit_bytes=GRANT),
        name=name,
    )(*args)


def on_device(groups, pressure, source_term, coefficient, new_slot, face_links):
    cores, pairs, single, along, across, exchange, far = groups
    gather = lambda array, members: lax.all_gather(array, "d", axis=0, axis_index_groups=members)
    meet = lambda array: lax.ppermute(array, "d", exchange)
    field = f32(CELLS // LANES, RANGE, LANES)
    packed = f32(RANGE, FACES * 2 * LANES)
    index = jax.ShapeDtypeStruct((RANGE, LANES), jnp.int32)
    whole, rest = call(
        pack_kernel,
        [f32(RANGE // 2, PACKED), f32(RANGE // 2, 2 * CELLS)],
        "pack",
        *[
            pltpu.with_memory_space_constraint(array, pltpu.HBM)
            for array in (pressure, source_term, coefficient, new_slot, face_links)
        ],
        specs=[HBM] * 5,
        scratch=[
            pltpu.SMEM((RANGE // 2,), jnp.int32),
            pltpu.VMEM((RANGE // 2, FACES), jnp.int32),
            pltpu.SemaphoreType.DMA((5,)),
        ],
    )
    u, links, rows, faces = call(
        reorder_kernel, [field, index, index, packed], "reorder", gather(whole, cores)
    )
    met = meet(faces)
    rest, _ = lax.optimization_barrier((rest, faces))
    f, c, w = call(reorder_rest_kernel, [field] * 3, "rest", gather(rest, cores), rows)
    u, faces = call(sweep_kernel, [field, packed], "sweep", u, f, w, links, faces, gather(met, cores))
    met = call(choose_kernel, packed, "choose", gather(faces, pairs), lax.ppermute(faces, "d", single))
    u, faces = call(sweep_kernel, [field, packed], "smooth", u, f, w, links, faces, gather(met, cores))
    coarse = gather(call(coarse_kernel, f32(RANGE, LANES), "coarse", u, f, c, links, faces), along)
    faces, coarse = lax.optimization_barrier((faces, coarse))
    met = meet(faces)
    coarse = gather(coarse, across)
    row = call(row_kernel, f32(RANGE, 2 * LANES), "row", coarse, met)
    joined = call(join_kernel, f32(RANGE, (FACES + 1) * 2 * LANES), "join", met, gather(row, far))
    return call(
        final_kernel,
        f32(RANGE // 2, CELLS),
        "final",
        u,
        f,
        w,
        links,
        faces,
        row,
        gather(joined, cores),
    )


def solution(mesh):
    devices = mesh.devices.reshape(-1)
    count = devices.size // 2
    cores = [[2 * i, 2 * i + 1] for i in range(count)]
    firsts = [2 * i + core for i in range(0, count, ROW) for core in range(2)]
    along = [[i + k, i + k + 2] for i in firsts for k in (0, 4)]
    across = [[i + k, i + 6 - k] for i in firsts for k in (0, 2)]
    far = [[2 * i + 1, 2 * (i + ROW)] for i in range(count - ROW)]
    for i in range(0, ROW, 2):
        far += [[2 * i, 2 * i + 2], [2 * (count - 1 - i) - 1, 2 * (count - 1 - i) + 1]]
    pairs = [[2 * i, 2 * i + 3] for i in range(count - 1) if i != BROKEN]
    pairs += [[2 * BROKEN, 1], [2 * count - 2, 2 * BROKEN + 3]]
    single = [(2 * BROKEN, 2 * BROKEN + 3), (2 * BROKEN + 3, 2 * BROKEN)]
    exchange = [pair for i in range(count - 1) for pair in ((2 * i, 2 * i + 3), (2 * i + 3, 2 * i))]
    split, line = P("d", None), P("d")
    return jax.shard_map(
        functools.partial(on_device, (cores, pairs, single, along, across, exchange, far)),
        mesh=Mesh(devices, ("d",)),
        in_specs=(split, split, split, line, split),
        out_specs=split,
        check_vma=False,
    )
```

```python
import functools

import jax
import jax.numpy as jnp
from jax import lax
from jax.experimental import pallas as pl
from jax.experimental.pallas import tpu as pltpu
from jax.sharding import Mesh, PartitionSpec as P

PRE_SWEEPS = 2
COARSE_SWEEPS = 4
RELAXATION = 0.8

SIDE = 16
RANGE = 8
LANES = 128
CELLS = 4096
FACES = 6
FLIPPED = (1, 0, 3, 2, 5, 4)
TURN = {3: LANES - SIDE, 5: 2 * SIDE - 2}
ROW = 4
BROKEN = 2
SLOTS = 16
PACKED = CELLS + LANES

VMEM = pl.BlockSpec(memory_space=pltpu.VMEM)
HBM = pl.BlockSpec(memory_space=pltpu.HBM)
GRANT = 4 * 1024 * 1024


def f32(*shape):
    return jax.ShapeDtypeStruct(shape, jnp.float32)


def lanes():
    return lax.broadcasted_iota(jnp.int32, (RANGE, LANES), 1)


def sublanes():
    return lax.broadcasted_iota(jnp.int32, (RANGE, LANES), 0)


def roll(tile, amount):
    amount = amount % LANES
    return tile if amount == 0 else pltpu.roll(tile, amount, 1)


def load(ref):
    return [[ref[2 * x + h] for h in range(2)] for x in range(SIDE)]


def store(ref, tiles):
    for x in range(SIDE):
        for h in range(2):
            ref[2 * x + h] = tiles[x][h]


def pack_faces(tiles):
    lane = lanes()
    zero = jnp.zeros((RANGE, LANES), jnp.float32)
    y_low, y_high, z_low, z_high = [[zero, zero] for _ in range(4)]
    for x in range(SIDE):
        part, place = x // 8, x % 8
        here = lane // SIDE == place
        y_low[part] = jnp.where(here, roll(tiles[x][0], SIDE * place), y_low[part])
        y_high[part] = jnp.where(here, roll(tiles[x][1], SIDE * place + SIDE), y_high[part])
        for h in range(2):
            turned = roll(tiles[x][h], x)
            z_low[h] = jnp.where(lane % SIDE == x, turned, z_low[h])
            z_high[h] = jnp.where(lane % SIDE == (x + SIDE - 1) % SIDE, turned, z_high[h])
    return [tiles[0], tiles[SIDE - 1], y_low, y_high, z_low, z_high]


def store_faces(ref, faces):
    for f in range(FACES):
        for h in range(2):
            ref[:, (2 * f + h) * LANES : (2 * f + h + 1) * LANES] = faces[f][h]


def load_face(ref, f, h, *lead):
    return ref[(*lead, slice(None), slice((2 * f + h) * LANES, (2 * f + h + 1) * LANES))]


def pick_rows(tile, rows):
    return jnp.take_along_axis(tile, rows, axis=0)


def ghost_faces(links, base, before, own, after):
    ghosts, valid = [], []
    for d in range(FACES):
        link = jnp.broadcast_to(links[:, d : d + 1], (RANGE, LANES))
        local = link - base
        rows = link & (RANGE - 1)
        face = FLIPPED[d]
        halves = []
        for h in range(2):
            low = pick_rows(before(face, h), rows)
            mid = pick_rows(own(face, h), rows)
            high = pick_rows(after(face, h), rows)
            picked = jnp.where(local < 0, low, jnp.where(local >= RANGE, high, mid))
            halves.append(roll(jnp.where(link >= 0, picked, 0.0), TURN.get(d, 0)))
        ghosts.append(halves)
        valid.append(link >= 0)
    return ghosts, valid


def beside(tiles, ghosts, x, h):
    lane = lanes()
    here = tiles[x][h]
    minus = tiles[x - 1][h] if x > 0 else ghosts[0][h]
    plus = tiles[x + 1][h] if x < SIDE - 1 else ghosts[1][h]
    total = minus + plus
    part, place = x // 8, x % 8
    outer_y = roll(jnp.where(lane // SIDE == place, ghosts[2][part], ghosts[3][part]), -SIDE * place)
    if h == 0:
        outer_minus, outer_plus = outer_y, roll(tiles[x][1], -SIDE)
    else:
        outer_minus, outer_plus = roll(tiles[x][0], SIDE), outer_y
    total = total + jnp.where(lane < SIDE, outer_minus, roll(here, SIDE))
    total = total + jnp.where(lane >= LANES - SIDE, outer_plus, roll(here, -SIDE))
    z = lane % SIDE
    column = (x + SIDE - 1) % SIDE
    outer_z = roll(jnp.where(z == column, ghosts[4][h], ghosts[5][h]), 1 - SIDE - x)
    total = total + jnp.where(z == 0, outer_z, roll(here, 1))
    total = total + jnp.where(z == SIDE - 1, outer_z, roll(here, -1))
    return total


def relax(tiles, ghosts, source_ref, weight_ref, x, h):
    weight = weight_ref[2 * x + h]
    gathered = source_ref[2 * x + h] + beside(tiles, ghosts, x, h)
    return (1.0 - RELAXATION) * tiles[x][h] + weight * gathered


def sweep(tiles, ghosts, source_ref, weight_ref):
    return [[relax(tiles, ghosts, source_ref, weight_ref, x, h) for h in range(2)] for x in range(SIDE)]


def range_base():
    return lax.axis_index("d") // 2 * RANGE


def pack_kernel(p_ref, f_ref, c_ref, slot_ref, links_ref, p_out, rest_out, slots, links, sems):
    targets = (p_out.at[:, :CELLS], rest_out.at[:, :CELLS], rest_out.at[:, CELLS:], slots, links)
    copies = [
        pltpu.make_async_copy(ref, target, sems.at[i])
        for i, (ref, target) in enumerate(zip((p_ref, f_ref, c_ref, slot_ref, links_ref), targets))
    ]
    for copy in copies[3:] + copies[:3]:
        copy.start()
    for copy in copies[3:]:
        copy.wait()
    lane = lanes()[: RANGE // 2]
    row = sublanes()[: RANGE // 2]
    tile = jnp.zeros((RANGE // 2, LANES), jnp.int32)
    for d in range(FACES):
        tile = jnp.where(lane == d, links[:, d : d + 1], tile)
    for i in range(RANGE // 2):
        tile = jnp.where(jnp.logical_and(lane == FACES, row == i), slots[i], tile)
    p_out[:, CELLS:] = tile.astype(jnp.float32)
    for copy in copies[:3]:
        copy.wait()


def both(ref, start):
    span = slice(start, start + LANES)
    return jnp.concatenate([ref[0, :, span], ref[1, :, span]], axis=0)


def reorder(ref, start, rows, target):
    for t in range(CELLS // LANES):
        target[t] = pick_rows(both(ref, start + t * LANES), rows)


def reorder_kernel(packed_ref, p_out, links_out, rows_out, faces_out):
    lane, row = lanes(), sublanes()
    names = both(packed_ref, CELLS)
    links_out[...] = names.astype(jnp.int32)
    slot = jnp.broadcast_to(names[:, FACES : FACES + 1], (RANGE, LANES)).astype(jnp.int32)
    placed = jnp.sum(jnp.where(slot == lane, row, 0).astype(jnp.float32), axis=0, keepdims=True)
    chosen = jnp.sum(jnp.where(lane == row, placed, 0.0), axis=1, keepdims=True)
    rows = jnp.broadcast_to(chosen, (RANGE, LANES)).astype(jnp.int32)
    rows_out[...] = rows
    reorder(packed_ref, 0, rows, p_out)
    store_faces(faces_out, pack_faces(load(p_out)))


def reorder_rest_kernel(rest_ref, rows_ref, f_out, c_out, weight_out):
    rows = rows_ref[...]
    reorder(rest_ref, 0, rows, f_out)
    reorder(rest_ref, CELLS, rows, c_out)
    for t in range(CELLS // LANES):
        weight_out[t] = RELAXATION / (6.0 + c_out[t])


def choose_kernel(pair_ref, single_ref, out_ref):
    me = lax.axis_index("d")
    single = jnp.logical_or(me == 2 * BROKEN, me == 2 * BROKEN + 3)
    out_ref[...] = jnp.where(single, single_ref[...], jnp.where(me % 2 == 0, pair_ref[1], pair_ref[0]))


def window(met_ref, faces_ref):
    before = lambda f, h: load_face(met_ref, f, h, 1)
    own = lambda f, h: load_face(faces_ref, f, h)
    after = lambda f, h: load_face(met_ref, f, h, 0)
    return before, own, after


def sweep_kernel(u_ref, f_ref, weight_ref, links_ref, faces_ref, met_ref, u_out, faces_out):
    ghosts, _ = ghost_faces(links_ref[...], range_base(), *window(met_ref, faces_ref))
    tiles = sweep(load(u_ref), ghosts, f_ref, weight_ref)
    store(u_out, tiles)
    store_faces(faces_out, pack_faces(tiles))


def lane_sum(tile):
    return jnp.sum(tile, axis=1, keepdims=True)


def face_sums(face):
    return [lane_sum(face(FLIPPED[d], 0) + face(FLIPPED[d], 1)) * (1.0 / CELLS) for d in range(FACES)]


def coarse_kernel(u_ref, f_ref, c_ref, links_ref, faces_ref, coarse_out):
    links = links_ref[...]
    defect = jnp.zeros((RANGE, LANES), jnp.float32)
    weights = jnp.zeros((RANGE, LANES), jnp.float32)
    for t in range(CELLS // LANES):
        c = c_ref[t]
        defect = defect + (f_ref[t] - c * u_ref[t])
        weights = weights + c
    sums = face_sums(lambda f, h: load_face(faces_ref, f, h))
    inner = lane_sum(defect) * (1.0 / CELLS)
    for s in sums:
        inner = inner - s
    diag = 6.0 + lane_sum(weights) * (1.0 / CELLS)
    lane = lanes()
    tile = jnp.zeros((RANGE, LANES), jnp.float32)
    for d in range(FACES):
        tile = jnp.where(lane == d, sums[d], tile)
        tile = jnp.where(lane == RANGE + d, links[:, d : d + 1].astype(jnp.float32), tile)
    tile = jnp.where(lane == FACES, inner, tile)
    tile = jnp.where(lane == FACES + 1, diag, tile)
    coarse_out[...] = tile


def row_kernel(row_ref, met_ref, out_ref):
    core, curve = lax.axis_index("d") % 2, lax.axis_index("d") // 2
    met = jnp.where(core == 0, curve + 1, curve + SLOTS - 1) % SLOTS
    lane = lanes()
    edge = jnp.zeros((RANGE, LANES), jnp.float32)
    for d, column in enumerate(face_sums(lambda f, h: load_face(met_ref, f, h))):
        edge = jnp.where(lane == d, column, edge)
    tiles = []
    for slot in range(SLOTS):
        place = slot % ROW
        own = slot // ROW == curve // ROW % (SLOTS // ROW)
        other = jnp.where(slot == met, edge, 0.0)
        tiles.append(jnp.where(own, row_ref[place // 2, place % 2], other))
    values = jnp.concatenate(tiles, axis=0).T
    out_ref[:, :LANES] = values[:RANGE]
    out_ref[:, LANES:] = values[RANGE : 2 * RANGE]


def join_kernel(met_ref, far_ref, out_ref):
    width = FACES * 2 * LANES
    core = lax.axis_index("d") % 2
    out_ref[:, :width] = met_ref[...]
    out_ref[:, width:] = jnp.where(core == 0, far_ref[0], far_ref[1])


def final_kernel(u_ref, f_ref, weight_ref, links_ref, faces_ref, row_ref, met_ref, out_ref):
    core, curve = lax.axis_index("d") % 2, lax.axis_index("d") // 2
    row = sublanes()
    part = (lanes() // (ROW * RANGE) + SLOTS // ROW - curve // ROW % (SLOTS // ROW)) % (SLOTS // ROW)
    first = jnp.logical_or(part == 3, jnp.logical_and(part == 2, curve % ROW == 0))
    sums, names = [
        jnp.where(
            part == 0,
            row_ref[:, h * LANES : (h + 1) * LANES],
            jnp.where(first, load_face(met_ref, FACES, h, 0), load_face(met_ref, FACES, h, 1)),
        )
        for h in range(2)
    ]
    valid = jnp.logical_and(names >= 0.0, row < FACES)
    at = names.astype(jnp.int32) & (LANES - 1)

    def named(tile):
        return jnp.where(valid, jnp.take_along_axis(tile, at, axis=1), 0.0)

    def total(tile):
        return jnp.broadcast_to(jnp.sum(tile, axis=0, keepdims=True), (RANGE, LANES))

    inner = jnp.broadcast_to(sums[FACES : FACES + 1], (RANGE, LANES))
    diag = jnp.broadcast_to(sums[FACES + 1 : FACES + 2], (RANGE, LANES))
    diag = jnp.where(diag > 0.0, diag, 1.0)
    residual = inner + total(named(sums))
    weight = RELAXATION / diag
    error = weight * residual
    for step in range(COARSE_SWEEPS - 1):
        error = (1.0 - RELAXATION) * error + weight * (residual + total(named(error)))
    near = named(error)
    own = lanes() == curve % SLOTS * RANGE + row
    lift = lane_sum(jnp.where(own, error, 0.0))
    ghosts, _ = ghost_faces(links_ref[...], range_base(), *window(met_ref, faces_ref))
    raised = []
    for d in range(FACES):
        raised.append(lane_sum(jnp.where(own, jnp.broadcast_to(near[d : d + 1], (RANGE, LANES)), 0.0)))
    lane = lanes()
    z = lane % SIDE
    around = []
    for h in range(2):
        low_y = jnp.where(lane < SIDE, raised[2], lift) if h == 0 else lift
        high_y = jnp.where(lane >= LANES - SIDE, raised[3], lift) if h == 1 else lift
        around.append(low_y + high_y + jnp.where(z == 0, raised[4], lift) + jnp.where(z == SIDE - 1, raised[5], lift))
    tiles = load(u_ref)
    for x in range(SIDE):
        for h in range(2):
            t = 2 * x + h
            near = around[h] + (lift if x else raised[0]) + (lift if x < SIDE - 1 else raised[1])
            tile = relax(tiles, ghosts, f_ref, weight_ref, x, h) + ((1.0 - RELAXATION) * lift + weight_ref[t] * near)
            half = jnp.where(core == 0, tile[0 : RANGE // 2], tile[RANGE // 2 :])
            out_ref[:, t * LANES : (t + 1) * LANES] = half


def call(kernel, out_shape, name, *args, specs=None, scratch=()):
    many = isinstance(out_shape, (list, tuple))
    return pl.pallas_call(
        kernel,
        out_shape=out_shape,
        in_specs=specs or [VMEM] * len(args),
        out_specs=[VMEM] * len(out_shape) if many else VMEM,
        scratch_shapes=scratch,
        compiler_params=pltpu.CompilerParams(vmem_limit_bytes=GRANT),
        name=name,
    )(*args)


def on_device(groups, pressure, source_term, coefficient, new_slot, face_links):
    cores, pairs, single, along, across, exchange, far = groups
    gather = lambda array, members: lax.all_gather(array, "d", axis=0, axis_index_groups=members)
    meet = lambda array: lax.ppermute(array, "d", exchange)
    field = f32(CELLS // LANES, RANGE, LANES)
    packed = f32(RANGE, FACES * 2 * LANES)
    index = jax.ShapeDtypeStruct((RANGE, LANES), jnp.int32)
    whole, rest = call(
        pack_kernel,
        [f32(RANGE // 2, PACKED), f32(RANGE // 2, 2 * CELLS)],
        "pack",
        *[
            pltpu.with_memory_space_constraint(array, pltpu.HBM)
            for array in (pressure, source_term, coefficient, new_slot, face_links)
        ],
        specs=[HBM] * 5,
        scratch=[
            pltpu.SMEM((RANGE // 2,), jnp.int32),
            pltpu.VMEM((RANGE // 2, FACES), jnp.int32),
            pltpu.SemaphoreType.DMA((5,)),
        ],
    )
    u, links, rows, faces = call(
        reorder_kernel, [field, index, index, packed], "reorder", gather(whole, cores)
    )
    met = meet(faces)
    rest, _ = lax.optimization_barrier((rest, faces))
    f, c, w = call(reorder_rest_kernel, [field] * 3, "rest", gather(rest, cores), rows)
    u, faces = call(sweep_kernel, [field, packed], "sweep", u, f, w, links, faces, gather(met, cores))
    met = call(choose_kernel, packed, "choose", gather(faces, pairs), lax.ppermute(faces, "d", single))
    u, faces = call(sweep_kernel, [field, packed], "smooth", u, f, w, links, faces, gather(met, cores))
    met = meet(faces)
    coarse = call(coarse_kernel, f32(RANGE, LANES), "coarse", u, f, c, links, faces)
    coarse = gather(gather(coarse, along), across)
    row = call(row_kernel, f32(RANGE, 2 * LANES), "row", coarse, met)
    joined = call(join_kernel, f32(RANGE, (FACES + 1) * 2 * LANES), "join", met, gather(row, far))
    return call(
        final_kernel,
        f32(RANGE // 2, CELLS),
        "final",
        u,
        f,
        w,
        links,
        faces,
        row,
        gather(joined, cores),
    )


def solution(mesh):
    devices = mesh.devices.reshape(-1)
    count = devices.size // 2
    cores = [[2 * i, 2 * i + 1] for i in range(count)]
    firsts = [2 * i + core for i in range(0, count, ROW) for core in range(2)]
    along = [[i + k, i + k + 2] for i in firsts for k in (0, 4)]
    across = [[i + k, i + 6 - k] for i in firsts for k in (0, 2)]
    far = [[2 * i + 1, 2 * (i + ROW)] for i in range(count - ROW)]
    for i in range(0, ROW, 2):
        far += [[2 * i, 2 * i + 2], [2 * (count - 1 - i) - 1, 2 * (count - 1 - i) + 1]]
    pairs = [[2 * i, 2 * i + 3] for i in range(count - 1) if i != BROKEN]
    pairs += [[2 * BROKEN, 1], [2 * count - 2, 2 * BROKEN + 3]]
    single = [(2 * BROKEN, 2 * BROKEN + 3), (2 * BROKEN + 3, 2 * BROKEN)]
    exchange = [pair for i in range(count - 1) for pair in ((2 * i, 2 * i + 3), (2 * i + 3, 2 * i))]
    split, line = P("d", None), P("d")
    return jax.shard_map(
        functools.partial(on_device, (cores, pairs, single, along, across, exchange, far)),
        mesh=Mesh(devices, ("d",)),
        in_specs=(split, split, split, line, split),
        out_specs=split,
        check_vma=False,
    )
```

```python
import functools

import jax
import jax.numpy as jnp
from jax import lax
from jax.experimental import pallas as pl
from jax.experimental.pallas import tpu as pltpu
from jax.sharding import Mesh, PartitionSpec as P

PRE_SWEEPS = 2
COARSE_SWEEPS = 4
RELAXATION = 0.8

SIDE = 16
RANGE = 8
LANES = 128
CELLS = 4096
FACES = 6
FLIPPED = (1, 0, 3, 2, 5, 4)
TURN = {3: LANES - SIDE, 5: 2 * SIDE - 2}
ROW = 4
BROKEN = 2
SLOTS = 16
PACKED = CELLS + LANES

VMEM = pl.BlockSpec(memory_space=pltpu.VMEM)
HBM = pl.BlockSpec(memory_space=pltpu.HBM)
GRANT = 4 * 1024 * 1024


def f32(*shape):
    return jax.ShapeDtypeStruct(shape, jnp.float32)


def lanes():
    return lax.broadcasted_iota(jnp.int32, (RANGE, LANES), 1)


def sublanes():
    return lax.broadcasted_iota(jnp.int32, (RANGE, LANES), 0)


def roll(tile, amount):
    amount = amount % LANES
    return tile if amount == 0 else pltpu.roll(tile, amount, 1)


def load(ref):
    return [[ref[2 * x + h] for h in range(2)] for x in range(SIDE)]


def store(ref, tiles):
    for x in range(SIDE):
        for h in range(2):
            ref[2 * x + h] = tiles[x][h]


def pack_faces(tiles):
    lane = lanes()
    zero = jnp.zeros((RANGE, LANES), jnp.float32)
    y_low, y_high, z_low, z_high = [[zero, zero] for _ in range(4)]
    for x in range(SIDE):
        part, place = x // 8, x % 8
        here = lane // SIDE == place
        y_low[part] = jnp.where(here, roll(tiles[x][0], SIDE * place), y_low[part])
        y_high[part] = jnp.where(here, roll(tiles[x][1], SIDE * place + SIDE), y_high[part])
        for h in range(2):
            turned = roll(tiles[x][h], x)
            z_low[h] = jnp.where(lane % SIDE == x, turned, z_low[h])
            z_high[h] = jnp.where(lane % SIDE == (x + SIDE - 1) % SIDE, turned, z_high[h])
    return [tiles[0], tiles[SIDE - 1], y_low, y_high, z_low, z_high]


def store_faces(ref, faces):
    for f in range(FACES):
        for h in range(2):
            ref[:, (2 * f + h) * LANES : (2 * f + h + 1) * LANES] = faces[f][h]


def load_face(ref, f, h, *lead):
    return ref[(*lead, slice(None), slice((2 * f + h) * LANES, (2 * f + h + 1) * LANES))]


def pick_rows(tile, rows):
    return jnp.take_along_axis(tile, rows, axis=0)


def ghost_faces(links, base, before, own, after):
    ghosts, valid = [], []
    for d in range(FACES):
        link = jnp.broadcast_to(links[:, d : d + 1], (RANGE, LANES))
        local = link - base
        rows = link & (RANGE - 1)
        face = FLIPPED[d]
        halves = []
        for h in range(2):
            low = pick_rows(before(face, h), rows)
            mid = pick_rows(own(face, h), rows)
            high = pick_rows(after(face, h), rows)
            picked = jnp.where(local < 0, low, jnp.where(local >= RANGE, high, mid))
            halves.append(roll(jnp.where(link >= 0, picked, 0.0), TURN.get(d, 0)))
        ghosts.append(halves)
        valid.append(link >= 0)
    return ghosts, valid


def beside(tiles, ghosts, x, h):
    lane = lanes()
    here = tiles[x][h]
    minus = tiles[x - 1][h] if x > 0 else ghosts[0][h]
    plus = tiles[x + 1][h] if x < SIDE - 1 else ghosts[1][h]
    total = minus + plus
    part, place = x // 8, x % 8
    outer_y = roll(jnp.where(lane // SIDE == place, ghosts[2][part], ghosts[3][part]), -SIDE * place)
    if h == 0:
        outer_minus, outer_plus = outer_y, roll(tiles[x][1], -SIDE)
    else:
        outer_minus, outer_plus = roll(tiles[x][0], SIDE), outer_y
    total = total + jnp.where(lane < SIDE, outer_minus, roll(here, SIDE))
    total = total + jnp.where(lane >= LANES - SIDE, outer_plus, roll(here, -SIDE))
    z = lane % SIDE
    column = (x + SIDE - 1) % SIDE
    outer_z = roll(jnp.where(z == column, ghosts[4][h], ghosts[5][h]), 1 - SIDE - x)
    total = total + jnp.where(z == 0, outer_z, roll(here, 1))
    total = total + jnp.where(z == SIDE - 1, outer_z, roll(here, -1))
    return total


def relax(tiles, ghosts, source_ref, weight_ref, x, h):
    weight = weight_ref[2 * x + h]
    gathered = source_ref[2 * x + h] + beside(tiles, ghosts, x, h)
    return (1.0 - RELAXATION) * tiles[x][h] + weight * gathered


def sweep(tiles, ghosts, source_ref, weight_ref):
    return [[relax(tiles, ghosts, source_ref, weight_ref, x, h) for h in range(2)] for x in range(SIDE)]


def range_base():
    return lax.axis_index("d") // 2 * RANGE


def pack_kernel(p_ref, f_ref, c_ref, slot_ref, links_ref, p_out, rest_out, slots, links, sems):
    targets = (p_out.at[:, :CELLS], rest_out.at[:, :CELLS], rest_out.at[:, CELLS:], slots, links)
    copies = [
        pltpu.make_async_copy(ref, target, sems.at[i])
        for i, (ref, target) in enumerate(zip((p_ref, f_ref, c_ref, slot_ref, links_ref), targets))
    ]
    for copy in copies[3:] + copies[:3]:
        copy.start()
    for copy in copies[3:]:
        copy.wait()
    lane = lanes()[: RANGE // 2]
    row = sublanes()[: RANGE // 2]
    tile = jnp.zeros((RANGE // 2, LANES), jnp.int32)
    for d in range(FACES):
        tile = jnp.where(lane == d, links[:, d : d + 1], tile)
    for i in range(RANGE // 2):
        tile = jnp.where(jnp.logical_and(lane == FACES, row == i), slots[i], tile)
    p_out[:, CELLS:] = tile.astype(jnp.float32)
    for copy in copies[:3]:
        copy.wait()


def both(ref, start):
    span = slice(start, start + LANES)
    return jnp.concatenate([ref[0, :, span], ref[1, :, span]], axis=0)


def reorder(ref, start, rows, target):
    for t in range(CELLS // LANES):
        target[t] = pick_rows(both(ref, start + t * LANES), rows)


def reorder_kernel(packed_ref, p_out, links_out, rows_out, faces_out):
    lane, row = lanes(), sublanes()
    names = both(packed_ref, CELLS)
    links_out[...] = names.astype(jnp.int32)
    slot = jnp.broadcast_to(names[:, FACES : FACES + 1], (RANGE, LANES)).astype(jnp.int32)
    placed = jnp.sum(jnp.where(slot == lane, row, 0).astype(jnp.float32), axis=0, keepdims=True)
    chosen = jnp.sum(jnp.where(lane == row, placed, 0.0), axis=1, keepdims=True)
    rows = jnp.broadcast_to(chosen, (RANGE, LANES)).astype(jnp.int32)
    rows_out[...] = rows
    reorder(packed_ref, 0, rows, p_out)
    store_faces(faces_out, pack_faces(load(p_out)))


def reorder_rest_kernel(rest_ref, rows_ref, f_out, c_out, weight_out):
    rows = rows_ref[...]
    reorder(rest_ref, 0, rows, f_out)
    reorder(rest_ref, CELLS, rows, c_out)
    for t in range(CELLS // LANES):
        weight_out[t] = RELAXATION / (6.0 + c_out[t])


def choose_kernel(pair_ref, single_ref, out_ref):
    me = lax.axis_index("d")
    single = jnp.logical_or(me == 2 * BROKEN, me == 2 * BROKEN + 3)
    out_ref[...] = jnp.where(single, single_ref[...], jnp.where(me % 2 == 0, pair_ref[1], pair_ref[0]))


def window(met_ref, faces_ref):
    before = lambda f, h: load_face(met_ref, f, h, 1)
    own = lambda f, h: load_face(faces_ref, f, h)
    after = lambda f, h: load_face(met_ref, f, h, 0)
    return before, own, after


def sweep_kernel(u_ref, f_ref, weight_ref, links_ref, faces_ref, met_ref, u_out, faces_out):
    ghosts, _ = ghost_faces(links_ref[...], range_base(), *window(met_ref, faces_ref))
    tiles = sweep(load(u_ref), ghosts, f_ref, weight_ref)
    store(u_out, tiles)
    store_faces(faces_out, pack_faces(tiles))


def lane_sum(tile):
    return jnp.sum(tile, axis=1, keepdims=True)


def face_sums(face):
    return [lane_sum(face(FLIPPED[d], 0) + face(FLIPPED[d], 1)) * (1.0 / CELLS) for d in range(FACES)]


def coarse_kernel(u_ref, f_ref, c_ref, links_ref, faces_ref, coarse_out):
    links = links_ref[...]
    defect = jnp.zeros((RANGE, LANES), jnp.float32)
    weights = jnp.zeros((RANGE, LANES), jnp.float32)
    for t in range(CELLS // LANES):
        c = c_ref[t]
        defect = defect + (f_ref[t] - c * u_ref[t])
        weights = weights + c
    sums = face_sums(lambda f, h: load_face(faces_ref, f, h))
    inner = lane_sum(defect) * (1.0 / CELLS)
    for s in sums:
        inner = inner - s
    diag = 6.0 + lane_sum(weights) * (1.0 / CELLS)
    lane = lanes()
    tile = jnp.zeros((RANGE, LANES), jnp.float32)
    for d in range(FACES):
        tile = jnp.where(lane == d, sums[d], tile)
        tile = jnp.where(lane == RANGE + d, links[:, d : d + 1].astype(jnp.float32), tile)
    tile = jnp.where(lane == FACES, inner, tile)
    tile = jnp.where(lane == FACES + 1, diag, tile)
    coarse_out[...] = tile


def row_kernel(row_ref, met_ref, out_ref):
    core, curve = lax.axis_index("d") % 2, lax.axis_index("d") // 2
    met = jnp.where(core == 0, curve + 1, curve + SLOTS - 1) % SLOTS
    lane = lanes()
    edge = jnp.zeros((RANGE, LANES), jnp.float32)
    for d, column in enumerate(face_sums(lambda f, h: load_face(met_ref, f, h))):
        edge = jnp.where(lane == d, column, edge)
    tiles = []
    for slot in range(SLOTS):
        place = slot % ROW
        own = slot // ROW == curve // ROW % (SLOTS // ROW)
        other = jnp.where(slot == met, edge, 0.0)
        tiles.append(jnp.where(own, row_ref[place // 2, place % 2], other))
    values = jnp.concatenate(tiles, axis=0).T
    out_ref[:, :LANES] = values[:RANGE]
    out_ref[:, LANES:] = values[RANGE : 2 * RANGE]


def join_kernel(met_ref, far_ref, out_ref):
    width = FACES * 2 * LANES
    core = lax.axis_index("d") % 2
    out_ref[:, :width] = met_ref[...]
    out_ref[:, width:] = jnp.where(core == 0, far_ref[0], far_ref[1])


def final_kernel(u_ref, f_ref, weight_ref, links_ref, faces_ref, row_ref, met_ref, out_ref):
    core, curve = lax.axis_index("d") % 2, lax.axis_index("d") // 2
    row = sublanes()
    part = (lanes() // (ROW * RANGE) + SLOTS // ROW - curve // ROW % (SLOTS // ROW)) % (SLOTS // ROW)
    first = jnp.logical_or(part == 3, jnp.logical_and(part == 2, curve % ROW == 0))
    sums, names = [
        jnp.where(
            part == 0,
            row_ref[:, h * LANES : (h + 1) * LANES],
            jnp.where(first, load_face(met_ref, FACES, h, 0), load_face(met_ref, FACES, h, 1)),
        )
        for h in range(2)
    ]
    valid = jnp.logical_and(names >= 0.0, row < FACES)
    at = names.astype(jnp.int32) & (LANES - 1)

    def named(tile):
        return jnp.where(valid, jnp.take_along_axis(tile, at, axis=1), 0.0)

    def total(tile):
        return jnp.broadcast_to(jnp.sum(tile, axis=0, keepdims=True), (RANGE, LANES))

    inner = jnp.broadcast_to(sums[FACES : FACES + 1], (RANGE, LANES))
    diag = jnp.broadcast_to(sums[FACES + 1 : FACES + 2], (RANGE, LANES))
    diag = jnp.where(diag > 0.0, diag, 1.0)
    residual = inner + total(named(sums))
    weight = RELAXATION / diag
    error = weight * residual
    for step in range(COARSE_SWEEPS - 1):
        error = (1.0 - RELAXATION) * error + weight * (residual + total(named(error)))
    near = named(error)
    own = curve % SLOTS * RANGE + row
    lift = jnp.take_along_axis(error, own, axis=1)
    ghosts, _ = ghost_faces(links_ref[...], range_base(), *window(met_ref, faces_ref))
    raised = []
    for d in range(FACES):
        raised.append(jnp.take_along_axis(jnp.broadcast_to(near[d : d + 1], (RANGE, LANES)), own, axis=1))
    lane = lanes()
    z = lane % SIDE
    around = []
    for h in range(2):
        low_y = jnp.where(lane < SIDE, raised[2], lift) if h == 0 else lift
        high_y = jnp.where(lane >= LANES - SIDE, raised[3], lift) if h == 1 else lift
        around.append(low_y + high_y + jnp.where(z == 0, raised[4], lift) + jnp.where(z == SIDE - 1, raised[5], lift))
    tiles = load(u_ref)
    for x in range(SIDE):
        for h in range(2):
            t = 2 * x + h
            near = around[h] + (lift if x else raised[0]) + (lift if x < SIDE - 1 else raised[1])
            tile = relax(tiles, ghosts, f_ref, weight_ref, x, h) + ((1.0 - RELAXATION) * lift + weight_ref[t] * near)
            half = jnp.where(core == 0, tile[0 : RANGE // 2], tile[RANGE // 2 :])
            out_ref[:, t * LANES : (t + 1) * LANES] = half


def call(kernel, out_shape, name, *args, specs=None, scratch=()):
    many = isinstance(out_shape, (list, tuple))
    return pl.pallas_call(
        kernel,
        out_shape=out_shape,
        in_specs=specs or [VMEM] * len(args),
        out_specs=[VMEM] * len(out_shape) if many else VMEM,
        scratch_shapes=scratch,
        compiler_params=pltpu.CompilerParams(vmem_limit_bytes=GRANT),
        name=name,
    )(*args)


def on_device(groups, pressure, source_term, coefficient, new_slot, face_links):
    cores, pairs, single, along, across, exchange, far = groups
    gather = lambda array, members: lax.all_gather(array, "d", axis=0, axis_index_groups=members)
    meet = lambda array: lax.ppermute(array, "d", exchange)
    field = f32(CELLS // LANES, RANGE, LANES)
    packed = f32(RANGE, FACES * 2 * LANES)
    index = jax.ShapeDtypeStruct((RANGE, LANES), jnp.int32)
    whole, rest = call(
        pack_kernel,
        [f32(RANGE // 2, PACKED), f32(RANGE // 2, 2 * CELLS)],
        "pack",
        *[
            pltpu.with_memory_space_constraint(array, pltpu.HBM)
            for array in (pressure, source_term, coefficient, new_slot, face_links)
        ],
        specs=[HBM] * 5,
        scratch=[
            pltpu.SMEM((RANGE // 2,), jnp.int32),
            pltpu.VMEM((RANGE // 2, FACES), jnp.int32),
            pltpu.SemaphoreType.DMA((5,)),
        ],
    )
    u, links, rows, faces = call(
        reorder_kernel, [field, index, index, packed], "reorder", gather(whole, cores)
    )
    met = meet(faces)
    rest, _ = lax.optimization_barrier((rest, faces))
    f, c, w = call(reorder_rest_kernel, [field] * 3, "rest", gather(rest, cores), rows)
    u, faces = call(sweep_kernel, [field, packed], "sweep", u, f, w, links, faces, gather(met, cores))
    met = call(choose_kernel, packed, "choose", gather(faces, pairs), lax.ppermute(faces, "d", single))
    u, faces = call(sweep_kernel, [field, packed], "smooth", u, f, w, links, faces, gather(met, cores))
    met = meet(faces)
    coarse = call(coarse_kernel, f32(RANGE, LANES), "coarse", u, f, c, links, faces)
    coarse = gather(gather(coarse, along), across)
    row = call(row_kernel, f32(RANGE, 2 * LANES), "row", coarse, met)
    joined = call(join_kernel, f32(RANGE, (FACES + 1) * 2 * LANES), "join", met, gather(row, far))
    return call(
        final_kernel,
        f32(RANGE // 2, CELLS),
        "final",
        u,
        f,
        w,
        links,
        faces,
        row,
        gather(joined, cores),
    )


def solution(mesh):
    devices = mesh.devices.reshape(-1)
    count = devices.size // 2
    cores = [[2 * i, 2 * i + 1] for i in range(count)]
    firsts = [2 * i + core for i in range(0, count, ROW) for core in range(2)]
    along = [[i + k, i + k + 2] for i in firsts for k in (0, 4)]
    across = [[i + k, i + 6 - k] for i in firsts for k in (0, 2)]
    far = [[2 * i + 1, 2 * (i + ROW)] for i in range(count - ROW)]
    for i in range(0, ROW, 2):
        far += [[2 * i, 2 * i + 2], [2 * (count - 1 - i) - 1, 2 * (count - 1 - i) + 1]]
    pairs = [[2 * i, 2 * i + 3] for i in range(count - 1) if i != BROKEN]
    pairs += [[2 * BROKEN, 1], [2 * count - 2, 2 * BROKEN + 3]]
    single = [(2 * BROKEN, 2 * BROKEN + 3), (2 * BROKEN + 3, 2 * BROKEN)]
    exchange = [pair for i in range(count - 1) for pair in ((2 * i, 2 * i + 3), (2 * i + 3, 2 * i))]
    split, line = P("d", None), P("d")
    return jax.shard_map(
        functools.partial(on_device, (cores, pairs, single, along, across, exchange, far)),
        mesh=Mesh(devices, ("d",)),
        in_specs=(split, split, split, line, split),
        out_specs=split,
        check_vma=False,
    )
```
